128 devices in a mesh: wide: 16 (over z_hi, y, core), narrow: 8 (over x, z_lo).
Axes of the slice: x: 4, y: 4, z: 4 (z_hi: 2, z_lo: 2; z = z_hi * 2 + z_lo), core: 2. Of those that a mesh axis runs over, the one named last changes fastest.
Arguments:
- detail: bfloat16 [2048, 1024, 128], P('wide', 'narrow'), may hold values from -120 to 120
- coarse: bfloat16 [512, 256, 128], P('wide', 'narrow'), may hold values from -6 to 6
- diagonal: float32 [2048, 1024], P('wide', 'narrow'), may hold values from 0.5 to 4
- parents: int32 [256, 128], P('wide', 'narrow'), may hold values from 0 to 8191
- tile_mask: int32 [256, 128], P('wide', 'narrow'), may hold values 0 or 1
Outputs:
- embedding: float32 [2048, 1024, 128], P('wide', 'narrow')
The draws below stay inside these ranges and needn't reach their ends.
Inputs may be any that keep to these rules, and one draw needn't show every extreme that they name: `parents`: A tile in row a names a coarse cell of the coarse rows band * 32 to band * 32 + 31, band = a // 16, any coarse column.
All inputs are finite; a program needn't handle non-finite values. No bound on the sum of `tile_mask` on one device may be relied on, other than what follows from the above.
Results may differ from the reference program's by a relative error of at most 0.0003.
Values may be sent and summed in bfloat16 or wider, within the bound.
A program may use at most 128 MiB of HBM per device.

```python
import math
import jax
import jax.numpy as jnp
from jax import lax

K = 128
TS = 8
CX = 128
CCX = 32
NX = 2048
NY = 1024
NCX = 512
NCY = 256
NTX = 256
NTY = 128


def draw_detail(key, part):
    key_rows, key_cols, key_base = jax.random.split(key, 3)
    rising = jnp.exp(math.log(3.0) * jnp.arange(NX, dtype=jnp.float32) / max(NX - 1, 1))
    row_scale = rising * jnp.exp(jax.random.uniform(key_rows, (NX,), jnp.float32, 0.0, math.log(10.0)))
    col_scale = jnp.exp(jax.random.uniform(key_cols, (K,), jnp.float32, 0.0, math.log(10.0)))
    base = jnp.clip(jax.random.normal(key_base, (NX, NY, K), jnp.float32), -4.0, 4.0)
    values = base * row_scale[:, None, None] * col_scale[None, None, :] / 10.0
    return values.astype(jnp.bfloat16)


def set_ends(result, own_key, low, top_value):
    spot = [jax.random.randint(jax.random.fold_in(own_key, axis), (), 0, length) for axis, length in enumerate(result.shape)]
    widest = result.shape.index(max(result.shape))
    next_to = spot[:widest] + [(spot[widest] + 1) % result.shape[widest]] + spot[widest + 1:]
    return result.at[tuple(spot)].set(low).at[tuple(next_to)].set(top_value)


def block_scale(own_key, shape, shards, smallest, high):
    factor_of = 1.0
    for axis_at, blocks in shards:
        heights = jax.random.uniform(jax.random.fold_in(jax.random.fold_in(own_key, 6), axis_at), (blocks,), jnp.float32, smallest / len(shards), high / len(shards))
        factor_of = factor_of * jnp.repeat(jnp.exp(heights), shape[axis_at] // blocks).reshape((-1,) + (1,) * (len(shape) - 1 - axis_at))
    return factor_of


def bell_draw(rng, extent, width, reach, cuts=(), kind=jnp.bfloat16):
    drawn = width * jax.random.normal(rng, extent, jnp.float32)
    if cuts:
        drawn = drawn * block_scale(rng, extent, cuts, -0.22, 0.18)
    return jnp.clip(drawn, -reach, reach).astype(kind)


def setup_inputs(seed: int = 0) -> dict:
    key_list = jax.random.split(jax.random.key(seed), 6)
    detail = draw_detail(jax.random.fold_in(key_list[5], 71), 0)
    coarse = bell_draw(key_list[1], (NCX, NCY, K), 1.0, 6.0, ((0, 16), (1, 8)))
    diagonal = jnp.clip(jnp.exp(math.log(4.0) - 2.0794415 * jax.random.uniform(key_list[2], (NX, NY), jnp.float32) ** block_scale(key_list[2], (NX, NY), ((0, 16), (1, 8)), -0.2, 0.2)), 0.5, 4.0)
    parents = set_ends(jax.random.randint(key_list[3], (NTX, NTY), 0, CCX * NCY), jax.random.fold_in(key_list[3], 1), 0, (CCX * NCY) - 1).astype(jnp.int32)
    tile_mask = set_ends((jax.random.randint(key_list[4], (NTX, NTY), 0, 8) < 7).astype(jnp.int32), jax.random.fold_in(key_list[4], 1), 0, 1)
    return dict(detail=detail, coarse=coarse, diagonal=diagonal, parents=parents, tile_mask=tile_mask)


CENTER = 7.5
HALF_WIDTH = 4.5
EPSILON = 1e-06

def apply_operator(field, diag_cells, cell_mask):
    padded = jnp.pad(field, ((1, 1), (1, 1), (0, 0)))
    neighbours = padded[2:, 1:-1] + padded[:-2, 1:-1]
    neighbours = neighbours + padded[1:-1, 2:] + padded[1:-1, :-2]
    return cell_mask[..., None] * ((4.0 + diag_cells)[..., None] * field - neighbours)

def reference(detail, coarse, diagonal, parents, tile_mask):
    tiles_x = parents.shape[0]
    band_row = (jnp.arange(tiles_x, dtype=jnp.int32) // (CX // TS)).astype(jnp.int32)[:, None]
    row_index = (band_row * CCX + parents // NCY).astype(jnp.int32)
    col_index = (parents % NCY).astype(jnp.int32)
    cell_mask = jnp.repeat(jnp.repeat(tile_mask, TS, 0), TS, 1).astype(jnp.float32)
    block_cols = math.gcd(K, 16)

    def filter_block(group):
        first = (group * block_cols).astype(jnp.int32)
        coarse_part = lax.dynamic_slice_in_dim(coarse, first, block_cols, 2)
        detail_part = lax.dynamic_slice_in_dim(detail, first, block_cols, 2)
        vectors = coarse_part[row_index, col_index].astype(jnp.float32)
        cells = jnp.repeat(jnp.repeat(vectors, TS, 0), TS, 1)
        cheb_zero = cell_mask[..., None] * (cells + detail_part.astype(jnp.float32))
        cheb_one = (apply_operator(cheb_zero, diagonal, cell_mask) - CENTER * cheb_zero) / HALF_WIDTH
        cheb_two = 2.0 * (apply_operator(cheb_one, diagonal, cell_mask) - CENTER * cheb_one) / HALF_WIDTH - cheb_zero
        cheb_three = 2.0 * (apply_operator(cheb_two, diagonal, cell_mask) - CENTER * cheb_two) / HALF_WIDTH - cheb_one
        squares = lax.optimization_barrier(jnp.sum(cheb_three * cheb_three, axis=(0, 1)))
        return cheb_three / jnp.sqrt(squares / (NX * NY) + EPSILON)
    blocks = lax.map(filter_block, jnp.arange(K // block_cols, dtype=jnp.int32))
    return jnp.moveaxis(blocks, 0, 2).reshape(NX, NY, K)
```

```python
import functools

import jax
import jax.numpy as jnp
from jax import lax
from jax.experimental import pallas as pl
from jax.experimental.pallas import tpu as pltpu
from jax.sharding import PartitionSpec as P

TS = 8
CENTER = 7.5
HALF_WIDTH = 4.5
EPSILON = 1e-06

HALO = 3
LPAD = 8
RING = 16
ROWS = 8


def shift_pairs(dw, dn, nw, nn):
    pairs = []
    for w in range(nw):
        for n in range(nn):
            tw, tn = w + dw, n + dn
            if 0 <= tw < nw and 0 <= tn < nn:
                pairs.append((w * nn + n, tw * nn + tn))
    return pairs


def exchange(pieces, dw, dn, nw, nn):
    flat = jnp.concatenate([p.reshape(-1) for p in pieces])
    got = lax.ppermute(flat, ("wide", "narrow"), shift_pairs(dw, dn, nw, nn))
    out, at = [], 0
    for p in pieces:
        out.append(got[at : at + p.size].reshape(p.shape))
        at += p.size
    return out


def stencil_kernel(det_ref, cm_ref, m_ref, top_ref, bot_ref, left_ref, right_ref, g_ref, h_ref,
                   out_ref, ss_ref, r0, r1, r2):
    i = pl.program_id(0)
    cx = det_ref.shape[0]
    width = g_ref.shape[1]
    ext_rows = g_ref.shape[0]
    cy = det_ref.shape[1]

    def c0_row(x):
        s = x % RING

        @pl.when(x < HALO)
        def _():
            r0[s] = top_ref[jnp.minimum(x, HALO - 1)]

        @pl.when(x >= HALO + cx)
        def _():
            r0[s] = bot_ref[jnp.maximum(x - HALO - cx, 0)]

        @pl.when(jnp.logical_and(x >= HALO, x < HALO + cx))
        def _():
            b = jnp.clip(x - HALO, 0, cx - 1)
            t = b // TS
            r0[s, 0:LPAD] = left_ref[b]
            r0[s, LPAD:LPAD + cy] = cm_ref[t] + m_ref[t] * det_ref[b].astype(jnp.float32)
            r0[s, LPAD + cy:width] = right_ref[b]

    def apply_b(src, x):
        v = src[x % RING]
        nb = src[(x + 1) % RING] + src[(x + RING - 1) % RING]
        nb = nb + pltpu.roll(v, width - 1, 0) + pltpu.roll(v, 1, 0)
        return g_ref[x] * v - h_ref[(x + TS - HALO) // TS] * nb

    def c1_row(x):
        r1[x % RING] = apply_b(r0, x)

    def c2_row(x):
        r2[x % RING] = 2.0 * apply_b(r1, x) - r0[x % RING]

    def c3_row(x):
        c3 = 2.0 * apply_b(r2, x) - r1[x % RING]
        c3 = c3[LPAD:LPAD + cy]
        out_ref[x - HALO - ROWS * i] = c3
        sq = c3 * c3
        ss_ref[...] += jnp.sum(sq.reshape(cy // 8, 8, sq.shape[-1]), axis=0)

    def rows(fn, lo, n):
        def body(k, carry):
            fn(lo + k)
            return carry
        lax.fori_loop(0, n, body, 0)

    @pl.when(i == 0)
    def _():
        ss_ref[...] = jnp.zeros_like(ss_ref)
        rows(c0_row, 0, 2 * HALO)
        rows(c1_row, 1, 2 * HALO - 2)
        rows(c2_row, 2, 2 * HALO - 4)

    base = ROWS * i
    rows(c0_row, base + 2 * HALO, ROWS)
    rows(c1_row, base + 2 * HALO - 1, ROWS)
    rows(c2_row, base + 2 * HALO - 2, ROWS)
    rows(c3_row, base + HALO, ROWS)


def run_stencil(det, cm, m, top, bot, left, right, g, h):
    cx, cy, k = det.shape
    width = g.shape[1]
    steps = cx // ROWS
    vmem = pl.BlockSpec(memory_space=pltpu.VMEM)
    ops = cx * cy * k * 3 * 12
    return pl.pallas_call(
        stencil_kernel,
        grid=(steps,),
        in_specs=[vmem] * 9,
        out_specs=[
            pl.BlockSpec((ROWS, cy, k), lambda i: (i, 0, 0)),
            pl.BlockSpec((8, k), lambda i: (0, 0)),
        ],
        out_shape=[
            jax.ShapeDtypeStruct((cx, cy, k), jnp.float32),
            jax.ShapeDtypeStruct((8, k), jnp.float32),
        ],
        scratch_shapes=[pltpu.VMEM((RING, width, k), jnp.float32) for _ in range(3)],
        compiler_params=pltpu.CompilerParams(
            dimension_semantics=("arbitrary",), vmem_limit_bytes=56 * 1024 * 1024
        ),
        cost_estimate=pl.CostEstimate(
            flops=ops, transcendentals=0, bytes_accessed=det.size * 2 + cx * cy * k * 4 + g.size * 4
        ),
    )(det, cm, m, top, bot, left, right, g, h)


def local(detail, coarse, diagonal, parents, tile_mask):
    tiles_x, tiles_y = parents.shape
    cells_x, cells_y, columns = detail.shape
    nw, nn = lax.axis_size("wide"), lax.axis_size("narrow")
    total_cells = cells_x * nw * cells_y * nn
    mask_float = tile_mask.astype(jnp.float32)

    panels = lax.all_gather(coarse, "narrow", axis=1, tiled=True)
    flat_panel = panels.reshape(-1, columns)
    parent_flat = parents.reshape(-1)
    onehot = (
        parent_flat[:, None] == jnp.arange(flat_panel.shape[0], dtype=jnp.int32)[None, :]
    ).astype(jnp.bfloat16)
    tile_values = jnp.dot(onehot, flat_panel, preferred_element_type=jnp.float32)
    tv = tile_values.reshape(tiles_x, tiles_y, columns)

    m_rows = jnp.repeat(mask_float, TS, axis=1)
    m0 = jnp.broadcast_to(m_rows[:, :, None], (tiles_x, cells_y, columns))
    cm0 = m0 * jnp.repeat(tv, TS, axis=1)

    det_f = detail.astype(jnp.float32)
    h = HALO
    c0_top = cm0[0][None] + m0[0][None] * det_f[:h]
    c0_bot = cm0[-1][None] + m0[-1][None] * det_f[-h:]
    cm_rep = jnp.repeat(cm0, TS, axis=0)
    m_rep = jnp.repeat(m0, TS, axis=0)
    c0_left = cm_rep[:, :h] + m_rep[:, :h] * det_f[:, :h]
    c0_right = cm_rep[:, -h:] + m_rep[:, -h:] * det_f[:, -h:]

    d = diagonal
    mf = mask_float
    top_c, top_d, top_m = exchange([c0_bot, d[-h:], mf[-1:]], 1, 0, nw, nn)
    bot_c, bot_d, bot_m = exchange([c0_top, d[:h], mf[:1]], -1, 0, nw, nn)
    lft_c, lft_d, lft_m = exchange([c0_right, d[:, -h:], mf[:, -1:]], 0, 1, nw, nn)
    rgt_c, rgt_d, rgt_m = exchange([c0_left, d[:, :h], mf[:, :1]], 0, -1, nw, nn)
    tl_c, tl_d, tl_m = exchange([c0_bot[:, -h:], d[-h:, -h:], mf[-1:, -1:]], 1, 1, nw, nn)
    tr_c, tr_d, tr_m = exchange([c0_bot[:, :h], d[-h:, :h], mf[-1:, :1]], 1, -1, nw, nn)
    bl_c, bl_d, bl_m = exchange([c0_top[:, -h:], d[:h, -h:], mf[:1, -1:]], -1, 1, nw, nn)
    br_c, br_d, br_m = exchange([c0_top[:, :h], d[:h, :h], mf[:1, :1]], -1, -1, nw, nn)

    rpad = LPAD - h
    z3 = jnp.zeros((h, rpad, columns), jnp.float32)
    top = jnp.concatenate([z3, tl_c, top_c, tr_c, z3], axis=1)
    bot = jnp.concatenate([z3, bl_c, bot_c, br_c, z3], axis=1)
    zc = jnp.zeros((cells_x, rpad, columns), jnp.float32)
    left = jnp.concatenate([zc, lft_c], axis=1)
    right = jnp.concatenate([rgt_c, zc], axis=1)

    zd3 = jnp.zeros((h, rpad), jnp.float32)
    zdc = jnp.zeros((cells_x, rpad), jnp.float32)
    diag_ext = jnp.concatenate(
        [
            jnp.concatenate([zd3, tl_d, top_d, tr_d, zd3], axis=1),
            jnp.concatenate([zdc, lft_d, d, rgt_d, zdc], axis=1),
            jnp.concatenate([zd3, bl_d, bot_d, br_d, zd3], axis=1),
        ],
        axis=0,
    )
    mask_ext = jnp.concatenate(
        [
            jnp.concatenate([tl_m, top_m, tr_m], axis=1),
            jnp.concatenate([lft_m, mf, rgt_m], axis=1),
            jnp.concatenate([bl_m, bot_m, br_m], axis=1),
        ],
        axis=0,
    )
    reps = [h] + [TS] * tiles_x + [h]
    cell_mask_ext = jnp.repeat(
        jnp.repeat(mask_ext, jnp.array(reps), axis=0, total_repeat_length=cells_x + 2 * h), TS, axis=1
    )
    g = (cell_mask_ext * (4.0 + diag_ext) - CENTER) / HALF_WIDTH
    width = cells_y + 2 * LPAD
    g_b = jnp.broadcast_to(g[:, :, None], (cells_x + 2 * h, width, columns))
    h_t = jnp.repeat(mask_ext / HALF_WIDTH, TS, axis=1)
    h_b = jnp.broadcast_to(h_t[:, :, None], (tiles_x + 2, width, columns))

    cheb_three, ss = run_stencil(detail, cm0, m0, top, bot, left, right, g_b, h_b)
    local_squares = jnp.sum(ss, axis=0)
    squares = lax.psum(local_squares, ("wide", "narrow"))
    return cheb_three / jnp.sqrt(squares / total_cells + EPSILON)


def solution(mesh):
    in_specs = (
        P("wide", "narrow", None),
        P("wide", "narrow", None),
        P("wide", "narrow"),
        P("wide", "narrow"),
        P("wide", "narrow"),
    )
    out_specs = P("wide", "narrow", None)
    return jax.shard_map(local, mesh=mesh, in_specs=in_specs, out_specs=out_specs, check_vma=False)
```

```python
import functools

import jax
import jax.numpy as jnp
from jax import lax
from jax.experimental import pallas as pl
from jax.experimental.pallas import tpu as pltpu
from jax.sharding import PartitionSpec as P

TS = 8
CENTER = 7.5
HALF_WIDTH = 4.5
EPSILON = 1e-06

HALO = 3
LPAD = 8
RING = 16
ROWS = 8


def shift_pairs(dw, dn, nw, nn):
    pairs = []
    for w in range(nw):
        for n in range(nn):
            tw, tn = w + dw, n + dn
            if 0 <= tw < nw and 0 <= tn < nn:
                pairs.append((w * nn + n, tw * nn + tn))
    return pairs


def exchange(pieces, dw, dn, nw, nn):
    flat = jnp.concatenate([p.reshape(-1) for p in pieces])
    got = lax.ppermute(flat, ("wide", "narrow"), shift_pairs(dw, dn, nw, nn))
    out, at = [], 0
    for p in pieces:
        out.append(got[at : at + p.size].reshape(p.shape))
        at += p.size
    return out


def stencil_kernel(det_ref, cm_ref, m_ref, top_ref, bot_ref, left_ref, right_ref, g_ref, h_ref,
                   out_ref, ss_ref, r0, r1, r2):
    i = pl.program_id(0)
    cx = det_ref.shape[0]
    width = g_ref.shape[1]
    ext_rows = g_ref.shape[0]
    cy = det_ref.shape[1]

    def c0_row(x):
        s = x % RING

        @pl.when(x < HALO)
        def _():
            r0[s] = top_ref[jnp.minimum(x, HALO - 1)]

        @pl.when(x >= HALO + cx)
        def _():
            r0[s] = bot_ref[jnp.maximum(x - HALO - cx, 0)]

        @pl.when(jnp.logical_and(x >= HALO, x < HALO + cx))
        def _():
            b = jnp.clip(x - HALO, 0, cx - 1)
            t = b // TS
            r0[s, 0:LPAD] = left_ref[b]
            r0[s, LPAD:LPAD + cy] = cm_ref[t] + m_ref[t] * det_ref[b].astype(jnp.float32)
            r0[s, LPAD + cy:width] = right_ref[b]

    def apply_b(src, x):
        v = src[x % RING]
        nb = src[(x + 1) % RING] + src[(x + RING - 1) % RING]
        nb = nb + pltpu.roll(v, width - 1, 0) + pltpu.roll(v, 1, 0)
        return g_ref[x] * v - h_ref[(x + TS - HALO) // TS] * nb

    def c1_row(x):
        r1[x % RING] = apply_b(r0, x)

    def c2_row(x):
        r2[x % RING] = 2.0 * apply_b(r1, x) - r0[x % RING]

    def c3_row(x):
        c3 = 2.0 * apply_b(r2, x) - r1[x % RING]
        c3 = c3[LPAD:LPAD + cy]
        out_ref[x - HALO - ROWS * i] = c3
        sq = c3 * c3
        ss_ref[...] += jnp.sum(sq.reshape(cy // 8, 8, sq.shape[-1]), axis=0)

    def rows(fn, lo, n):
        def body(k, carry):
            fn(lo + k)
            return carry
        lax.fori_loop(0, n, body, 0)

    @pl.when(i == 0)
    def _():
        ss_ref[...] = jnp.zeros_like(ss_ref)
        rows(c0_row, 0, 2 * HALO)
        rows(c1_row, 1, 2 * HALO - 2)
        rows(c2_row, 2, 2 * HALO - 4)

    base = ROWS * i
    rows(c0_row, base + 2 * HALO, ROWS)
    rows(c1_row, base + 2 * HALO - 1, ROWS)
    rows(c2_row, base + 2 * HALO - 2, ROWS)
    rows(c3_row, base + HALO, ROWS)


def run_stencil(det, cm, m, top, bot, left, right, g, h):
    cx, cy, k = det.shape
    width = g.shape[1]
    steps = cx // ROWS
    vmem = pl.BlockSpec(memory_space=pltpu.VMEM)
    ops = cx * cy * k * 3 * 12
    return pl.pallas_call(
        stencil_kernel,
        grid=(steps,),
        in_specs=[vmem] * 9,
        out_specs=[
            pl.BlockSpec((ROWS, cy, k), lambda i: (i, 0, 0)),
            pl.BlockSpec((8, k), lambda i: (0, 0)),
        ],
        out_shape=[
            jax.ShapeDtypeStruct((cx, cy, k), jnp.float32),
            jax.ShapeDtypeStruct((8, k), jnp.float32),
        ],
        scratch_shapes=[pltpu.VMEM((RING, width, k), jnp.float32) for _ in range(3)],
        compiler_params=pltpu.CompilerParams(
            dimension_semantics=("arbitrary",), vmem_limit_bytes=56 * 1024 * 1024
        ),
        cost_estimate=pl.CostEstimate(
            flops=ops, transcendentals=0, bytes_accessed=det.size * 2 + cx * cy * k * 4 + g.size * 4
        ),
    )(det, cm, m, top, bot, left, right, g, h)


def allreduce_kernel(nw, nn, x_ref, o_ref, r1, r2, s1, q1, s2, q2):
    me_w = lax.axis_index("wide")
    me_n = lax.axis_index("narrow")
    mesh_id = pl.DeviceIdType.MESH
    barrier = pltpu.get_barrier_semaphore()
    for k in range(1, nn):
        pl.semaphore_signal(barrier, inc=1, device_id=(me_w, (me_n + k) % nn), device_id_type=mesh_id)
    for k in range(1, nw):
        pl.semaphore_signal(barrier, inc=1, device_id=((me_w + k) % nw, me_n), device_id_type=mesh_id)
    pl.semaphore_wait(barrier, nn - 1 + nw - 1)

    def phase(src, slots, send, recv, me, n, peer_of):
        copies = []
        for k in range(1, n):
            c = pltpu.make_async_remote_copy(
                src_ref=src, dst_ref=slots.at[me], send_sem=send.at[k], recv_sem=recv.at[me],
                device_id=peer_of((me + k) % n), device_id_type=mesh_id)
            c.start()
            copies.append(c)
        slots[me] = src[...]
        for k in range(1, n):
            other = (me + k) % n
            pltpu.make_async_remote_copy(
                src_ref=src, dst_ref=slots.at[other], send_sem=send.at[k], recv_sem=recv.at[other],
                device_id=peer_of(other), device_id_type=mesh_id).wait_recv()
        for c in copies:
            c.wait_send()
        return jnp.sum(slots[...], axis=0)

    part = phase(x_ref, r1, s1, q1, me_n, nn, lambda j: (me_w, j))
    o_ref[...] = part
    o_ref[...] = phase(o_ref, r2, s2, q2, me_w, nw, lambda j: (j, me_n))


def allreduce(x, nw, nn):
    k = x.shape[-1]
    vmem = pl.BlockSpec(memory_space=pltpu.VMEM)
    return pl.pallas_call(
        functools.partial(allreduce_kernel, nw, nn),
        in_specs=[vmem],
        out_specs=vmem,
        out_shape=jax.ShapeDtypeStruct((1, k), jnp.float32),
        scratch_shapes=[
            pltpu.VMEM((nn, 1, k), jnp.float32),
            pltpu.VMEM((nw, 1, k), jnp.float32),
            pltpu.SemaphoreType.DMA((nn,)),
            pltpu.SemaphoreType.DMA((nn,)),
            pltpu.SemaphoreType.DMA((nw,)),
            pltpu.SemaphoreType.DMA((nw,)),
        ],
        compiler_params=pltpu.CompilerParams(collective_id=0, has_side_effects=True),
    )(x)


def local(detail, coarse, diagonal, parents, tile_mask):
    tiles_x, tiles_y = parents.shape
    cells_x, cells_y, columns = detail.shape
    nw, nn = lax.axis_size("wide"), lax.axis_size("narrow")
    total_cells = cells_x * nw * cells_y * nn
    mask_float = tile_mask.astype(jnp.float32)

    panels = lax.all_gather(coarse, "narrow", axis=1, tiled=True)
    flat_panel = panels.reshape(-1, columns)
    parent_flat = parents.reshape(-1)
    onehot = (
        parent_flat[:, None] == jnp.arange(flat_panel.shape[0], dtype=jnp.int32)[None, :]
    ).astype(jnp.bfloat16)
    tile_values = jnp.dot(onehot, flat_panel, preferred_element_type=jnp.float32)
    tv = tile_values.reshape(tiles_x, tiles_y, columns)

    m_rows = jnp.repeat(mask_float, TS, axis=1)
    m0 = jnp.broadcast_to(m_rows[:, :, None], (tiles_x, cells_y, columns))
    cm0 = m0 * jnp.repeat(tv, TS, axis=1)

    det_f = detail.astype(jnp.float32)
    h = HALO
    c0_top = cm0[0][None] + m0[0][None] * det_f[:h]
    c0_bot = cm0[-1][None] + m0[-1][None] * det_f[-h:]
    cm_rep = jnp.repeat(cm0, TS, axis=0)
    m_rep = jnp.repeat(m0, TS, axis=0)
    c0_left = cm_rep[:, :h] + m_rep[:, :h] * det_f[:, :h]
    c0_right = cm_rep[:, -h:] + m_rep[:, -h:] * det_f[:, -h:]

    d = diagonal
    mf = mask_float
    top_c, top_d, top_m = exchange([c0_bot, d[-h:], mf[-1:]], 1, 0, nw, nn)
    bot_c, bot_d, bot_m = exchange([c0_top, d[:h], mf[:1]], -1, 0, nw, nn)
    lft_c, lft_d, lft_m = exchange([c0_right, d[:, -h:], mf[:, -1:]], 0, 1, nw, nn)
    rgt_c, rgt_d, rgt_m = exchange([c0_left, d[:, :h], mf[:, :1]], 0, -1, nw, nn)
    tl_c, tl_d, tl_m = exchange([c0_bot[:, -h:], d[-h:, -h:], mf[-1:, -1:]], 1, 1, nw, nn)
    tr_c, tr_d, tr_m = exchange([c0_bot[:, :h], d[-h:, :h], mf[-1:, :1]], 1, -1, nw, nn)
    bl_c, bl_d, bl_m = exchange([c0_top[:, -h:], d[:h, -h:], mf[:1, -1:]], -1, 1, nw, nn)
    br_c, br_d, br_m = exchange([c0_top[:, :h], d[:h, :h], mf[:1, :1]], -1, -1, nw, nn)

    rpad = LPAD - h
    z3 = jnp.zeros((h, rpad, columns), jnp.float32)
    top = jnp.concatenate([z3, tl_c, top_c, tr_c, z3], axis=1)
    bot = jnp.concatenate([z3, bl_c, bot_c, br_c, z3], axis=1)
    zc = jnp.zeros((cells_x, rpad, columns), jnp.float32)
    left = jnp.concatenate([zc, lft_c], axis=1)
    right = jnp.concatenate([rgt_c, zc], axis=1)

    zd3 = jnp.zeros((h, rpad), jnp.float32)
    zdc = jnp.zeros((cells_x, rpad), jnp.float32)
    diag_ext = jnp.concatenate(
        [
            jnp.concatenate([zd3, tl_d, top_d, tr_d, zd3], axis=1),
            jnp.concatenate([zdc, lft_d, d, rgt_d, zdc], axis=1),
            jnp.concatenate([zd3, bl_d, bot_d, br_d, zd3], axis=1),
        ],
        axis=0,
    )
    mask_ext = jnp.concatenate(
        [
            jnp.concatenate([tl_m, top_m, tr_m], axis=1),
            jnp.concatenate([lft_m, mf, rgt_m], axis=1),
            jnp.concatenate([bl_m, bot_m, br_m], axis=1),
        ],
        axis=0,
    )
    reps = [h] + [TS] * tiles_x + [h]
    cell_mask_ext = jnp.repeat(
        jnp.repeat(mask_ext, jnp.array(reps), axis=0, total_repeat_length=cells_x + 2 * h), TS, axis=1
    )
    g = (cell_mask_ext * (4.0 + diag_ext) - CENTER) / HALF_WIDTH
    width = cells_y + 2 * LPAD
    g_b = jnp.broadcast_to(g[:, :, None], (cells_x + 2 * h, width, columns))
    h_t = jnp.repeat(mask_ext / HALF_WIDTH, TS, axis=1)
    h_b = jnp.broadcast_to(h_t[:, :, None], (tiles_x + 2, width, columns))

    cheb_three, ss = run_stencil(detail, cm0, m0, top, bot, left, right, g_b, h_b)
    local_squares = jnp.sum(ss, axis=0, keepdims=True)
    squares = allreduce(local_squares, nw, nn)[0]
    return cheb_three / jnp.sqrt(squares / total_cells + EPSILON)


def solution(mesh):
    in_specs = (
        P("wide", "narrow", None),
        P("wide", "narrow", None),
        P("wide", "narrow"),
        P("wide", "narrow"),
        P("wide", "narrow"),
    )
    out_specs = P("wide", "narrow", None)
    return jax.shard_map(local, mesh=mesh, in_specs=in_specs, out_specs=out_specs, check_vma=False)
```

```python
import functools

import jax
import jax.numpy as jnp
from jax import lax
from jax.experimental import pallas as pl
from jax.experimental.pallas import tpu as pltpu
from jax.sharding import PartitionSpec as P

TS = 8
CENTER = 7.5
HALF_WIDTH = 4.5
EPSILON = 1e-06

HALO = 3
LPAD = 8
RING = 16
ROWS = 8


def shift_pairs(dw, dn, nw, nn):
    pairs = []
    for w in range(nw):
        for n in range(nn):
            tw, tn = w + dw, n + dn
            if 0 <= tw < nw and 0 <= tn < nn:
                pairs.append((w * nn + n, tw * nn + tn))
    return pairs


def exchange(pieces, dw, dn, nw, nn):
    flat = jnp.concatenate([p.reshape(-1) for p in pieces])
    got = lax.ppermute(flat, ("wide", "narrow"), shift_pairs(dw, dn, nw, nn))
    out, at = [], 0
    for p in pieces:
        out.append(got[at : at + p.size].reshape(p.shape))
        at += p.size
    return out


def stencil_kernel(det_ref, cm_ref, m_ref, top_ref, bot_ref, left_ref, right_ref, g_ref, h_ref,
                   out_ref, ss_ref, r0, r1, r2):
    i = pl.program_id(0)
    cx = det_ref.shape[0]
    width = g_ref.shape[1]
    ext_rows = g_ref.shape[0]
    cy = det_ref.shape[1]

    def c0_row(x):
        s = x % RING

        @pl.when(x < HALO)
        def _():
            r0[s] = top_ref[jnp.minimum(x, HALO - 1)]

        @pl.when(x >= HALO + cx)
        def _():
            r0[s] = bot_ref[jnp.maximum(x - HALO - cx, 0)]

        @pl.when(jnp.logical_and(x >= HALO, x < HALO + cx))
        def _():
            b = jnp.clip(x - HALO, 0, cx - 1)
            t = b // TS
            r0[s, 0:LPAD] = left_ref[b]
            r0[s, LPAD:LPAD + cy] = cm_ref[t] + m_ref[t] * det_ref[b].astype(jnp.float32)
            r0[s, LPAD + cy:width] = right_ref[b]

    def apply_b(src, x):
        v = src[x % RING]
        nb = src[(x + 1) % RING] + src[(x + RING - 1) % RING]
        nb = nb + pltpu.roll(v, width - 1, 0) + pltpu.roll(v, 1, 0)
        return g_ref[x] * v - h_ref[(x + TS - HALO) // TS] * nb

    def c1_row(x):
        r1[x % RING] = apply_b(r0, x)

    def c2_row(x):
        r2[x % RING] = 2.0 * apply_b(r1, x) - r0[x % RING]

    def c3_row(x):
        c3 = 2.0 * apply_b(r2, x) - r1[x % RING]
        c3 = c3[LPAD:LPAD + cy]
        out_ref[x - HALO - ROWS * i] = c3
        sq = c3 * c3
        ss_ref[...] += jnp.sum(sq.reshape(cy // 8, 8, sq.shape[-1]), axis=0)

    def rows(fn, lo, n):
        def body(k, carry):
            fn(lo + k)
            return carry
        lax.fori_loop(0, n, body, 0)

    @pl.when(i == 0)
    def _():
        ss_ref[...] = jnp.zeros_like(ss_ref)
        rows(c0_row, 0, 2 * HALO)
        rows(c1_row, 1, 2 * HALO - 2)
        rows(c2_row, 2, 2 * HALO - 4)

    base = ROWS * i
    rows(c0_row, base + 2 * HALO, ROWS)
    rows(c1_row, base + 2 * HALO - 1, ROWS)
    rows(c2_row, base + 2 * HALO - 2, ROWS)
    rows(c3_row, base + HALO, ROWS)


def run_stencil(det, cm, m, top, bot, left, right, g, h):
    cx, cy, k = det.shape
    width = g.shape[1]
    steps = cx // ROWS
    vmem = pl.BlockSpec(memory_space=pltpu.VMEM)
    ops = cx * cy * k * 3 * 12
    return pl.pallas_call(
        stencil_kernel,
        grid=(steps,),
        in_specs=[vmem] * 9,
        out_specs=[
            pl.BlockSpec((ROWS, cy, k), lambda i: (i, 0, 0)),
            pl.BlockSpec((8, k), lambda i: (0, 0)),
        ],
        out_shape=[
            jax.ShapeDtypeStruct((cx, cy, k), jnp.float32),
            jax.ShapeDtypeStruct((8, k), jnp.float32),
        ],
        scratch_shapes=[pltpu.VMEM((RING, width, k), jnp.float32) for _ in range(3)],
        compiler_params=pltpu.CompilerParams(
            dimension_semantics=("arbitrary",), vmem_limit_bytes=56 * 1024 * 1024
        ),
        cost_estimate=pl.CostEstimate(
            flops=ops, transcendentals=0, bytes_accessed=det.size * 2 + cx * cy * k * 4 + g.size * 4
        ),
    )(det, cm, m, top, bot, left, right, g, h)


def allreduce_kernel(nw, nn, x_ref, o_ref, r1, r2, s1, q1, s2, q2):
    me_w = lax.axis_index("wide")
    me_n = lax.axis_index("narrow")
    mesh_id = pl.DeviceIdType.MESH
    barrier = pltpu.get_barrier_semaphore()
    for k in range(1, nn):
        pl.semaphore_signal(barrier, inc=1, device_id=(me_w, (me_n + k) % nn), device_id_type=mesh_id)
    for k in range(1, nw):
        pl.semaphore_signal(barrier, inc=1, device_id=((me_w + k) % nw, me_n), device_id_type=mesh_id)
    pl.semaphore_wait(barrier, nn - 1 + nw - 1)

    def phase(src, slots, send, recv, me, n, peer_of):
        copies = []
        for k in range(1, n):
            c = pltpu.make_async_remote_copy(
                src_ref=src, dst_ref=slots.at[me], send_sem=send.at[k], recv_sem=recv.at[me],
                device_id=peer_of((me + k) % n), device_id_type=mesh_id)
            c.start()
            copies.append(c)
        slots[me] = src[...]
        for k in range(1, n):
            other = (me + k) % n
            pltpu.make_async_remote_copy(
                src_ref=src, dst_ref=slots.at[other], send_sem=send.at[k], recv_sem=recv.at[other],
                device_id=peer_of(other), device_id_type=mesh_id).wait_recv()
        for c in copies:
            c.wait_send()
        return jnp.sum(slots[...], axis=0)

    part = phase(x_ref, r1, s1, q1, me_n, nn, lambda j: (me_w, j))
    o_ref[...] = part
    o_ref[...] = phase(o_ref, r2, s2, q2, me_w, nw, lambda j: (j, me_n))


def allreduce(x, nw, nn):
    k = x.shape[-1]
    vmem = pl.BlockSpec(memory_space=pltpu.VMEM)
    return pl.pallas_call(
        functools.partial(allreduce_kernel, nw, nn),
        in_specs=[vmem],
        out_specs=vmem,
        out_shape=jax.ShapeDtypeStruct((1, k), jnp.float32),
        scratch_shapes=[
            pltpu.VMEM((nn, 1, k), jnp.float32),
            pltpu.VMEM((nw, 1, k), jnp.float32),
            pltpu.SemaphoreType.DMA((nn,)),
            pltpu.SemaphoreType.DMA((nn,)),
            pltpu.SemaphoreType.DMA((nw,)),
            pltpu.SemaphoreType.DMA((nw,)),
        ],
        compiler_params=pltpu.CompilerParams(collective_id=0, has_side_effects=True),
    )(x)


def gather_kernel(nn, cols, par_ref, ct_ref, o_ref, pslots, stage, tslots, ps, pq, ts, tq):
    me_w = lax.axis_index("wide")
    me_n = lax.axis_index("narrow")
    mesh_id = pl.DeviceIdType.MESH
    barrier = pltpu.get_barrier_semaphore()
    for k in range(1, nn):
        pl.semaphore_signal(barrier, inc=1, device_id=(me_w, (me_n + k) % nn), device_id_type=mesh_id)
    pl.semaphore_wait(barrier, nn - 1)

    def par_copy(k, other, slot):
        return pltpu.make_async_remote_copy(
            src_ref=par_ref, dst_ref=pslots.at[slot], send_sem=ps.at[k], recv_sem=pq.at[slot],
            device_id=(me_w, other), device_id_type=mesh_id)

    sent = []
    for k in range(1, nn):
        c = par_copy(k, (me_n + k) % nn, me_n)
        c.start()
        sent.append(c)

    local_cells = ct_ref.shape[1]
    ncols = local_cells // cols

    def contribution(par):
        col = par % (ncols * nn)
        idx = (par // (ncols * nn)) * ncols + col % ncols
        idx = jnp.where(col // ncols == me_n, idx, -1)
        rows = lax.broadcasted_iota(jnp.int32, (local_cells, par.shape[-1]), 0)
        onehot = (rows == idx).astype(jnp.bfloat16)
        got = jnp.dot(ct_ref[...], onehot, preferred_element_type=jnp.float32)
        return got.astype(jnp.bfloat16)

    tslots[me_n] = contribution(par_ref[...])
    out_copies = []
    for k in range(1, nn):
        other = (me_n + k) % nn
        par_copy(k, other, other).wait_recv()
        stage[k] = contribution(pslots[other])
        c = pltpu.make_async_remote_copy(
            src_ref=stage.at[k], dst_ref=tslots.at[me_n], send_sem=ts.at[k], recv_sem=tq.at[me_n],
            device_id=(me_w, other), device_id_type=mesh_id)
        c.start()
        out_copies.append(c)
    for k in range(1, nn):
        other = (me_n + k) % nn
        pltpu.make_async_remote_copy(
            src_ref=stage.at[k], dst_ref=tslots.at[other], send_sem=ts.at[k], recv_sem=tq.at[other],
            device_id=(me_w, other), device_id_type=mesh_id).wait_recv()
    for c in sent + out_copies:
        c.wait_send()
    total = tslots[0].astype(jnp.float32)
    for j in range(1, nn):
        total = total + tslots[j].astype(jnp.float32)
    o_ref[...] = total


def gather_tiles(parents, coarse, nn):
    ccx, ccy, k = coarse.shape
    par = parents.reshape(1, -1)
    n_t = par.shape[-1]
    ct = coarse.reshape(ccx * ccy, k).T
    vmem = pl.BlockSpec(memory_space=pltpu.VMEM)
    return pl.pallas_call(
        functools.partial(gather_kernel, nn, ccx),
        in_specs=[vmem, vmem],
        out_specs=vmem,
        out_shape=jax.ShapeDtypeStruct((k, n_t), jnp.float32),
        scratch_shapes=[
            pltpu.VMEM((nn, 1, n_t), jnp.int32),
            pltpu.VMEM((nn, k, n_t), jnp.bfloat16),
            pltpu.VMEM((nn, k, n_t), jnp.bfloat16),
            pltpu.SemaphoreType.DMA((nn,)),
            pltpu.SemaphoreType.DMA((nn,)),
            pltpu.SemaphoreType.DMA((nn,)),
            pltpu.SemaphoreType.DMA((nn,)),
        ],
        compiler_params=pltpu.CompilerParams(collective_id=1, has_side_effects=True),
    )(par, ct)


def local(detail, coarse, diagonal, parents, tile_mask):
    tiles_x, tiles_y = parents.shape
    cells_x, cells_y, columns = detail.shape
    nw, nn = lax.axis_size("wide"), lax.axis_size("narrow")
    total_cells = cells_x * nw * cells_y * nn
    mask_float = tile_mask.astype(jnp.float32)

    tile_values = gather_tiles(parents, coarse, nn).T
    tv = tile_values.reshape(tiles_x, tiles_y, columns)

    m_rows = jnp.repeat(mask_float, TS, axis=1)
    m0 = jnp.broadcast_to(m_rows[:, :, None], (tiles_x, cells_y, columns))
    cm0 = m0 * jnp.repeat(tv, TS, axis=1)

    h = HALO
    c0_top = cm0[0][None] + m0[0][None] * detail[:h].astype(jnp.float32)
    c0_bot = cm0[-1][None] + m0[-1][None] * detail[-h:].astype(jnp.float32)
    cm_rep = jnp.repeat(cm0, TS, axis=0)
    m_rep = jnp.repeat(m0, TS, axis=0)
    c0_left = cm_rep[:, :h] + m_rep[:, :h] * detail[:, :h].astype(jnp.float32)
    c0_right = cm_rep[:, -h:] + m_rep[:, -h:] * detail[:, -h:].astype(jnp.float32)

    d = diagonal
    mf = mask_float
    top_c, top_d, top_m = exchange([c0_bot, d[-h:], mf[-1:]], 1, 0, nw, nn)
    bot_c, bot_d, bot_m = exchange([c0_top, d[:h], mf[:1]], -1, 0, nw, nn)
    lft_c, lft_d, lft_m = exchange([c0_right, d[:, -h:], mf[:, -1:]], 0, 1, nw, nn)
    rgt_c, rgt_d, rgt_m = exchange([c0_left, d[:, :h], mf[:, :1]], 0, -1, nw, nn)
    tl_c, tl_d, tl_m = exchange([c0_bot[:, -h:], d[-h:, -h:], mf[-1:, -1:]], 1, 1, nw, nn)
    tr_c, tr_d, tr_m = exchange([c0_bot[:, :h], d[-h:, :h], mf[-1:, :1]], 1, -1, nw, nn)
    bl_c, bl_d, bl_m = exchange([c0_top[:, -h:], d[:h, -h:], mf[:1, -1:]], -1, 1, nw, nn)
    br_c, br_d, br_m = exchange([c0_top[:, :h], d[:h, :h], mf[:1, :1]], -1, -1, nw, nn)

    rpad = LPAD - h
    z3 = jnp.zeros((h, rpad, columns), jnp.float32)
    top = jnp.concatenate([z3, tl_c, top_c, tr_c, z3], axis=1)
    bot = jnp.concatenate([z3, bl_c, bot_c, br_c, z3], axis=1)
    zc = jnp.zeros((cells_x, rpad, columns), jnp.float32)
    left = jnp.concatenate([zc, lft_c], axis=1)
    right = jnp.concatenate([rgt_c, zc], axis=1)

    zd3 = jnp.zeros((h, rpad), jnp.float32)
    zdc = jnp.zeros((cells_x, rpad), jnp.float32)
    diag_ext = jnp.concatenate(
        [
            jnp.concatenate([zd3, tl_d, top_d, tr_d, zd3], axis=1),
            jnp.concatenate([zdc, lft_d, d, rgt_d, zdc], axis=1),
            jnp.concatenate([zd3, bl_d, bot_d, br_d, zd3], axis=1),
        ],
        axis=0,
    )
    mask_ext = jnp.concatenate(
        [
            jnp.concatenate([tl_m, top_m, tr_m], axis=1),
            jnp.concatenate([lft_m, mf, rgt_m], axis=1),
            jnp.concatenate([bl_m, bot_m, br_m], axis=1),
        ],
        axis=0,
    )
    reps = [h] + [TS] * tiles_x + [h]
    cell_mask_ext = jnp.repeat(
        jnp.repeat(mask_ext, jnp.array(reps), axis=0, total_repeat_length=cells_x + 2 * h), TS, axis=1
    )
    g = (cell_mask_ext * (4.0 + diag_ext) - CENTER) / HALF_WIDTH
    width = cells_y + 2 * LPAD
    g_b = jnp.broadcast_to(g[:, :, None], (cells_x + 2 * h, width, columns))
    h_t = jnp.repeat(mask_ext / HALF_WIDTH, TS, axis=1)
    h_b = jnp.broadcast_to(h_t[:, :, None], (tiles_x + 2, width, columns))

    cheb_three, ss = run_stencil(detail, cm0, m0, top, bot, left, right, g_b, h_b)
    local_squares = jnp.sum(ss, axis=0, keepdims=True)
    squares = allreduce(local_squares, nw, nn)[0]
    return cheb_three / jnp.sqrt(squares / total_cells + EPSILON)


def solution(mesh):
    in_specs = (
        P("wide", "narrow", None),
        P("wide", "narrow", None),
        P("wide", "narrow"),
        P("wide", "narrow"),
        P("wide", "narrow"),
    )
    out_specs = P("wide", "narrow", None)
    return jax.shard_map(local, mesh=mesh, in_specs=in_specs, out_specs=out_specs, check_vma=False)
```

```python
import functools

import jax
import jax.numpy as jnp
from jax import lax
from jax.experimental import pallas as pl
from jax.experimental.pallas import tpu as pltpu
from jax.sharding import PartitionSpec as P

TS = 8
CENTER = 7.5
HALF_WIDTH = 4.5
EPSILON = 1e-06

HALO = 3
LPAD = 8
RING = 16
ROWS = 8


def shift_pairs(dw, dn, nw, nn):
    pairs = []
    for w in range(nw):
        for n in range(nn):
            tw, tn = w + dw, n + dn
            if 0 <= tw < nw and 0 <= tn < nn:
                pairs.append((w * nn + n, tw * nn + tn))
    return pairs


def exchange(pieces, dw, dn, nw, nn):
    flat = jnp.concatenate([p.reshape(-1) for p in pieces])
    got = lax.ppermute(flat, ("wide", "narrow"), shift_pairs(dw, dn, nw, nn))
    out, at = [], 0
    for p in pieces:
        out.append(got[at : at + p.size].reshape(p.shape))
        at += p.size
    return out


def stencil_kernel(det_ref, cm_ref, m_ref, top_ref, bot_ref, left_ref, right_ref,
                   tl_ref, tr_ref, bl_ref, br_ref, g_ref, h_ref, out_ref, ss_ref, r0, r1, r2):
    i = pl.program_id(0)
    cx = det_ref.shape[0]
    width = g_ref.shape[1]
    ext_rows = g_ref.shape[0]
    cy = det_ref.shape[1]

    def c0_row(x):
        s = x % RING
        zero = jnp.zeros((width, det_ref.shape[2]), jnp.float32)

        @pl.when(x < HALO)
        def _():
            j = jnp.minimum(x, HALO - 1)
            r0[s] = zero
            r0[s, LPAD - HALO:LPAD] = tl_ref[j]
            r0[s, LPAD:LPAD + cy] = top_ref[j]
            r0[s, LPAD + cy:LPAD + cy + HALO] = tr_ref[j]

        @pl.when(x >= HALO + cx)
        def _():
            j = jnp.clip(x - HALO - cx, 0, HALO - 1)
            r0[s] = zero
            r0[s, LPAD - HALO:LPAD] = bl_ref[j]
            r0[s, LPAD:LPAD + cy] = bot_ref[j]
            r0[s, LPAD + cy:LPAD + cy + HALO] = br_ref[j]

        @pl.when(jnp.logical_and(x >= HALO, x < HALO + cx))
        def _():
            b = jnp.clip(x - HALO, 0, cx - 1)
            t = b // TS
            r0[s, 0:LPAD] = zero[0:LPAD]
            r0[s, LPAD - HALO:LPAD] = left_ref[b]
            r0[s, LPAD:LPAD + cy] = cm_ref[t] + m_ref[t] * det_ref[b].astype(jnp.float32)
            r0[s, LPAD + cy:width] = zero[0:width - LPAD - cy]
            r0[s, LPAD + cy:LPAD + cy + HALO] = right_ref[b]

    def apply_b(src, x):
        v = src[x % RING]
        nb = src[(x + 1) % RING] + src[(x + RING - 1) % RING]
        nb = nb + pltpu.roll(v, width - 1, 0) + pltpu.roll(v, 1, 0)
        return g_ref[x] * v - h_ref[(x + TS - HALO) // TS] * nb

    def c1_row(x):
        r1[x % RING] = apply_b(r0, x)

    def c2_row(x):
        r2[x % RING] = 2.0 * apply_b(r1, x) - r0[x % RING]

    def c3_row(x):
        c3 = 2.0 * apply_b(r2, x) - r1[x % RING]
        c3 = c3[LPAD:LPAD + cy]
        out_ref[x - HALO - ROWS * i] = c3
        sq = c3 * c3
        ss_ref[...] += jnp.sum(sq.reshape(cy // 8, 8, sq.shape[-1]), axis=0)

    def rows(fn, lo, n):
        def body(k, carry):
            fn(lo + k)
            return carry
        lax.fori_loop(0, n, body, 0)

    @pl.when(i == 0)
    def _():
        ss_ref[...] = jnp.zeros_like(ss_ref)
        rows(c0_row, 0, 2 * HALO)
        rows(c1_row, 1, 2 * HALO - 2)
        rows(c2_row, 2, 2 * HALO - 4)

    base = ROWS * i
    rows(c0_row, base + 2 * HALO, ROWS)
    rows(c1_row, base + 2 * HALO - 1, ROWS)
    rows(c2_row, base + 2 * HALO - 2, ROWS)
    rows(c3_row, base + HALO, ROWS)


def run_stencil(det, cm, m, halos, g, h):
    cx, cy, k = det.shape
    width = g.shape[1]
    steps = cx // ROWS
    vmem = pl.BlockSpec(memory_space=pltpu.VMEM)
    ops = cx * cy * k * 3 * 12
    return pl.pallas_call(
        stencil_kernel,
        grid=(steps,),
        in_specs=[vmem] * 13,
        out_specs=[
            pl.BlockSpec((ROWS, cy, k), lambda i: (i, 0, 0)),
            pl.BlockSpec((8, k), lambda i: (0, 0)),
        ],
        out_shape=[
            jax.ShapeDtypeStruct((cx, cy, k), jnp.float32),
            jax.ShapeDtypeStruct((8, k), jnp.float32),
        ],
        scratch_shapes=[pltpu.VMEM((RING, width, k), jnp.float32) for _ in range(3)],
        compiler_params=pltpu.CompilerParams(
            dimension_semantics=("arbitrary",), vmem_limit_bytes=56 * 1024 * 1024
        ),
        cost_estimate=pl.CostEstimate(
            flops=ops, transcendentals=0, bytes_accessed=det.size * 2 + cx * cy * k * 4 + g.size * 4
        ),
    )(det, cm, m, *halos, g, h)


def allreduce_kernel(nw, nn, x_ref, o_ref, r1, r2, s1, q1, s2, q2):
    me_w = lax.axis_index("wide")
    me_n = lax.axis_index("narrow")
    mesh_id = pl.DeviceIdType.MESH
    barrier = pltpu.get_barrier_semaphore()
    for k in range(1, nn):
        pl.semaphore_signal(barrier, inc=1, device_id=(me_w, (me_n + k) % nn), device_id_type=mesh_id)
    for k in range(1, nw):
        pl.semaphore_signal(barrier, inc=1, device_id=((me_w + k) % nw, me_n), device_id_type=mesh_id)
    pl.semaphore_wait(barrier, nn - 1 + nw - 1)

    def phase(src, slots, send, recv, me, n, peer_of):
        copies = []
        for k in range(1, n):
            c = pltpu.make_async_remote_copy(
                src_ref=src, dst_ref=slots.at[me], send_sem=send.at[k], recv_sem=recv.at[me],
                device_id=peer_of((me + k) % n), device_id_type=mesh_id)
            c.start()
            copies.append(c)
        slots[me] = src[...]
        for k in range(1, n):
            other = (me + k) % n
            pltpu.make_async_remote_copy(
                src_ref=src, dst_ref=slots.at[other], send_sem=send.at[k], recv_sem=recv.at[other],
                device_id=peer_of(other), device_id_type=mesh_id).wait_recv()
        for c in copies:
            c.wait_send()
        return jnp.sum(slots[...], axis=0)

    part = phase(x_ref, r1, s1, q1, me_n, nn, lambda j: (me_w, j))
    o_ref[...] = part
    o_ref[...] = phase(o_ref, r2, s2, q2, me_w, nw, lambda j: (j, me_n))


def allreduce(x, nw, nn):
    k = x.shape[-1]
    vmem = pl.BlockSpec(memory_space=pltpu.VMEM)
    return pl.pallas_call(
        functools.partial(allreduce_kernel, nw, nn),
        in_specs=[vmem],
        out_specs=vmem,
        out_shape=jax.ShapeDtypeStruct((1, k), jnp.float32),
        scratch_shapes=[
            pltpu.VMEM((nn, 1, k), jnp.float32),
            pltpu.VMEM((nw, 1, k), jnp.float32),
            pltpu.SemaphoreType.DMA((nn,)),
            pltpu.SemaphoreType.DMA((nn,)),
            pltpu.SemaphoreType.DMA((nw,)),
            pltpu.SemaphoreType.DMA((nw,)),
        ],
        compiler_params=pltpu.CompilerParams(collective_id=0, has_side_effects=True),
    )(x)


def gather_kernel(nn, cols, par_ref, ct_ref, o_ref, pslots, stage, tslots, ps, pq, ts, tq):
    me_w = lax.axis_index("wide")
    me_n = lax.axis_index("narrow")
    mesh_id = pl.DeviceIdType.MESH
    barrier = pltpu.get_barrier_semaphore()
    for k in range(1, nn):
        pl.semaphore_signal(barrier, inc=1, device_id=(me_w, (me_n + k) % nn), device_id_type=mesh_id)
    pl.semaphore_wait(barrier, nn - 1)

    def par_copy(k, other, slot):
        return pltpu.make_async_remote_copy(
            src_ref=par_ref, dst_ref=pslots.at[slot], send_sem=ps.at[k], recv_sem=pq.at[slot],
            device_id=(me_w, other), device_id_type=mesh_id)

    sent = []
    for k in range(1, nn):
        c = par_copy(k, (me_n + k) % nn, me_n)
        c.start()
        sent.append(c)

    local_cells = ct_ref.shape[1]
    ncols = local_cells // cols

    def contribution(par):
        col = par % (ncols * nn)
        idx = (par // (ncols * nn)) * ncols + col % ncols
        idx = jnp.where(col // ncols == me_n, idx, -1)
        rows = lax.broadcasted_iota(jnp.int32, (local_cells, par.shape[-1]), 0)
        onehot = (rows == idx).astype(jnp.bfloat16)
        got = jnp.dot(ct_ref[...], onehot, preferred_element_type=jnp.float32)
        return got.astype(jnp.bfloat16)

    tslots[me_n] = contribution(par_ref[...])
    out_copies = []
    for k in range(1, nn):
        other = (me_n + k) % nn
        par_copy(k, other, other).wait_recv()
        stage[k] = contribution(pslots[other])
        c = pltpu.make_async_remote_copy(
            src_ref=stage.at[k], dst_ref=tslots.at[me_n], send_sem=ts.at[k], recv_sem=tq.at[me_n],
            device_id=(me_w, other), device_id_type=mesh_id)
        c.start()
        out_copies.append(c)
    for k in range(1, nn):
        other = (me_n + k) % nn
        pltpu.make_async_remote_copy(
            src_ref=stage.at[k], dst_ref=tslots.at[other], send_sem=ts.at[k], recv_sem=tq.at[other],
            device_id=(me_w, other), device_id_type=mesh_id).wait_recv()
    for c in sent + out_copies:
        c.wait_send()
    total = tslots[0].astype(jnp.float32)
    for j in range(1, nn):
        total = total + tslots[j].astype(jnp.float32)
    o_ref[...] = total


def gather_tiles(parents, coarse, nn):
    ccx, ccy, k = coarse.shape
    par = parents.reshape(1, -1)
    n_t = par.shape[-1]
    ct = coarse.reshape(ccx * ccy, k).T
    vmem = pl.BlockSpec(memory_space=pltpu.VMEM)
    return pl.pallas_call(
        functools.partial(gather_kernel, nn, ccx),
        in_specs=[vmem, vmem],
        out_specs=vmem,
        out_shape=jax.ShapeDtypeStruct((k, n_t), jnp.float32),
        scratch_shapes=[
            pltpu.VMEM((nn, 1, n_t), jnp.int32),
            pltpu.VMEM((nn, k, n_t), jnp.bfloat16),
            pltpu.VMEM((nn, k, n_t), jnp.bfloat16),
            pltpu.SemaphoreType.DMA((nn,)),
            pltpu.SemaphoreType.DMA((nn,)),
            pltpu.SemaphoreType.DMA((nn,)),
            pltpu.SemaphoreType.DMA((nn,)),
        ],
        compiler_params=pltpu.CompilerParams(collective_id=1, has_side_effects=True),
    )(par, ct)


DIRS = ((1, 0), (-1, 0), (0, 1), (0, -1), (1, 1), (1, -1), (-1, 1), (-1, -1))


def halo_kernel(nw, nn, *refs):
    nd = len(DIRS)
    ins, outs = refs[:2 * nd], refs[2 * nd:4 * nd]
    send, recv = refs[4 * nd], refs[4 * nd + 1]
    me_w = lax.axis_index("wide")
    me_n = lax.axis_index("narrow")
    mesh_id = pl.DeviceIdType.MESH

    def inside(dw, dn, sign):
        w, n = me_w + sign * dw, me_n + sign * dn
        return jnp.logical_and(jnp.logical_and(w >= 0, w < nw), jnp.logical_and(n >= 0, n < nn))

    def clamp(v, n):
        return jnp.clip(v, 0, n - 1)

    barrier = pltpu.get_barrier_semaphore()
    count = 0
    for dw, dn in DIRS:
        ok = inside(dw, dn, 1)

        @pl.when(ok)
        def _():
            pl.semaphore_signal(barrier, inc=1, device_id=(clamp(me_w + dw, nw), clamp(me_n + dn, nn)),
                                device_id_type=mesh_id)
        count = count + ok.astype(jnp.int32)
    pl.semaphore_wait(barrier, count)

    def copy(d, p, sign):
        dw, dn = DIRS[d]
        j = 2 * d + p
        return pltpu.make_async_remote_copy(
            src_ref=ins[j], dst_ref=outs[j], send_sem=send.at[j], recv_sem=recv.at[j],
            device_id=(clamp(me_w + sign * dw, nw), clamp(me_n + sign * dn, nn)), device_id_type=mesh_id)

    for d, (dw, dn) in enumerate(DIRS):
        @pl.when(inside(dw, dn, 1))
        def _():
            for p in range(2):
                copy(d, p, 1).start()

    for d, (dw, dn) in enumerate(DIRS):
        src_ok = inside(dw, dn, -1)

        @pl.when(src_ok)
        def _():
            for p in range(2):
                copy(d, p, -1).wait_recv()

        @pl.when(jnp.logical_not(src_ok))
        def _():
            for p in range(2):
                outs[2 * d + p][...] = jnp.zeros(outs[2 * d + p].shape, outs[2 * d + p].dtype)

    for d, (dw, dn) in enumerate(DIRS):
        @pl.when(inside(dw, dn, 1))
        def _():
            for p in range(2):
                copy(d, p, 1).wait_send()


def exchange_halos(pieces, nw, nn):
    vmem = pl.BlockSpec(memory_space=pltpu.VMEM)
    n = len(pieces)
    return pl.pallas_call(
        functools.partial(halo_kernel, nw, nn),
        in_specs=[vmem] * n,
        out_specs=[vmem] * n,
        out_shape=[jax.ShapeDtypeStruct(p.shape, p.dtype) for p in pieces],
        scratch_shapes=[pltpu.SemaphoreType.DMA((n,)), pltpu.SemaphoreType.DMA((n,))],
        compiler_params=pltpu.CompilerParams(collective_id=2, has_side_effects=True),
    )(*pieces)


def local(detail, coarse, diagonal, parents, tile_mask):
    tiles_x, tiles_y = parents.shape
    cells_x, cells_y, columns = detail.shape
    nw, nn = lax.axis_size("wide"), lax.axis_size("narrow")
    total_cells = cells_x * nw * cells_y * nn
    mask_float = tile_mask.astype(jnp.float32)

    tile_values = gather_tiles(parents, coarse, nn).T
    tv = tile_values.reshape(tiles_x, tiles_y, columns)

    m_rows = jnp.repeat(mask_float, TS, axis=1)
    m0 = jnp.broadcast_to(m_rows[:, :, None], (tiles_x, cells_y, columns))
    cm0 = m0 * jnp.repeat(tv, TS, axis=1)

    h = HALO
    c0_top = cm0[0][None] + m0[0][None] * detail[:h].astype(jnp.float32)
    c0_bot = cm0[-1][None] + m0[-1][None] * detail[-h:].astype(jnp.float32)
    cm_rep = jnp.repeat(cm0, TS, axis=0)
    m_rep = jnp.repeat(m0, TS, axis=0)
    c0_left = cm_rep[:, :h] + m_rep[:, :h] * detail[:, :h].astype(jnp.float32)
    c0_right = cm_rep[:, -h:] + m_rep[:, -h:] * detail[:, -h:].astype(jnp.float32)

    cell_mask = jnp.repeat(jnp.repeat(mask_float, TS, axis=0), TS, axis=1)
    g_own = (cell_mask * (4.0 + diagonal) - CENTER) / HALF_WIDTH
    h_own = cell_mask / HALF_WIDTH
    gh = jnp.stack([g_own, h_own])

    def edge(a, dw, dn, rows_axis, cols_axis):
        idx = [slice(None)] * a.ndim
        if dw == 1:
            idx[rows_axis] = slice(a.shape[rows_axis] - h, None)
        elif dw == -1:
            idx[rows_axis] = slice(0, h)
        if dn == 1:
            idx[cols_axis] = slice(a.shape[cols_axis] - h, None)
        elif dn == -1:
            idx[cols_axis] = slice(0, h)
        return a[tuple(idx)]

    c0_pieces = {
        (1, 0): c0_bot, (-1, 0): c0_top, (0, 1): c0_right, (0, -1): c0_left,
        (1, 1): c0_bot[:, -h:], (1, -1): c0_bot[:, :h], (-1, 1): c0_top[:, -h:], (-1, -1): c0_top[:, :h],
    }
    pieces = []
    for dw, dn in DIRS:
        pieces.append(c0_pieces[(dw, dn)])
        pieces.append(edge(gh, dw, dn, 1, 2))
    got = exchange_halos(pieces, nw, nn)
    hc = {dirn: got[2 * k] for k, dirn in enumerate(DIRS)}
    hg = {dirn: got[2 * k + 1] for k, dirn in enumerate(DIRS)}
    halos = [hc[(1, 0)], hc[(-1, 0)], hc[(0, 1)], hc[(0, -1)],
             hc[(1, 1)], hc[(1, -1)], hc[(-1, 1)], hc[(-1, -1)]]

    rpad = LPAD - h
    z3 = jnp.zeros((2, h, rpad), jnp.float32)
    zc = jnp.zeros((2, cells_x, rpad), jnp.float32)
    gh_ext = jnp.concatenate(
        [
            jnp.concatenate([z3, hg[(1, 1)], hg[(1, 0)], hg[(1, -1)], z3], axis=2),
            jnp.concatenate([zc, hg[(0, 1)], gh, hg[(0, -1)], zc], axis=2),
            jnp.concatenate([z3, hg[(-1, 1)], hg[(-1, 0)], hg[(-1, -1)], z3], axis=2),
        ],
        axis=1,
    )
    width = cells_y + 2 * LPAD
    g_b = jnp.broadcast_to(gh_ext[0][:, :, None], (cells_x + 2 * h, width, columns))
    h_rows = gh_ext[1][jnp.array([0] + [h + TS * t for t in range(tiles_x)] + [h + cells_x])]
    h_b = jnp.broadcast_to(h_rows[:, :, None], (tiles_x + 2, width, columns))

    cheb_three, ss = run_stencil(detail, cm0, m0, halos, g_b, h_b)
    local_squares = jnp.sum(ss, axis=0, keepdims=True)
    squares = allreduce(local_squares, nw, nn)[0]
    return cheb_three / jnp.sqrt(squares / total_cells + EPSILON)


def solution(mesh):
    in_specs = (
        P("wide", "narrow", None),
        P("wide", "narrow", None),
        P("wide", "narrow"),
        P("wide", "narrow"),
        P("wide", "narrow"),
    )
    out_specs = P("wide", "narrow", None)
    return jax.shard_map(local, mesh=mesh, in_specs=in_specs, out_specs=out_specs, check_vma=False)
```

```python
import functools

import jax
import jax.numpy as jnp
from jax import lax
from jax.experimental import pallas as pl
from jax.experimental.pallas import tpu as pltpu
from jax.sharding import PartitionSpec as P

TS = 8
CENTER = 7.5
HALF_WIDTH = 4.5
EPSILON = 1e-06

HALO = 3
LPAD = 8
RING = 16
ROWS = 8


def shift_pairs(dw, dn, nw, nn):
    pairs = []
    for w in range(nw):
        for n in range(nn):
            tw, tn = w + dw, n + dn
            if 0 <= tw < nw and 0 <= tn < nn:
                pairs.append((w * nn + n, tw * nn + tn))
    return pairs


def exchange(pieces, dw, dn, nw, nn):
    flat = jnp.concatenate([p.reshape(-1) for p in pieces])
    got = lax.ppermute(flat, ("wide", "narrow"), shift_pairs(dw, dn, nw, nn))
    out, at = [], 0
    for p in pieces:
        out.append(got[at : at + p.size].reshape(p.shape))
        at += p.size
    return out


def stencil_kernel(det_ref, cm_ref, m_ref, top_ref, bot_ref, left_ref, right_ref,
                   tl_ref, tr_ref, bl_ref, br_ref, g_ref, h_ref, out_ref, ss_ref, r0, r1, r2):
    i = pl.program_id(0)
    cx = det_ref.shape[0]
    width = g_ref.shape[1]
    ext_rows = g_ref.shape[0]
    cy = det_ref.shape[1]

    def c0_row(x):
        s = x % RING
        zero = jnp.zeros((width, det_ref.shape[2]), jnp.float32)

        @pl.when(x < HALO)
        def _():
            j = jnp.minimum(x, HALO - 1)
            r0[s] = zero
            r0[s, LPAD - HALO:LPAD] = tl_ref[j]
            r0[s, LPAD:LPAD + cy] = top_ref[j]
            r0[s, LPAD + cy:LPAD + cy + HALO] = tr_ref[j]

        @pl.when(x >= HALO + cx)
        def _():
            j = jnp.clip(x - HALO - cx, 0, HALO - 1)
            r0[s] = zero
            r0[s, LPAD - HALO:LPAD] = bl_ref[j]
            r0[s, LPAD:LPAD + cy] = bot_ref[j]
            r0[s, LPAD + cy:LPAD + cy + HALO] = br_ref[j]

        @pl.when(jnp.logical_and(x >= HALO, x < HALO + cx))
        def _():
            b = jnp.clip(x - HALO, 0, cx - 1)
            t = b // TS
            r0[s, 0:LPAD] = zero[0:LPAD]
            for p in range(HALO):
                r0[s, pl.ds(LPAD - HALO + p, 1)] = left_ref[p, pl.ds(b, 1)]
            r0[s, LPAD:LPAD + cy] = cm_ref[t] + m_ref[t] * det_ref[b].astype(jnp.float32)
            r0[s, LPAD + cy:width] = zero[0:width - LPAD - cy]
            for p in range(HALO):
                r0[s, pl.ds(LPAD + cy + p, 1)] = right_ref[p, pl.ds(b, 1)]

    def apply_b(src, x):
        v = src[x % RING]
        nb = src[(x + 1) % RING] + src[(x + RING - 1) % RING]
        nb = nb + pltpu.roll(v, width - 1, 0) + pltpu.roll(v, 1, 0)
        return g_ref[x] * v - h_ref[(x + TS - HALO) // TS] * nb

    def c1_row(x):
        r1[x % RING] = apply_b(r0, x)

    def c2_row(x):
        r2[x % RING] = 2.0 * apply_b(r1, x) - r0[x % RING]

    def c3_row(x):
        c3 = 2.0 * apply_b(r2, x) - r1[x % RING]
        c3 = c3[LPAD:LPAD + cy]
        out_ref[x - HALO - ROWS * i] = c3
        sq = c3 * c3
        ss_ref[...] += jnp.sum(sq.reshape(cy // 8, 8, sq.shape[-1]), axis=0)

    def rows(fn, lo, n):
        def body(k, carry):
            fn(lo + k)
            return carry
        lax.fori_loop(0, n, body, 0)

    @pl.when(i == 0)
    def _():
        ss_ref[...] = jnp.zeros_like(ss_ref)
        rows(c0_row, 0, 2 * HALO)
        rows(c1_row, 1, 2 * HALO - 2)
        rows(c2_row, 2, 2 * HALO - 4)

    base = ROWS * i
    rows(c0_row, base + 2 * HALO, ROWS)
    rows(c1_row, base + 2 * HALO - 1, ROWS)
    rows(c2_row, base + 2 * HALO - 2, ROWS)
    rows(c3_row, base + HALO, ROWS)


def run_stencil(det, cm, m, halos, g, h):
    cx, cy, k = det.shape
    width = g.shape[1]
    steps = cx // ROWS
    vmem = pl.BlockSpec(memory_space=pltpu.VMEM)
    ops = cx * cy * k * 3 * 12
    return pl.pallas_call(
        stencil_kernel,
        grid=(steps,),
        in_specs=[vmem] * 13,
        out_specs=[
            pl.BlockSpec((ROWS, cy, k), lambda i: (i, 0, 0)),
            pl.BlockSpec((8, k), lambda i: (0, 0)),
        ],
        out_shape=[
            jax.ShapeDtypeStruct((cx, cy, k), jnp.float32),
            jax.ShapeDtypeStruct((8, k), jnp.float32),
        ],
        scratch_shapes=[pltpu.VMEM((RING, width, k), jnp.float32) for _ in range(3)],
        compiler_params=pltpu.CompilerParams(
            dimension_semantics=("arbitrary",), vmem_limit_bytes=56 * 1024 * 1024
        ),
        cost_estimate=pl.CostEstimate(
            flops=ops, transcendentals=0, bytes_accessed=det.size * 2 + cx * cy * k * 4 + g.size * 4
        ),
    )(det, cm, m, *halos, g, h)


def allreduce_kernel(nw, nn, x_ref, o_ref, r1, r2, s1, q1, s2, q2):
    me_w = lax.axis_index("wide")
    me_n = lax.axis_index("narrow")
    mesh_id = pl.DeviceIdType.MESH
    barrier = pltpu.get_barrier_semaphore()
    for k in range(1, nn):
        pl.semaphore_signal(barrier, inc=1, device_id=(me_w, (me_n + k) % nn), device_id_type=mesh_id)
    for k in range(1, nw):
        pl.semaphore_signal(barrier, inc=1, device_id=((me_w + k) % nw, me_n), device_id_type=mesh_id)
    pl.semaphore_wait(barrier, nn - 1 + nw - 1)

    def phase(src, slots, send, recv, me, n, peer_of):
        copies = []
        for k in range(1, n):
            c = pltpu.make_async_remote_copy(
                src_ref=src, dst_ref=slots.at[me], send_sem=send.at[k], recv_sem=recv.at[me],
                device_id=peer_of((me + k) % n), device_id_type=mesh_id)
            c.start()
            copies.append(c)
        slots[me] = src[...]
        for k in range(1, n):
            other = (me + k) % n
            pltpu.make_async_remote_copy(
                src_ref=src, dst_ref=slots.at[other], send_sem=send.at[k], recv_sem=recv.at[other],
                device_id=peer_of(other), device_id_type=mesh_id).wait_recv()
        for c in copies:
            c.wait_send()
        return jnp.sum(slots[...], axis=0)

    part = phase(x_ref, r1, s1, q1, me_n, nn, lambda j: (me_w, j))
    o_ref[...] = part
    o_ref[...] = phase(o_ref, r2, s2, q2, me_w, nw, lambda j: (j, me_n))


def allreduce(x, nw, nn):
    k = x.shape[-1]
    vmem = pl.BlockSpec(memory_space=pltpu.VMEM)
    return pl.pallas_call(
        functools.partial(allreduce_kernel, nw, nn),
        in_specs=[vmem],
        out_specs=vmem,
        out_shape=jax.ShapeDtypeStruct((1, k), jnp.float32),
        scratch_shapes=[
            pltpu.VMEM((nn, 1, k), jnp.float32),
            pltpu.VMEM((nw, 1, k), jnp.float32),
            pltpu.SemaphoreType.DMA((nn,)),
            pltpu.SemaphoreType.DMA((nn,)),
            pltpu.SemaphoreType.DMA((nw,)),
            pltpu.SemaphoreType.DMA((nw,)),
        ],
        compiler_params=pltpu.CompilerParams(collective_id=0, has_side_effects=True),
    )(x)


def gather_kernel(nn, cols, par_ref, ct_ref, o_ref, pslots, stage, tslots, ps, pq, ts, tq):
    me_w = lax.axis_index("wide")
    me_n = lax.axis_index("narrow")
    mesh_id = pl.DeviceIdType.MESH
    barrier = pltpu.get_barrier_semaphore()
    for k in range(1, nn):
        pl.semaphore_signal(barrier, inc=1, device_id=(me_w, (me_n + k) % nn), device_id_type=mesh_id)
    pl.semaphore_wait(barrier, nn - 1)

    def par_copy(k, other, slot):
        return pltpu.make_async_remote_copy(
            src_ref=par_ref, dst_ref=pslots.at[slot], send_sem=ps.at[k], recv_sem=pq.at[slot],
            device_id=(me_w, other), device_id_type=mesh_id)

    sent = []
    for k in range(1, nn):
        c = par_copy(k, (me_n + k) % nn, me_n)
        c.start()
        sent.append(c)

    local_cells = ct_ref.shape[1]
    ncols = local_cells // cols

    def contribution(par):
        col = par % (ncols * nn)
        idx = (par // (ncols * nn)) * ncols + col % ncols
        idx = jnp.where(col // ncols == me_n, idx, -1)
        rows = lax.broadcasted_iota(jnp.int32, (local_cells, par.shape[-1]), 0)
        onehot = (rows == idx).astype(jnp.bfloat16)
        got = jnp.dot(ct_ref[...], onehot, preferred_element_type=jnp.float32)
        return got.astype(jnp.bfloat16)

    tslots[me_n] = contribution(par_ref[...])
    out_copies = []
    for k in range(1, nn):
        other = (me_n + k) % nn
        par_copy(k, other, other).wait_recv()
        stage[k] = contribution(pslots[other])
        c = pltpu.make_async_remote_copy(
            src_ref=stage.at[k], dst_ref=tslots.at[me_n], send_sem=ts.at[k], recv_sem=tq.at[me_n],
            device_id=(me_w, other), device_id_type=mesh_id)
        c.start()
        out_copies.append(c)
    for k in range(1, nn):
        other = (me_n + k) % nn
        pltpu.make_async_remote_copy(
            src_ref=stage.at[k], dst_ref=tslots.at[other], send_sem=ts.at[k], recv_sem=tq.at[other],
            device_id=(me_w, other), device_id_type=mesh_id).wait_recv()
    for c in sent + out_copies:
        c.wait_send()
    total = tslots[0].astype(jnp.float32)
    for j in range(1, nn):
        total = total + tslots[j].astype(jnp.float32)
    o_ref[...] = total


def gather_tiles(parents, coarse, nn):
    ccx, ccy, k = coarse.shape
    par = parents.reshape(1, -1)
    n_t = par.shape[-1]
    ct = coarse.reshape(ccx * ccy, k).T
    vmem = pl.BlockSpec(memory_space=pltpu.VMEM)
    return pl.pallas_call(
        functools.partial(gather_kernel, nn, ccx),
        in_specs=[vmem, vmem],
        out_specs=vmem,
        out_shape=jax.ShapeDtypeStruct((k, n_t), jnp.float32),
        scratch_shapes=[
            pltpu.VMEM((nn, 1, n_t), jnp.int32),
            pltpu.VMEM((nn, k, n_t), jnp.bfloat16),
            pltpu.VMEM((nn, k, n_t), jnp.bfloat16),
            pltpu.SemaphoreType.DMA((nn,)),
            pltpu.SemaphoreType.DMA((nn,)),
            pltpu.SemaphoreType.DMA((nn,)),
            pltpu.SemaphoreType.DMA((nn,)),
        ],
        compiler_params=pltpu.CompilerParams(collective_id=1, has_side_effects=True),
    )(par, ct)


DIRS = ((1, 0), (-1, 0), (0, 1), (0, -1), (1, 1), (1, -1), (-1, 1), (-1, -1))


def halo_kernel(nw, nn, *refs):
    nd = len(DIRS)
    ins, outs = refs[:2 * nd], refs[2 * nd:4 * nd]
    send, recv = refs[4 * nd], refs[4 * nd + 1]
    me_w = lax.axis_index("wide")
    me_n = lax.axis_index("narrow")
    mesh_id = pl.DeviceIdType.MESH

    def inside(dw, dn, sign):
        w, n = me_w + sign * dw, me_n + sign * dn
        return jnp.logical_and(jnp.logical_and(w >= 0, w < nw), jnp.logical_and(n >= 0, n < nn))

    def clamp(v, n):
        return jnp.clip(v, 0, n - 1)

    barrier = pltpu.get_barrier_semaphore()
    count = 0
    for dw, dn in DIRS:
        ok = inside(dw, dn, 1)

        @pl.when(ok)
        def _():
            pl.semaphore_signal(barrier, inc=1, device_id=(clamp(me_w + dw, nw), clamp(me_n + dn, nn)),
                                device_id_type=mesh_id)
        count = count + ok.astype(jnp.int32)
    pl.semaphore_wait(barrier, count)

    def copy(d, p, sign):
        dw, dn = DIRS[d]
        j = 2 * d + p
        return pltpu.make_async_remote_copy(
            src_ref=ins[j], dst_ref=outs[j], send_sem=send.at[j], recv_sem=recv.at[j],
            device_id=(clamp(me_w + sign * dw, nw), clamp(me_n + sign * dn, nn)), device_id_type=mesh_id)

    for d, (dw, dn) in enumerate(DIRS):
        @pl.when(inside(dw, dn, 1))
        def _():
            for p in range(2):
                copy(d, p, 1).start()

    for d, (dw, dn) in enumerate(DIRS):
        src_ok = inside(dw, dn, -1)

        @pl.when(src_ok)
        def _():
            for p in range(2):
                copy(d, p, -1).wait_recv()

        @pl.when(jnp.logical_not(src_ok))
        def _():
            for p in range(2):
                outs[2 * d + p][...] = jnp.zeros(outs[2 * d + p].shape, outs[2 * d + p].dtype)

    for d, (dw, dn) in enumerate(DIRS):
        @pl.when(inside(dw, dn, 1))
        def _():
            for p in range(2):
                copy(d, p, 1).wait_send()


def exchange_halos(pieces, nw, nn):
    vmem = pl.BlockSpec(memory_space=pltpu.VMEM)
    n = len(pieces)
    return pl.pallas_call(
        functools.partial(halo_kernel, nw, nn),
        in_specs=[vmem] * n,
        out_specs=[vmem] * n,
        out_shape=[jax.ShapeDtypeStruct(p.shape, p.dtype) for p in pieces],
        scratch_shapes=[pltpu.SemaphoreType.DMA((n,)), pltpu.SemaphoreType.DMA((n,))],
        compiler_params=pltpu.CompilerParams(collective_id=2, has_side_effects=True),
    )(*pieces)


def scale_kernel(x_ref, s_ref, o_ref):
    o_ref[...] = x_ref[...] * s_ref[...]


def scale_rows(x, inv):
    cx, cy, k = x.shape
    return pl.pallas_call(
        scale_kernel,
        grid=(cx // ROWS,),
        in_specs=[pl.BlockSpec((ROWS, cy, k), lambda i: (i, 0, 0)), pl.BlockSpec((1, k), lambda i: (0, 0))],
        out_specs=pl.BlockSpec((ROWS, cy, k), lambda i: (i, 0, 0)),
        out_shape=jax.ShapeDtypeStruct(x.shape, x.dtype),
        input_output_aliases={0: 0},
        cost_estimate=pl.CostEstimate(flops=x.size, transcendentals=0, bytes_accessed=x.size * 8),
    )(x, inv)


def local(detail, coarse, diagonal, parents, tile_mask):
    tiles_x, tiles_y = parents.shape
    cells_x, cells_y, columns = detail.shape
    nw, nn = lax.axis_size("wide"), lax.axis_size("narrow")
    total_cells = cells_x * nw * cells_y * nn
    mask_float = tile_mask.astype(jnp.float32)

    tile_values = gather_tiles(parents, coarse, nn).T
    tv = tile_values.reshape(tiles_x, tiles_y, columns)

    m_rows = jnp.repeat(mask_float, TS, axis=1)
    m0 = jnp.broadcast_to(m_rows[:, :, None], (tiles_x, cells_y, columns))
    cm0 = m0 * jnp.repeat(tv, TS, axis=1)

    h = HALO
    c0_top = cm0[0][None] + m0[0][None] * detail[:h].astype(jnp.float32)
    c0_bot = cm0[-1][None] + m0[-1][None] * detail[-h:].astype(jnp.float32)
    cm_rep = jnp.repeat(cm0, TS, axis=0)
    m_rep = jnp.repeat(m0, TS, axis=0)
    c0_left = cm_rep[:, :h] + m_rep[:, :h] * detail[:, :h].astype(jnp.float32)
    c0_right = cm_rep[:, -h:] + m_rep[:, -h:] * detail[:, -h:].astype(jnp.float32)

    cell_mask = jnp.repeat(jnp.repeat(mask_float, TS, axis=0), TS, axis=1)
    g_own = (cell_mask * (4.0 + diagonal) - CENTER) / HALF_WIDTH
    h_own = cell_mask / HALF_WIDTH
    gh = jnp.stack([g_own, h_own])

    def edge(a, dw, dn, rows_axis, cols_axis):
        idx = [slice(None)] * a.ndim
        if dw == 1:
            idx[rows_axis] = slice(a.shape[rows_axis] - h, None)
        elif dw == -1:
            idx[rows_axis] = slice(0, h)
        if dn == 1:
            idx[cols_axis] = slice(a.shape[cols_axis] - h, None)
        elif dn == -1:
            idx[cols_axis] = slice(0, h)
        return a[tuple(idx)]

    c0_pieces = {
        (1, 0): c0_bot, (-1, 0): c0_top,
        (0, 1): c0_right.transpose(1, 0, 2), (0, -1): c0_left.transpose(1, 0, 2),
        (1, 1): c0_bot[:, -h:], (1, -1): c0_bot[:, :h], (-1, 1): c0_top[:, -h:], (-1, -1): c0_top[:, :h],
    }
    pieces = []
    for dw, dn in DIRS:
        pieces.append(c0_pieces[(dw, dn)])
        e = edge(gh, dw, dn, 1, 2)
        pieces.append(e.transpose(0, 2, 1) if dw == 0 else e)
    got = exchange_halos(pieces, nw, nn)
    hc = {dirn: got[2 * k] for k, dirn in enumerate(DIRS)}
    hg = {dirn: got[2 * k + 1] for k, dirn in enumerate(DIRS)}
    for dirn in ((0, 1), (0, -1)):
        hg[dirn] = hg[dirn].transpose(0, 2, 1)
    halos = [hc[(1, 0)], hc[(-1, 0)], hc[(0, 1)], hc[(0, -1)],
             hc[(1, 1)], hc[(1, -1)], hc[(-1, 1)], hc[(-1, -1)]]

    rpad = LPAD - h
    z3 = jnp.zeros((2, h, rpad), jnp.float32)
    zc = jnp.zeros((2, cells_x, rpad), jnp.float32)
    gh_ext = jnp.concatenate(
        [
            jnp.concatenate([z3, hg[(1, 1)], hg[(1, 0)], hg[(1, -1)], z3], axis=2),
            jnp.concatenate([zc, hg[(0, 1)], gh, hg[(0, -1)], zc], axis=2),
            jnp.concatenate([z3, hg[(-1, 1)], hg[(-1, 0)], hg[(-1, -1)], z3], axis=2),
        ],
        axis=1,
    )
    width = cells_y + 2 * LPAD
    g_b = jnp.broadcast_to(gh_ext[0][:, :, None], (cells_x + 2 * h, width, columns))
    h_rows = gh_ext[1][jnp.array([0] + [h + TS * t for t in range(tiles_x)] + [h + cells_x])]
    h_b = jnp.broadcast_to(h_rows[:, :, None], (tiles_x + 2, width, columns))

    cheb_three, ss = run_stencil(detail, cm0, m0, halos, g_b, h_b)
    local_squares = jnp.sum(ss, axis=0, keepdims=True)
    squares = allreduce(local_squares, nw, nn)
    inv = 1.0 / jnp.sqrt(squares / total_cells + EPSILON)
    return scale_rows(cheb_three, inv)


def solution(mesh):
    in_specs = (
        P("wide", "narrow", None),
        P("wide", "narrow", None),
        P("wide", "narrow"),
        P("wide", "narrow"),
        P("wide", "narrow"),
    )
    out_specs = P("wide", "narrow", None)
    return jax.shard_map(local, mesh=mesh, in_specs=in_specs, out_specs=out_specs, check_vma=False)
```

```python
import functools

import jax
import jax.numpy as jnp
from jax import lax
from jax.experimental import pallas as pl
from jax.experimental.pallas import tpu as pltpu
from jax.sharding import PartitionSpec as P

TS = 8
CENTER = 7.5
HALF_WIDTH = 4.5
EPSILON = 1e-06

HALO = 3
LPAD = 8
RING = 16
ROWS = 8
SCALE_ROWS = 32


def shift_pairs(dw, dn, nw, nn):
    pairs = []
    for w in range(nw):
        for n in range(nn):
            tw, tn = w + dw, n + dn
            if 0 <= tw < nw and 0 <= tn < nn:
                pairs.append((w * nn + n, tw * nn + tn))
    return pairs


def exchange(pieces, dw, dn, nw, nn):
    flat = jnp.concatenate([p.reshape(-1) for p in pieces])
    got = lax.ppermute(flat, ("wide", "narrow"), shift_pairs(dw, dn, nw, nn))
    out, at = [], 0
    for p in pieces:
        out.append(got[at : at + p.size].reshape(p.shape))
        at += p.size
    return out


def stencil_kernel(det_ref, cm_ref, m_ref, top_ref, bot_ref, left_ref, right_ref,
                   tl_ref, tr_ref, bl_ref, br_ref, g_ref, h_ref, out_ref, ss_ref, r0, r1, r2):
    i = pl.program_id(0)
    cx = det_ref.shape[0]
    width = g_ref.shape[1]
    ext_rows = g_ref.shape[0]
    cy = det_ref.shape[1]

    def c0_row(x):
        s = x % RING
        zero = jnp.zeros((width, det_ref.shape[2]), jnp.float32)

        @pl.when(x < HALO)
        def _():
            j = jnp.minimum(x, HALO - 1)
            r0[s] = zero
            r0[s, LPAD - HALO:LPAD] = tl_ref[j]
            r0[s, LPAD:LPAD + cy] = top_ref[j]
            r0[s, LPAD + cy:LPAD + cy + HALO] = tr_ref[j]

        @pl.when(x >= HALO + cx)
        def _():
            j = jnp.clip(x - HALO - cx, 0, HALO - 1)
            r0[s] = zero
            r0[s, LPAD - HALO:LPAD] = bl_ref[j]
            r0[s, LPAD:LPAD + cy] = bot_ref[j]
            r0[s, LPAD + cy:LPAD + cy + HALO] = br_ref[j]

        @pl.when(jnp.logical_and(x >= HALO, x < HALO + cx))
        def _():
            b = jnp.clip(x - HALO, 0, cx - 1)
            t = b // TS
            r0[s, 0:LPAD] = zero[0:LPAD]
            for p in range(HALO):
                r0[s, pl.ds(LPAD - HALO + p, 1)] = left_ref[p, pl.ds(b, 1)]
            r0[s, LPAD:LPAD + cy] = cm_ref[t] + m_ref[t] * det_ref[b].astype(jnp.float32)
            r0[s, LPAD + cy:width] = zero[0:width - LPAD - cy]
            for p in range(HALO):
                r0[s, pl.ds(LPAD + cy + p, 1)] = right_ref[p, pl.ds(b, 1)]

    def apply_b(src, x):
        v = src[x % RING]
        nb = src[(x + 1) % RING] + src[(x + RING - 1) % RING]
        nb = nb + pltpu.roll(v, width - 1, 0) + pltpu.roll(v, 1, 0)
        return g_ref[x] * v - h_ref[(x + TS - HALO) // TS] * nb

    def c1_row(x):
        r1[x % RING] = apply_b(r0, x)

    def c2_row(x):
        r2[x % RING] = 2.0 * apply_b(r1, x) - r0[x % RING]

    def c3_row(x):
        c3 = 2.0 * apply_b(r2, x) - r1[x % RING]
        c3 = c3[LPAD:LPAD + cy]
        out_ref[x - HALO - ROWS * i] = c3
        sq = c3 * c3
        ss_ref[...] += jnp.sum(sq.reshape(cy // 8, 8, sq.shape[-1]), axis=0)

    def rows(fn, lo, n):
        def body(k, carry):
            fn(lo + k)
            return carry
        lax.fori_loop(0, n, body, 0)

    @pl.when(i == 0)
    def _():
        ss_ref[...] = jnp.zeros_like(ss_ref)
        rows(c0_row, 0, 2 * HALO)
        rows(c1_row, 1, 2 * HALO - 2)
        rows(c2_row, 2, 2 * HALO - 4)

    base = ROWS * i
    rows(c0_row, base + 2 * HALO, ROWS)
    rows(c1_row, base + 2 * HALO - 1, ROWS)
    rows(c2_row, base + 2 * HALO - 2, ROWS)
    rows(c3_row, base + HALO, ROWS)


def run_stencil(det, cm, m, halos, g, h):
    cx, cy, k = det.shape
    width = g.shape[1]
    steps = cx // ROWS
    vmem = pl.BlockSpec(memory_space=pltpu.VMEM)
    ops = cx * cy * k * 3 * 12
    return pl.pallas_call(
        stencil_kernel,
        grid=(steps,),
        in_specs=[vmem] * 13,
        out_specs=[
            pl.BlockSpec((ROWS, cy, k), lambda i: (i, 0, 0)),
            pl.BlockSpec((8, k), lambda i: (0, 0)),
        ],
        out_shape=[
            jax.ShapeDtypeStruct((cx, cy, k), jnp.float32),
            jax.ShapeDtypeStruct((8, k), jnp.float32),
        ],
        scratch_shapes=[pltpu.VMEM((RING, width, k), jnp.float32) for _ in range(3)],
        compiler_params=pltpu.CompilerParams(
            dimension_semantics=("arbitrary",), vmem_limit_bytes=56 * 1024 * 1024
        ),
        cost_estimate=pl.CostEstimate(
            flops=ops, transcendentals=0, bytes_accessed=det.size * 2 + cx * cy * k * 4 + g.size * 4
        ),
    )(det, cm, m, *halos, g, h)


def allreduce_kernel(nw, nn, x_ref, o_ref, r1, r2, s1, q1, s2, q2):
    me_w = lax.axis_index("wide")
    me_n = lax.axis_index("narrow")
    mesh_id = pl.DeviceIdType.MESH
    barrier = pltpu.get_barrier_semaphore()
    for k in range(1, nn):
        pl.semaphore_signal(barrier, inc=1, device_id=(me_w, (me_n + k) % nn), device_id_type=mesh_id)
    for k in range(1, nw):
        pl.semaphore_signal(barrier, inc=1, device_id=((me_w + k) % nw, me_n), device_id_type=mesh_id)
    pl.semaphore_wait(barrier, nn - 1 + nw - 1)

    def phase(src, slots, send, recv, me, n, peer_of):
        copies = []
        for k in range(1, n):
            c = pltpu.make_async_remote_copy(
                src_ref=src, dst_ref=slots.at[me], send_sem=send.at[k], recv_sem=recv.at[me],
                device_id=peer_of((me + k) % n), device_id_type=mesh_id)
            c.start()
            copies.append(c)
        slots[me] = src[...]
        for k in range(1, n):
            other = (me + k) % n
            pltpu.make_async_remote_copy(
                src_ref=src, dst_ref=slots.at[other], send_sem=send.at[k], recv_sem=recv.at[other],
                device_id=peer_of(other), device_id_type=mesh_id).wait_recv()
        for c in copies:
            c.wait_send()
        return jnp.sum(slots[...], axis=0)

    part = phase(x_ref, r1, s1, q1, me_n, nn, lambda j: (me_w, j))
    o_ref[...] = part
    o_ref[...] = phase(o_ref, r2, s2, q2, me_w, nw, lambda j: (j, me_n))


def allreduce(x, nw, nn):
    k = x.shape[-1]
    vmem = pl.BlockSpec(memory_space=pltpu.VMEM)
    return pl.pallas_call(
        functools.partial(allreduce_kernel, nw, nn),
        in_specs=[vmem],
        out_specs=vmem,
        out_shape=jax.ShapeDtypeStruct((1, k), jnp.float32),
        scratch_shapes=[
            pltpu.VMEM((nn, 1, k), jnp.float32),
            pltpu.VMEM((nw, 1, k), jnp.float32),
            pltpu.SemaphoreType.DMA((nn,)),
            pltpu.SemaphoreType.DMA((nn,)),
            pltpu.SemaphoreType.DMA((nw,)),
            pltpu.SemaphoreType.DMA((nw,)),
        ],
        compiler_params=pltpu.CompilerParams(collective_id=0, has_side_effects=True),
    )(x)


def gather_kernel(nn, cols, par_ref, ct_ref, o_ref, pslots, stage, tslots, ps, pq, ts, tq):
    me_w = lax.axis_index("wide")
    me_n = lax.axis_index("narrow")
    mesh_id = pl.DeviceIdType.MESH
    barrier = pltpu.get_barrier_semaphore()
    for k in range(1, nn):
        pl.semaphore_signal(barrier, inc=1, device_id=(me_w, (me_n + k) % nn), device_id_type=mesh_id)
    pl.semaphore_wait(barrier, nn - 1)

    def par_copy(k, other, slot):
        return pltpu.make_async_remote_copy(
            src_ref=par_ref, dst_ref=pslots.at[slot], send_sem=ps.at[k], recv_sem=pq.at[slot],
            device_id=(me_w, other), device_id_type=mesh_id)

    sent = []
    for k in range(1, nn):
        c = par_copy(k, (me_n + k) % nn, me_n)
        c.start()
        sent.append(c)

    local_cells = ct_ref.shape[1]
    ncols = local_cells // cols

    def contribution(par):
        col = par % (ncols * nn)
        idx = (par // (ncols * nn)) * ncols + col % ncols
        idx = jnp.where(col // ncols == me_n, idx, -1)
        rows = lax.broadcasted_iota(jnp.int32, (local_cells, par.shape[-1]), 0)
        onehot = (rows == idx).astype(jnp.bfloat16)
        got = jnp.dot(ct_ref[...], onehot, preferred_element_type=jnp.float32)
        return got.astype(jnp.bfloat16)

    tslots[me_n] = contribution(par_ref[...])
    out_copies = []
    for k in range(1, nn):
        other = (me_n + k) % nn
        par_copy(k, other, other).wait_recv()
        stage[k] = contribution(pslots[other])
        c = pltpu.make_async_remote_copy(
            src_ref=stage.at[k], dst_ref=tslots.at[me_n], send_sem=ts.at[k], recv_sem=tq.at[me_n],
            device_id=(me_w, other), device_id_type=mesh_id)
        c.start()
        out_copies.append(c)
    for k in range(1, nn):
        other = (me_n + k) % nn
        pltpu.make_async_remote_copy(
            src_ref=stage.at[k], dst_ref=tslots.at[other], send_sem=ts.at[k], recv_sem=tq.at[other],
            device_id=(me_w, other), device_id_type=mesh_id).wait_recv()
    for c in sent + out_copies:
        c.wait_send()
    total = tslots[0].astype(jnp.float32)
    for j in range(1, nn):
        total = total + tslots[j].astype(jnp.float32)
    o_ref[...] = total


def gather_tiles(parents, coarse, nn):
    ccx, ccy, k = coarse.shape
    par = parents.reshape(1, -1)
    n_t = par.shape[-1]
    ct = coarse.reshape(ccx * ccy, k).T
    vmem = pl.BlockSpec(memory_space=pltpu.VMEM)
    return pl.pallas_call(
        functools.partial(gather_kernel, nn, ccx),
        in_specs=[vmem, vmem],
        out_specs=vmem,
        out_shape=jax.ShapeDtypeStruct((k, n_t), jnp.float32),
        scratch_shapes=[
            pltpu.VMEM((nn, 1, n_t), jnp.int32),
            pltpu.VMEM((nn, k, n_t), jnp.bfloat16),
            pltpu.VMEM((nn, k, n_t), jnp.bfloat16),
            pltpu.SemaphoreType.DMA((nn,)),
            pltpu.SemaphoreType.DMA((nn,)),
            pltpu.SemaphoreType.DMA((nn,)),
            pltpu.SemaphoreType.DMA((nn,)),
        ],
        compiler_params=pltpu.CompilerParams(collective_id=1, has_side_effects=True),
    )(par, ct)


DIRS = ((1, 0), (-1, 0), (0, 1), (0, -1), (1, 1), (1, -1), (-1, 1), (-1, -1))


def halo_kernel(nw, nn, *refs):
    nd = len(DIRS)
    ins, outs = refs[:2 * nd], refs[2 * nd:4 * nd]
    send, recv = refs[4 * nd], refs[4 * nd + 1]
    me_w = lax.axis_index("wide")
    me_n = lax.axis_index("narrow")
    mesh_id = pl.DeviceIdType.MESH

    def inside(dw, dn, sign):
        w, n = me_w + sign * dw, me_n + sign * dn
        return jnp.logical_and(jnp.logical_and(w >= 0, w < nw), jnp.logical_and(n >= 0, n < nn))

    def clamp(v, n):
        return jnp.clip(v, 0, n - 1)

    barrier = pltpu.get_barrier_semaphore()
    count = 0
    for dw, dn in DIRS:
        ok = inside(dw, dn, 1)

        @pl.when(ok)
        def _():
            pl.semaphore_signal(barrier, inc=1, device_id=(clamp(me_w + dw, nw), clamp(me_n + dn, nn)),
                                device_id_type=mesh_id)
        count = count + ok.astype(jnp.int32)
    pl.semaphore_wait(barrier, count)

    def copy(d, p, sign):
        dw, dn = DIRS[d]
        j = 2 * d + p
        return pltpu.make_async_remote_copy(
            src_ref=ins[j], dst_ref=outs[j], send_sem=send.at[j], recv_sem=recv.at[j],
            device_id=(clamp(me_w + sign * dw, nw), clamp(me_n + sign * dn, nn)), device_id_type=mesh_id)

    for d, (dw, dn) in enumerate(DIRS):
        @pl.when(inside(dw, dn, 1))
        def _():
            for p in range(2):
                copy(d, p, 1).start()

    for d, (dw, dn) in enumerate(DIRS):
        src_ok = inside(dw, dn, -1)

        @pl.when(src_ok)
        def _():
            for p in range(2):
                copy(d, p, -1).wait_recv()

        @pl.when(jnp.logical_not(src_ok))
        def _():
            for p in range(2):
                outs[2 * d + p][...] = jnp.zeros(outs[2 * d + p].shape, outs[2 * d + p].dtype)

    for d, (dw, dn) in enumerate(DIRS):
        @pl.when(inside(dw, dn, 1))
        def _():
            for p in range(2):
                copy(d, p, 1).wait_send()


def exchange_halos(pieces, nw, nn):
    vmem = pl.BlockSpec(memory_space=pltpu.VMEM)
    n = len(pieces)
    return pl.pallas_call(
        functools.partial(halo_kernel, nw, nn),
        in_specs=[vmem] * n,
        out_specs=[vmem] * n,
        out_shape=[jax.ShapeDtypeStruct(p.shape, p.dtype) for p in pieces],
        scratch_shapes=[pltpu.SemaphoreType.DMA((n,)), pltpu.SemaphoreType.DMA((n,))],
        compiler_params=pltpu.CompilerParams(collective_id=2, has_side_effects=True),
    )(*pieces)


def scale_kernel(x_ref, s_ref, o_ref):
    o_ref[...] = x_ref[...] * s_ref[...]


def scale_rows(x, inv):
    cx, cy, k = x.shape
    return pl.pallas_call(
        scale_kernel,
        grid=(cx // SCALE_ROWS,),
        in_specs=[pl.BlockSpec((SCALE_ROWS, cy, k), lambda i: (i, 0, 0)), pl.BlockSpec((1, k), lambda i: (0, 0))],
        out_specs=pl.BlockSpec((SCALE_ROWS, cy, k), lambda i: (i, 0, 0)),
        out_shape=jax.ShapeDtypeStruct(x.shape, x.dtype),
        input_output_aliases={0: 0},
        cost_estimate=pl.CostEstimate(flops=x.size, transcendentals=0, bytes_accessed=x.size * 8),
    )(x, inv)


def local(detail, coarse, diagonal, parents, tile_mask):
    tiles_x, tiles_y = parents.shape
    cells_x, cells_y, columns = detail.shape
    nw, nn = lax.axis_size("wide"), lax.axis_size("narrow")
    total_cells = cells_x * nw * cells_y * nn
    mask_float = tile_mask.astype(jnp.float32)

    tile_values = gather_tiles(parents, coarse, nn).T
    tv = tile_values.reshape(tiles_x, tiles_y, columns)

    m_rows = jnp.repeat(mask_float, TS, axis=1)
    m0 = jnp.broadcast_to(m_rows[:, :, None], (tiles_x, cells_y, columns))
    cm0 = m0 * jnp.repeat(tv, TS, axis=1)

    h = HALO
    c0_top = cm0[0][None] + m0[0][None] * detail[:h].astype(jnp.float32)
    c0_bot = cm0[-1][None] + m0[-1][None] * detail[-h:].astype(jnp.float32)
    cm_rep = jnp.repeat(cm0, TS, axis=0)
    m_rep = jnp.repeat(m0, TS, axis=0)
    c0_left = cm_rep[:, :h] + m_rep[:, :h] * detail[:, :h].astype(jnp.float32)
    c0_right = cm_rep[:, -h:] + m_rep[:, -h:] * detail[:, -h:].astype(jnp.float32)

    cell_mask = jnp.repeat(jnp.repeat(mask_float, TS, axis=0), TS, axis=1)
    g_own = (cell_mask * (4.0 + diagonal) - CENTER) / HALF_WIDTH
    h_own = cell_mask / HALF_WIDTH
    gh = jnp.stack([g_own, h_own])

    def edge(a, dw, dn, rows_axis, cols_axis):
        idx = [slice(None)] * a.ndim
        if dw == 1:
            idx[rows_axis] = slice(a.shape[rows_axis] - h, None)
        elif dw == -1:
            idx[rows_axis] = slice(0, h)
        if dn == 1:
            idx[cols_axis] = slice(a.shape[cols_axis] - h, None)
        elif dn == -1:
            idx[cols_axis] = slice(0, h)
        return a[tuple(idx)]

    c0_pieces = {
        (1, 0): c0_bot, (-1, 0): c0_top,
        (0, 1): c0_right.transpose(1, 0, 2), (0, -1): c0_left.transpose(1, 0, 2),
        (1, 1): c0_bot[:, -h:], (1, -1): c0_bot[:, :h], (-1, 1): c0_top[:, -h:], (-1, -1): c0_top[:, :h],
    }
    pieces = []
    for dw, dn in DIRS:
        pieces.append(c0_pieces[(dw, dn)])
        e = edge(gh, dw, dn, 1, 2)
        pieces.append(e.transpose(0, 2, 1) if dw == 0 else e)
    got = exchange_halos(pieces, nw, nn)
    hc = {dirn: got[2 * k] for k, dirn in enumerate(DIRS)}
    hg = {dirn: got[2 * k + 1] for k, dirn in enumerate(DIRS)}
    for dirn in ((0, 1), (0, -1)):
        hg[dirn] = hg[dirn].transpose(0, 2, 1)
    halos = [hc[(1, 0)], hc[(-1, 0)], hc[(0, 1)], hc[(0, -1)],
             hc[(1, 1)], hc[(1, -1)], hc[(-1, 1)], hc[(-1, -1)]]

    rpad = LPAD - h
    z3 = jnp.zeros((2, h, rpad), jnp.float32)
    zc = jnp.zeros((2, cells_x, rpad), jnp.float32)
    gh_ext = jnp.concatenate(
        [
            jnp.concatenate([z3, hg[(1, 1)], hg[(1, 0)], hg[(1, -1)], z3], axis=2),
            jnp.concatenate([zc, hg[(0, 1)], gh, hg[(0, -1)], zc], axis=2),
            jnp.concatenate([z3, hg[(-1, 1)], hg[(-1, 0)], hg[(-1, -1)], z3], axis=2),
        ],
        axis=1,
    )
    width = cells_y + 2 * LPAD
    g_b = jnp.broadcast_to(gh_ext[0][:, :, None], (cells_x + 2 * h, width, columns))
    h_rows = gh_ext[1][jnp.array([0] + [h + TS * t for t in range(tiles_x)] + [h + cells_x])]
    h_b = jnp.broadcast_to(h_rows[:, :, None], (tiles_x + 2, width, columns))

    cheb_three, ss = run_stencil(detail, cm0, m0, halos, g_b, h_b)
    local_squares = jnp.sum(ss, axis=0, keepdims=True)
    squares = allreduce(local_squares, nw, nn)
    inv = 1.0 / jnp.sqrt(squares / total_cells + EPSILON)
    return scale_rows(cheb_three, inv)


def solution(mesh):
    in_specs = (
        P("wide", "narrow", None),
        P("wide", "narrow", None),
        P("wide", "narrow"),
        P("wide", "narrow"),
        P("wide", "narrow"),
    )
    out_specs = P("wide", "narrow", None)
    return jax.shard_map(local, mesh=mesh, in_specs=in_specs, out_specs=out_specs, check_vma=False)
```

```python
import functools

import jax
import jax.numpy as jnp
from jax import lax
from jax.experimental import pallas as pl
from jax.experimental.pallas import tpu as pltpu
from jax.sharding import PartitionSpec as P

TS = 8
CENTER = 7.5
HALF_WIDTH = 4.5
EPSILON = 1e-06

HALO = 3
LPAD = 8
RING = 16
ROWS = 8
SCALE_ROWS = 32


def shift_pairs(dw, dn, nw, nn):
    pairs = []
    for w in range(nw):
        for n in range(nn):
            tw, tn = w + dw, n + dn
            if 0 <= tw < nw and 0 <= tn < nn:
                pairs.append((w * nn + n, tw * nn + tn))
    return pairs


def exchange(pieces, dw, dn, nw, nn):
    flat = jnp.concatenate([p.reshape(-1) for p in pieces])
    got = lax.ppermute(flat, ("wide", "narrow"), shift_pairs(dw, dn, nw, nn))
    out, at = [], 0
    for p in pieces:
        out.append(got[at : at + p.size].reshape(p.shape))
        at += p.size
    return out


def stencil_kernel(nw, nn, det_ref, cm_ref, m_ref, top_ref, bot_ref, left_ref, right_ref,
                   tl_ref, tr_ref, bl_ref, br_ref, g_ref, h_ref, out_ref, sq_ref, r0, r1, r2, ss_ref,
                   part1, part2, q1, q2, s1, p1, s2, p2):
    i = pl.program_id(0)
    me_w = lax.axis_index("wide")
    me_n = lax.axis_index("narrow")
    mesh_id = pl.DeviceIdType.MESH
    barrier = pltpu.get_barrier_semaphore()
    cx = det_ref.shape[0]
    width = g_ref.shape[1]
    ext_rows = g_ref.shape[0]
    cy = det_ref.shape[1]

    def c0_row(x):
        s = x % RING
        zero = jnp.zeros((width, det_ref.shape[2]), jnp.float32)

        @pl.when(x < HALO)
        def _():
            j = jnp.minimum(x, HALO - 1)
            r0[s] = zero
            r0[s, LPAD - HALO:LPAD] = tl_ref[j]
            r0[s, LPAD:LPAD + cy] = top_ref[j]
            r0[s, LPAD + cy:LPAD + cy + HALO] = tr_ref[j]

        @pl.when(x >= HALO + cx)
        def _():
            j = jnp.clip(x - HALO - cx, 0, HALO - 1)
            r0[s] = zero
            r0[s, LPAD - HALO:LPAD] = bl_ref[j]
            r0[s, LPAD:LPAD + cy] = bot_ref[j]
            r0[s, LPAD + cy:LPAD + cy + HALO] = br_ref[j]

        @pl.when(jnp.logical_and(x >= HALO, x < HALO + cx))
        def _():
            b = jnp.clip(x - HALO, 0, cx - 1)
            t = b // TS
            r0[s, 0:LPAD] = zero[0:LPAD]
            for p in range(HALO):
                r0[s, pl.ds(LPAD - HALO + p, 1)] = left_ref[p, pl.ds(b, 1)]
            r0[s, LPAD:LPAD + cy] = cm_ref[t] + m_ref[t] * det_ref[b].astype(jnp.float32)
            r0[s, LPAD + cy:width] = zero[0:width - LPAD - cy]
            for p in range(HALO):
                r0[s, pl.ds(LPAD + cy + p, 1)] = right_ref[p, pl.ds(b, 1)]

    def apply_b(src, x):
        v = src[x % RING]
        nb = src[(x + 1) % RING] + src[(x + RING - 1) % RING]
        nb = nb + pltpu.roll(v, width - 1, 0) + pltpu.roll(v, 1, 0)
        return g_ref[x] * v - h_ref[(x + TS - HALO) // TS] * nb

    def c1_row(x):
        r1[x % RING] = apply_b(r0, x)

    def c2_row(x):
        r2[x % RING] = 2.0 * apply_b(r1, x) - r0[x % RING]

    def c3_row(x):
        c3 = 2.0 * apply_b(r2, x) - r1[x % RING]
        c3 = c3[LPAD:LPAD + cy]
        out_ref[x - HALO - ROWS * i] = c3
        sq = c3 * c3
        ss_ref[...] += jnp.sum(sq.reshape(cy // 8, 8, sq.shape[-1]), axis=0)

    def rows(fn, lo, n):
        def body(k, carry):
            fn(lo + k)
            return carry
        lax.fori_loop(0, n, body, 0)

    @pl.when(i == 0)
    def _():
        for k in range(1, nn):
            pl.semaphore_signal(barrier, inc=1, device_id=(me_w, (me_n + k) % nn), device_id_type=mesh_id)
        for k in range(1, nw):
            pl.semaphore_signal(barrier, inc=1, device_id=((me_w + k) % nw, me_n), device_id_type=mesh_id)
        ss_ref[...] = jnp.zeros_like(ss_ref)
        rows(c0_row, 0, 2 * HALO)
        rows(c1_row, 1, 2 * HALO - 2)
        rows(c2_row, 2, 2 * HALO - 4)

    base = ROWS * i
    rows(c0_row, base + 2 * HALO, ROWS)
    rows(c1_row, base + 2 * HALO - 1, ROWS)
    rows(c2_row, base + 2 * HALO - 2, ROWS)
    rows(c3_row, base + HALO, ROWS)

    @pl.when(i == pl.num_programs(0) - 1)
    def _():
        pl.semaphore_wait(barrier, nn - 1 + nw - 1)
        part1[...] = jnp.sum(ss_ref[...], axis=0, keepdims=True)
        part2[...] = exchange_sum(part1, q1, s1, p1, me_n, nn, lambda j: (me_w, j))
        sq_ref[...] = exchange_sum(part2, q2, s2, p2, me_w, nw, lambda j: (j, me_n))


def exchange_sum(src, slots, send, recv, me, n, peer_of):
    mesh_id = pl.DeviceIdType.MESH
    copies = []
    for k in range(1, n):
        c = pltpu.make_async_remote_copy(
            src_ref=src, dst_ref=slots.at[me], send_sem=send.at[k], recv_sem=recv.at[me],
            device_id=peer_of((me + k) % n), device_id_type=mesh_id)
        c.start()
        copies.append(c)
    slots[me] = src[...]
    for k in range(1, n):
        other = (me + k) % n
        pltpu.make_async_remote_copy(
            src_ref=src, dst_ref=slots.at[other], send_sem=send.at[k], recv_sem=recv.at[other],
            device_id=peer_of(other), device_id_type=mesh_id).wait_recv()
    for c in copies:
        c.wait_send()
    return jnp.sum(slots[...], axis=0)


def run_stencil(det, cm, m, halos, g, h, nw, nn):
    cx, cy, k = det.shape
    width = g.shape[1]
    steps = cx // ROWS
    vmem = pl.BlockSpec(memory_space=pltpu.VMEM)
    ops = cx * cy * k * 3 * 12
    return pl.pallas_call(
        functools.partial(stencil_kernel, nw, nn),
        grid=(steps,),
        in_specs=[vmem] * 13,
        out_specs=[
            pl.BlockSpec((ROWS, cy, k), lambda i: (i, 0, 0)),
            pl.BlockSpec((1, k), lambda i: (0, 0)),
        ],
        out_shape=[
            jax.ShapeDtypeStruct((cx, cy, k), jnp.float32),
            jax.ShapeDtypeStruct((1, k), jnp.float32),
        ],
        scratch_shapes=[pltpu.VMEM((RING, width, k), jnp.float32) for _ in range(3)] + [
            pltpu.VMEM((8, k), jnp.float32),
            pltpu.VMEM((1, k), jnp.float32),
            pltpu.VMEM((1, k), jnp.float32),
            pltpu.VMEM((nn, 1, k), jnp.float32),
            pltpu.VMEM((nw, 1, k), jnp.float32),
            pltpu.SemaphoreType.DMA((nn,)),
            pltpu.SemaphoreType.DMA((nn,)),
            pltpu.SemaphoreType.DMA((nw,)),
            pltpu.SemaphoreType.DMA((nw,)),
        ],
        compiler_params=pltpu.CompilerParams(
            dimension_semantics=("arbitrary",), vmem_limit_bytes=56 * 1024 * 1024,
            collective_id=0, has_side_effects=True,
        ),
        cost_estimate=pl.CostEstimate(
            flops=ops, transcendentals=0, bytes_accessed=det.size * 2 + cx * cy * k * 4 + g.size * 4
        ),
    )(det, cm, m, *halos, g, h)


def gather_kernel(nn, cols, par_ref, ct_ref, o_ref, pslots, stage, tslots, ps, pq, ts, tq):
    me_w = lax.axis_index("wide")
    me_n = lax.axis_index("narrow")
    mesh_id = pl.DeviceIdType.MESH
    barrier = pltpu.get_barrier_semaphore()
    for k in range(1, nn):
        pl.semaphore_signal(barrier, inc=1, device_id=(me_w, (me_n + k) % nn), device_id_type=mesh_id)
    pl.semaphore_wait(barrier, nn - 1)

    def par_copy(k, other, slot):
        return pltpu.make_async_remote_copy(
            src_ref=par_ref, dst_ref=pslots.at[slot], send_sem=ps.at[k], recv_sem=pq.at[slot],
            device_id=(me_w, other), device_id_type=mesh_id)

    sent = []
    for k in range(1, nn):
        c = par_copy(k, (me_n + k) % nn, me_n)
        c.start()
        sent.append(c)

    local_cells = ct_ref.shape[1]
    ncols = local_cells // cols

    def contribution(par):
        col = par % (ncols * nn)
        idx = (par // (ncols * nn)) * ncols + col % ncols
        idx = jnp.where(col // ncols == me_n, idx, -1)
        rows = lax.broadcasted_iota(jnp.int32, (local_cells, par.shape[-1]), 0)
        onehot = (rows == idx).astype(jnp.bfloat16)
        got = jnp.dot(ct_ref[...], onehot, preferred_element_type=jnp.float32)
        return got.astype(jnp.bfloat16)

    tslots[me_n] = contribution(par_ref[...])
    out_copies = []
    for k in range(1, nn):
        other = (me_n + k) % nn
        par_copy(k, other, other).wait_recv()
        stage[k] = contribution(pslots[other])
        c = pltpu.make_async_remote_copy(
            src_ref=stage.at[k], dst_ref=tslots.at[me_n], send_sem=ts.at[k], recv_sem=tq.at[me_n],
            device_id=(me_w, other), device_id_type=mesh_id)
        c.start()
        out_copies.append(c)
    for k in range(1, nn):
        other = (me_n + k) % nn
        pltpu.make_async_remote_copy(
            src_ref=stage.at[k], dst_ref=tslots.at[other], send_sem=ts.at[k], recv_sem=tq.at[other],
            device_id=(me_w, other), device_id_type=mesh_id).wait_recv()
    for c in sent + out_copies:
        c.wait_send()
    total = tslots[0].astype(jnp.float32)
    for j in range(1, nn):
        total = total + tslots[j].astype(jnp.float32)
    o_ref[...] = total


def gather_tiles(parents, coarse, nn):
    ccx, ccy, k = coarse.shape
    par = parents.reshape(1, -1)
    n_t = par.shape[-1]
    ct = coarse.reshape(ccx * ccy, k).T
    vmem = pl.BlockSpec(memory_space=pltpu.VMEM)
    return pl.pallas_call(
        functools.partial(gather_kernel, nn, ccx),
        in_specs=[vmem, vmem],
        out_specs=vmem,
        out_shape=jax.ShapeDtypeStruct((k, n_t), jnp.float32),
        scratch_shapes=[
            pltpu.VMEM((nn, 1, n_t), jnp.int32),
            pltpu.VMEM((nn, k, n_t), jnp.bfloat16),
            pltpu.VMEM((nn, k, n_t), jnp.bfloat16),
            pltpu.SemaphoreType.DMA((nn,)),
            pltpu.SemaphoreType.DMA((nn,)),
            pltpu.SemaphoreType.DMA((nn,)),
            pltpu.SemaphoreType.DMA((nn,)),
        ],
        compiler_params=pltpu.CompilerParams(collective_id=1, has_side_effects=True),
    )(par, ct)


DIRS = ((1, 0), (-1, 0), (0, 1), (0, -1), (1, 1), (1, -1), (-1, 1), (-1, -1))


def halo_kernel(nw, nn, *refs):
    nd = len(DIRS)
    ins, outs = refs[:2 * nd], refs[2 * nd:4 * nd]
    send, recv = refs[4 * nd], refs[4 * nd + 1]
    me_w = lax.axis_index("wide")
    me_n = lax.axis_index("narrow")
    mesh_id = pl.DeviceIdType.MESH

    def inside(dw, dn, sign):
        w, n = me_w + sign * dw, me_n + sign * dn
        return jnp.logical_and(jnp.logical_and(w >= 0, w < nw), jnp.logical_and(n >= 0, n < nn))

    def clamp(v, n):
        return jnp.clip(v, 0, n - 1)

    barrier = pltpu.get_barrier_semaphore()
    count = 0
    for dw, dn in DIRS:
        ok = inside(dw, dn, 1)

        @pl.when(ok)
        def _():
            pl.semaphore_signal(barrier, inc=1, device_id=(clamp(me_w + dw, nw), clamp(me_n + dn, nn)),
                                device_id_type=mesh_id)
        count = count + ok.astype(jnp.int32)
    pl.semaphore_wait(barrier, count)

    def copy(d, p, sign):
        dw, dn = DIRS[d]
        j = 2 * d + p
        return pltpu.make_async_remote_copy(
            src_ref=ins[j], dst_ref=outs[j], send_sem=send.at[j], recv_sem=recv.at[j],
            device_id=(clamp(me_w + sign * dw, nw), clamp(me_n + sign * dn, nn)), device_id_type=mesh_id)

    for d, (dw, dn) in enumerate(DIRS):
        @pl.when(inside(dw, dn, 1))
        def _():
            for p in range(2):
                copy(d, p, 1).start()

    for d, (dw, dn) in enumerate(DIRS):
        src_ok = inside(dw, dn, -1)

        @pl.when(src_ok)
        def _():
            for p in range(2):
                copy(d, p, -1).wait_recv()

        @pl.when(jnp.logical_not(src_ok))
        def _():
            for p in range(2):
                outs[2 * d + p][...] = jnp.zeros(outs[2 * d + p].shape, outs[2 * d + p].dtype)

    for d, (dw, dn) in enumerate(DIRS):
        @pl.when(inside(dw, dn, 1))
        def _():
            for p in range(2):
                copy(d, p, 1).wait_send()


def exchange_halos(pieces, nw, nn):
    vmem = pl.BlockSpec(memory_space=pltpu.VMEM)
    n = len(pieces)
    return pl.pallas_call(
        functools.partial(halo_kernel, nw, nn),
        in_specs=[vmem] * n,
        out_specs=[vmem] * n,
        out_shape=[jax.ShapeDtypeStruct(p.shape, p.dtype) for p in pieces],
        scratch_shapes=[pltpu.SemaphoreType.DMA((n,)), pltpu.SemaphoreType.DMA((n,))],
        compiler_params=pltpu.CompilerParams(collective_id=2, has_side_effects=True),
    )(*pieces)


def scale_kernel(x_ref, s_ref, o_ref):
    o_ref[...] = x_ref[...] * s_ref[...]


def scale_rows(x, inv):
    cx, cy, k = x.shape
    return pl.pallas_call(
        scale_kernel,
        grid=(cx // SCALE_ROWS,),
        in_specs=[pl.BlockSpec((SCALE_ROWS, cy, k), lambda i: (i, 0, 0)), pl.BlockSpec((1, k), lambda i: (0, 0))],
        out_specs=pl.BlockSpec((SCALE_ROWS, cy, k), lambda i: (i, 0, 0)),
        out_shape=jax.ShapeDtypeStruct(x.shape, x.dtype),
        cost_estimate=pl.CostEstimate(flops=x.size, transcendentals=0, bytes_accessed=x.size * 8),
    )(x, inv)


def local(detail, coarse, diagonal, parents, tile_mask):
    tiles_x, tiles_y = parents.shape
    cells_x, cells_y, columns = detail.shape
    nw, nn = lax.axis_size("wide"), lax.axis_size("narrow")
    total_cells = cells_x * nw * cells_y * nn
    mask_float = tile_mask.astype(jnp.float32)

    tile_values = gather_tiles(parents, coarse, nn).T
    tv = tile_values.reshape(tiles_x, tiles_y, columns)

    m_rows = jnp.repeat(mask_float, TS, axis=1)
    m0 = jnp.broadcast_to(m_rows[:, :, None], (tiles_x, cells_y, columns))
    cm0 = m0 * jnp.repeat(tv, TS, axis=1)

    h = HALO
    c0_top = cm0[0][None] + m0[0][None] * detail[:h].astype(jnp.float32)
    c0_bot = cm0[-1][None] + m0[-1][None] * detail[-h:].astype(jnp.float32)
    cm_rep = jnp.repeat(cm0, TS, axis=0)
    m_rep = jnp.repeat(m0, TS, axis=0)
    c0_left = cm_rep[:, :h] + m_rep[:, :h] * detail[:, :h].astype(jnp.float32)
    c0_right = cm_rep[:, -h:] + m_rep[:, -h:] * detail[:, -h:].astype(jnp.float32)

    cell_mask = jnp.repeat(jnp.repeat(mask_float, TS, axis=0), TS, axis=1)
    g_own = (cell_mask * (4.0 + diagonal) - CENTER) / HALF_WIDTH
    h_own = cell_mask / HALF_WIDTH
    gh = jnp.stack([g_own, h_own])

    def edge(a, dw, dn, rows_axis, cols_axis):
        idx = [slice(None)] * a.ndim
        if dw == 1:
            idx[rows_axis] = slice(a.shape[rows_axis] - h, None)
        elif dw == -1:
            idx[rows_axis] = slice(0, h)
        if dn == 1:
            idx[cols_axis] = slice(a.shape[cols_axis] - h, None)
        elif dn == -1:
            idx[cols_axis] = slice(0, h)
        return a[tuple(idx)]

    c0_pieces = {
        (1, 0): c0_bot, (-1, 0): c0_top,
        (0, 1): c0_right.transpose(1, 0, 2), (0, -1): c0_left.transpose(1, 0, 2),
        (1, 1): c0_bot[:, -h:], (1, -1): c0_bot[:, :h], (-1, 1): c0_top[:, -h:], (-1, -1): c0_top[:, :h],
    }
    pieces = []
    for dw, dn in DIRS:
        pieces.append(c0_pieces[(dw, dn)])
        e = edge(gh, dw, dn, 1, 2)
        pieces.append(e.transpose(0, 2, 1) if dw == 0 else e)
    got = exchange_halos(pieces, nw, nn)
    hc = {dirn: got[2 * k] for k, dirn in enumerate(DIRS)}
    hg = {dirn: got[2 * k + 1] for k, dirn in enumerate(DIRS)}
    for dirn in ((0, 1), (0, -1)):
        hg[dirn] = hg[dirn].transpose(0, 2, 1)
    halos = [hc[(1, 0)], hc[(-1, 0)], hc[(0, 1)], hc[(0, -1)],
             hc[(1, 1)], hc[(1, -1)], hc[(-1, 1)], hc[(-1, -1)]]

    rpad = LPAD - h
    z3 = jnp.zeros((2, h, rpad), jnp.float32)
    zc = jnp.zeros((2, cells_x, rpad), jnp.float32)
    gh_ext = jnp.concatenate(
        [
            jnp.concatenate([z3, hg[(1, 1)], hg[(1, 0)], hg[(1, -1)], z3], axis=2),
            jnp.concatenate([zc, hg[(0, 1)], gh, hg[(0, -1)], zc], axis=2),
            jnp.concatenate([z3, hg[(-1, 1)], hg[(-1, 0)], hg[(-1, -1)], z3], axis=2),
        ],
        axis=1,
    )
    width = cells_y + 2 * LPAD
    g_b = jnp.broadcast_to(gh_ext[0][:, :, None], (cells_x + 2 * h, width, columns))
    h_rows = gh_ext[1][jnp.array([0] + [h + TS * t for t in range(tiles_x)] + [h + cells_x])]
    h_b = jnp.broadcast_to(h_rows[:, :, None], (tiles_x + 2, width, columns))

    cheb_three, squares = run_stencil(detail, cm0, m0, halos, g_b, h_b, nw, nn)
    inv = 1.0 / jnp.sqrt(squares / total_cells + EPSILON)
    return scale_rows(cheb_three, inv)


def solution(mesh):
    in_specs = (
        P("wide", "narrow", None),
        P("wide", "narrow", None),
        P("wide", "narrow"),
        P("wide", "narrow"),
        P("wide", "narrow"),
    )
    out_specs = P("wide", "narrow", None)
    return jax.shard_map(local, mesh=mesh, in_specs=in_specs, out_specs=out_specs, check_vma=False)
```

```python
import functools

import jax
import jax.numpy as jnp
from jax import lax
from jax.experimental import pallas as pl
from jax.experimental.pallas import tpu as pltpu
from jax.sharding import PartitionSpec as P

TS = 8
CENTER = 7.5
HALF_WIDTH = 4.5
EPSILON = 1e-06

HALO = 3
LPAD = 8
RING = 16
ROWS = 8
SCALE_ROWS = 32


def shift_pairs(dw, dn, nw, nn):
    pairs = []
    for w in range(nw):
        for n in range(nn):
            tw, tn = w + dw, n + dn
            if 0 <= tw < nw and 0 <= tn < nn:
                pairs.append((w * nn + n, tw * nn + tn))
    return pairs


def exchange(pieces, dw, dn, nw, nn):
    flat = jnp.concatenate([p.reshape(-1) for p in pieces])
    got = lax.ppermute(flat, ("wide", "narrow"), shift_pairs(dw, dn, nw, nn))
    out, at = [], 0
    for p in pieces:
        out.append(got[at : at + p.size].reshape(p.shape))
        at += p.size
    return out


def stencil_kernel(nw, nn, det_ref, cm_ref, m_ref, top_ref, bot_ref, left_ref, right_ref,
                   tl_ref, tr_ref, bl_ref, br_ref, g_ref, h_ref, out_ref, sq_ref, r0, r1, r2, ss_ref,
                   part1, part2, q1, q2, s1, p1, s2, p2):
    i = pl.program_id(0)
    me_w = lax.axis_index("wide")
    me_n = lax.axis_index("narrow")
    mesh_id = pl.DeviceIdType.MESH
    barrier = pltpu.get_barrier_semaphore()
    cx = det_ref.shape[0]
    width = g_ref.shape[1]
    ext_rows = g_ref.shape[0]
    cy = det_ref.shape[1]

    def c0_row(x):
        s = x % RING
        zero = jnp.zeros((width, det_ref.shape[2]), jnp.float32)

        @pl.when(x < HALO)
        def _():
            j = jnp.minimum(x, HALO - 1)
            r0[s] = zero
            r0[s, LPAD - HALO:LPAD] = tl_ref[j]
            r0[s, LPAD:LPAD + cy] = top_ref[j]
            r0[s, LPAD + cy:LPAD + cy + HALO] = tr_ref[j]

        @pl.when(x >= HALO + cx)
        def _():
            j = jnp.clip(x - HALO - cx, 0, HALO - 1)
            r0[s] = zero
            r0[s, LPAD - HALO:LPAD] = bl_ref[j]
            r0[s, LPAD:LPAD + cy] = bot_ref[j]
            r0[s, LPAD + cy:LPAD + cy + HALO] = br_ref[j]

        @pl.when(jnp.logical_and(x >= HALO, x < HALO + cx))
        def _():
            b = jnp.clip(x - HALO, 0, cx - 1)
            t = b // TS
            r0[s, 0:LPAD] = zero[0:LPAD]
            for p in range(HALO):
                r0[s, pl.ds(LPAD - HALO + p, 1)] = left_ref[p, pl.ds(b, 1)]
            r0[s, LPAD:LPAD + cy] = cm_ref[t] + m_ref[t] * det_ref[b].astype(jnp.float32)
            r0[s, LPAD + cy:width] = zero[0:width - LPAD - cy]
            for p in range(HALO):
                r0[s, pl.ds(LPAD + cy + p, 1)] = right_ref[p, pl.ds(b, 1)]

    def apply_b(src, x):
        v = src[x % RING]
        nb = src[(x + 1) % RING] + src[(x + RING - 1) % RING]
        nb = nb + pltpu.roll(v, width - 1, 0) + pltpu.roll(v, 1, 0)
        return g_ref[x] * v - h_ref[(x + TS - HALO) // TS] * nb

    def c1_row(x):
        r1[x % RING] = apply_b(r0, x)

    def c2_row(x):
        r2[x % RING] = 2.0 * apply_b(r1, x) - r0[x % RING]

    def c3_row(x):
        c3 = 2.0 * apply_b(r2, x) - r1[x % RING]
        c3 = c3[LPAD:LPAD + cy]
        out_ref[x - HALO - ROWS * i] = c3
        sq = c3 * c3
        ss_ref[...] += jnp.sum(sq.reshape(cy // 8, 8, sq.shape[-1]), axis=0)

    def rows(fn, lo, n):
        def body(k, carry):
            fn(lo + k)
            return carry
        lax.fori_loop(0, n, body, 0)

    @pl.when(i == 0)
    def _():
        for k in range(1, nn):
            pl.semaphore_signal(barrier, inc=1, device_id=(me_w, (me_n + k) % nn), device_id_type=mesh_id)
        for k in range(1, nw):
            pl.semaphore_signal(barrier, inc=1, device_id=((me_w + k) % nw, me_n), device_id_type=mesh_id)
        ss_ref[...] = jnp.zeros_like(ss_ref)
        rows(c0_row, 0, 2 * HALO)
        rows(c1_row, 1, 2 * HALO - 2)
        rows(c2_row, 2, 2 * HALO - 4)

    base = ROWS * i
    rows(c0_row, base + 2 * HALO, ROWS)
    rows(c1_row, base + 2 * HALO - 1, ROWS)
    rows(c2_row, base + 2 * HALO - 2, ROWS)
    rows(c3_row, base + HALO, ROWS)

    @pl.when(i == pl.num_programs(0) - 1)
    def _():
        pl.semaphore_wait(barrier, nn - 1 + nw - 1)
        part1[...] = jnp.sum(ss_ref[...], axis=0, keepdims=True)
        part2[...] = exchange_sum(part1, q1, s1, p1, me_n, nn, lambda j: (me_w, j))
        sq_ref[...] = exchange_sum(part2, q2, s2, p2, me_w, nw, lambda j: (j, me_n))


def exchange_sum(src, slots, send, recv, me, n, peer_of):
    mesh_id = pl.DeviceIdType.MESH
    copies = []
    for k in range(1, n):
        c = pltpu.make_async_remote_copy(
            src_ref=src, dst_ref=slots.at[me], send_sem=send.at[k], recv_sem=recv.at[me],
            device_id=peer_of((me + k) % n), device_id_type=mesh_id)
        c.start()
        copies.append(c)
    slots[me] = src[...]
    for k in range(1, n):
        other = (me + k) % n
        pltpu.make_async_remote_copy(
            src_ref=src, dst_ref=slots.at[other], send_sem=send.at[k], recv_sem=recv.at[other],
            device_id=peer_of(other), device_id_type=mesh_id).wait_recv()
    for c in copies:
        c.wait_send()
    return jnp.sum(slots[...], axis=0)


def run_stencil(det, cm, m, halos, g, h, nw, nn):
    cx, cy, k = det.shape
    width = g.shape[1]
    steps = cx // ROWS
    vmem = pl.BlockSpec(memory_space=pltpu.VMEM)
    ops = cx * cy * k * 3 * 12
    return pl.pallas_call(
        functools.partial(stencil_kernel, nw, nn),
        grid=(steps,),
        in_specs=[vmem] * 13,
        out_specs=[
            pl.BlockSpec((ROWS, cy, k), lambda i: (i, 0, 0)),
            pl.BlockSpec((1, k), lambda i: (0, 0)),
        ],
        out_shape=[
            jax.ShapeDtypeStruct((cx, cy, k), jnp.float32),
            jax.ShapeDtypeStruct((1, k), jnp.float32),
        ],
        scratch_shapes=[pltpu.VMEM((RING, width, k), jnp.float32) for _ in range(3)] + [
            pltpu.VMEM((8, k), jnp.float32),
            pltpu.VMEM((1, k), jnp.float32),
            pltpu.VMEM((1, k), jnp.float32),
            pltpu.VMEM((nn, 1, k), jnp.float32),
            pltpu.VMEM((nw, 1, k), jnp.float32),
            pltpu.SemaphoreType.DMA((nn,)),
            pltpu.SemaphoreType.DMA((nn,)),
            pltpu.SemaphoreType.DMA((nw,)),
            pltpu.SemaphoreType.DMA((nw,)),
        ],
        compiler_params=pltpu.CompilerParams(
            dimension_semantics=("arbitrary",), vmem_limit_bytes=56 * 1024 * 1024,
            collective_id=0, has_side_effects=True,
        ),
        cost_estimate=pl.CostEstimate(
            flops=ops, transcendentals=0, bytes_accessed=det.size * 2 + cx * cy * k * 4 + g.size * 4
        ),
    )(det, cm, m, *halos, g, h)


def gather_kernel(nn, cols, par_ref, ct_ref, o_ref, pslots, stage, tslots, ps, pq, ts, tq):
    me_w = lax.axis_index("wide")
    me_n = lax.axis_index("narrow")
    mesh_id = pl.DeviceIdType.MESH
    barrier = pltpu.get_barrier_semaphore()
    for k in range(1, nn):
        pl.semaphore_signal(barrier, inc=1, device_id=(me_w, (me_n + k) % nn), device_id_type=mesh_id)
    pl.semaphore_wait(barrier, nn - 1)

    def par_copy(k, other, slot):
        return pltpu.make_async_remote_copy(
            src_ref=par_ref, dst_ref=pslots.at[slot], send_sem=ps.at[k], recv_sem=pq.at[slot],
            device_id=(me_w, other), device_id_type=mesh_id)

    sent = []
    for k in range(1, nn):
        c = par_copy(k, (me_n + k) % nn, me_n)
        c.start()
        sent.append(c)

    local_cells = ct_ref.shape[0]
    ncols = local_cells // cols

    def contribution(par):
        col = par % (ncols * nn)
        idx = (par // (ncols * nn)) * ncols + col % ncols
        idx = jnp.where(col // ncols == me_n, idx, -1)
        rows = lax.broadcasted_iota(jnp.int32, (local_cells, par.shape[-1]), 0)
        onehot = (rows == idx).astype(jnp.bfloat16)
        got = lax.dot_general(ct_ref[...], onehot, (((0,), (0,)), ((), ())),
                              preferred_element_type=jnp.float32)
        return got.astype(jnp.bfloat16)

    tslots[me_n] = contribution(par_ref[...])
    out_copies = []
    for k in range(1, nn):
        other = (me_n + k) % nn
        par_copy(k, other, other).wait_recv()
        stage[k] = contribution(pslots[other])
        c = pltpu.make_async_remote_copy(
            src_ref=stage.at[k], dst_ref=tslots.at[me_n], send_sem=ts.at[k], recv_sem=tq.at[me_n],
            device_id=(me_w, other), device_id_type=mesh_id)
        c.start()
        out_copies.append(c)
    for k in range(1, nn):
        other = (me_n + k) % nn
        pltpu.make_async_remote_copy(
            src_ref=stage.at[k], dst_ref=tslots.at[other], send_sem=ts.at[k], recv_sem=tq.at[other],
            device_id=(me_w, other), device_id_type=mesh_id).wait_recv()
    for c in sent + out_copies:
        c.wait_send()
    total = tslots[0].astype(jnp.float32)
    for j in range(1, nn):
        total = total + tslots[j].astype(jnp.float32)
    o_ref[...] = total


def gather_tiles(parents, coarse, nn):
    ccx, ccy, k = coarse.shape
    par = parents.reshape(1, -1)
    n_t = par.shape[-1]
    ct = coarse.reshape(ccx * ccy, k)
    vmem = pl.BlockSpec(memory_space=pltpu.VMEM)
    return pl.pallas_call(
        functools.partial(gather_kernel, nn, ccx),
        in_specs=[vmem, vmem],
        out_specs=vmem,
        out_shape=jax.ShapeDtypeStruct((k, n_t), jnp.float32),
        scratch_shapes=[
            pltpu.VMEM((nn, 1, n_t), jnp.int32),
            pltpu.VMEM((nn, k, n_t), jnp.bfloat16),
            pltpu.VMEM((nn, k, n_t), jnp.bfloat16),
            pltpu.SemaphoreType.DMA((nn,)),
            pltpu.SemaphoreType.DMA((nn,)),
            pltpu.SemaphoreType.DMA((nn,)),
            pltpu.SemaphoreType.DMA((nn,)),
        ],
        compiler_params=pltpu.CompilerParams(collective_id=1, has_side_effects=True),
    )(par, ct)


DIRS = ((1, 0), (-1, 0), (0, 1), (0, -1), (1, 1), (1, -1), (-1, 1), (-1, -1))


def halo_kernel(nw, nn, *refs):
    nd = len(DIRS)
    ins, outs = refs[:2 * nd], refs[2 * nd:4 * nd]
    send, recv = refs[4 * nd], refs[4 * nd + 1]
    me_w = lax.axis_index("wide")
    me_n = lax.axis_index("narrow")
    mesh_id = pl.DeviceIdType.MESH

    def inside(dw, dn, sign):
        w, n = me_w + sign * dw, me_n + sign * dn
        return jnp.logical_and(jnp.logical_and(w >= 0, w < nw), jnp.logical_and(n >= 0, n < nn))

    def clamp(v, n):
        return jnp.clip(v, 0, n - 1)

    barrier = pltpu.get_barrier_semaphore()
    count = 0
    for dw, dn in DIRS:
        ok = inside(dw, dn, 1)

        @pl.when(ok)
        def _():
            pl.semaphore_signal(barrier, inc=1, device_id=(clamp(me_w + dw, nw), clamp(me_n + dn, nn)),
                                device_id_type=mesh_id)
        count = count + ok.astype(jnp.int32)
    pl.semaphore_wait(barrier, count)

    def copy(d, p, sign):
        dw, dn = DIRS[d]
        j = 2 * d + p
        return pltpu.make_async_remote_copy(
            src_ref=ins[j], dst_ref=outs[j], send_sem=send.at[j], recv_sem=recv.at[j],
            device_id=(clamp(me_w + sign * dw, nw), clamp(me_n + sign * dn, nn)), device_id_type=mesh_id)

    for d, (dw, dn) in enumerate(DIRS):
        @pl.when(inside(dw, dn, 1))
        def _():
            for p in range(2):
                copy(d, p, 1).start()

    for d, (dw, dn) in enumerate(DIRS):
        src_ok = inside(dw, dn, -1)

        @pl.when(src_ok)
        def _():
            for p in range(2):
                copy(d, p, -1).wait_recv()

        @pl.when(jnp.logical_not(src_ok))
        def _():
            for p in range(2):
                outs[2 * d + p][...] = jnp.zeros(outs[2 * d + p].shape, outs[2 * d + p].dtype)

    for d, (dw, dn) in enumerate(DIRS):
        @pl.when(inside(dw, dn, 1))
        def _():
            for p in range(2):
                copy(d, p, 1).wait_send()


def exchange_halos(pieces, nw, nn):
    vmem = pl.BlockSpec(memory_space=pltpu.VMEM)
    n = len(pieces)
    return pl.pallas_call(
        functools.partial(halo_kernel, nw, nn),
        in_specs=[vmem] * n,
        out_specs=[vmem] * n,
        out_shape=[jax.ShapeDtypeStruct(p.shape, p.dtype) for p in pieces],
        scratch_shapes=[pltpu.SemaphoreType.DMA((n,)), pltpu.SemaphoreType.DMA((n,))],
        compiler_params=pltpu.CompilerParams(collective_id=2, has_side_effects=True),
    )(*pieces)


def scale_kernel(x_ref, s_ref, o_ref):
    o_ref[...] = x_ref[...] * s_ref[...]


def scale_rows(x, inv):
    cx, cy, k = x.shape
    return pl.pallas_call(
        scale_kernel,
        grid=(cx // SCALE_ROWS,),
        in_specs=[pl.BlockSpec((SCALE_ROWS, cy, k), lambda i: (i, 0, 0)), pl.BlockSpec((1, k), lambda i: (0, 0))],
        out_specs=pl.BlockSpec((SCALE_ROWS, cy, k), lambda i: (i, 0, 0)),
        out_shape=jax.ShapeDtypeStruct(x.shape, x.dtype),
        cost_estimate=pl.CostEstimate(flops=x.size, transcendentals=0, bytes_accessed=x.size * 8),
    )(x, inv)


def local(detail, coarse, diagonal, parents, tile_mask):
    tiles_x, tiles_y = parents.shape
    cells_x, cells_y, columns = detail.shape
    nw, nn = lax.axis_size("wide"), lax.axis_size("narrow")
    total_cells = cells_x * nw * cells_y * nn
    mask_float = tile_mask.astype(jnp.float32)

    tile_values = gather_tiles(parents, coarse, nn).T
    tv = tile_values.reshape(tiles_x, tiles_y, columns)

    m_rows = jnp.repeat(mask_float, TS, axis=1)
    m0 = jnp.broadcast_to(m_rows[:, :, None], (tiles_x, cells_y, columns))
    cm0 = m0 * jnp.repeat(tv, TS, axis=1)

    h = HALO
    c0_top = cm0[0][None] + m0[0][None] * detail[:h].astype(jnp.float32)
    c0_bot = cm0[-1][None] + m0[-1][None] * detail[-h:].astype(jnp.float32)
    cm_rep = jnp.repeat(cm0, TS, axis=0)
    m_rep = jnp.repeat(m0, TS, axis=0)
    c0_left = cm_rep[:, :h] + m_rep[:, :h] * detail[:, :h].astype(jnp.float32)
    c0_right = cm_rep[:, -h:] + m_rep[:, -h:] * detail[:, -h:].astype(jnp.float32)

    cell_mask = jnp.repeat(jnp.repeat(mask_float, TS, axis=0), TS, axis=1)
    g_own = (cell_mask * (4.0 + diagonal) - CENTER) / HALF_WIDTH
    h_own = cell_mask / HALF_WIDTH
    gh = jnp.stack([g_own, h_own])

    def edge(a, dw, dn, rows_axis, cols_axis):
        idx = [slice(None)] * a.ndim
        if dw == 1:
            idx[rows_axis] = slice(a.shape[rows_axis] - h, None)
        elif dw == -1:
            idx[rows_axis] = slice(0, h)
        if dn == 1:
            idx[cols_axis] = slice(a.shape[cols_axis] - h, None)
        elif dn == -1:
            idx[cols_axis] = slice(0, h)
        return a[tuple(idx)]

    c0_pieces = {
        (1, 0): c0_bot, (-1, 0): c0_top,
        (0, 1): c0_right.transpose(1, 0, 2), (0, -1): c0_left.transpose(1, 0, 2),
        (1, 1): c0_bot[:, -h:], (1, -1): c0_bot[:, :h], (-1, 1): c0_top[:, -h:], (-1, -1): c0_top[:, :h],
    }
    pieces = []
    for dw, dn in DIRS:
        pieces.append(c0_pieces[(dw, dn)])
        pieces.append(edge(gh, dw, dn, 1, 2))
    got = exchange_halos(pieces, nw, nn)
    hc = {dirn: got[2 * k] for k, dirn in enumerate(DIRS)}
    hg = {dirn: got[2 * k + 1] for k, dirn in enumerate(DIRS)}
    halos = [hc[(1, 0)], hc[(-1, 0)], hc[(0, 1)], hc[(0, -1)],
             hc[(1, 1)], hc[(1, -1)], hc[(-1, 1)], hc[(-1, -1)]]

    rpad = LPAD - h
    z3 = jnp.zeros((2, h, rpad), jnp.float32)
    zc = jnp.zeros((2, cells_x, rpad), jnp.float32)
    gh_ext = jnp.concatenate(
        [
            jnp.concatenate([z3, hg[(1, 1)], hg[(1, 0)], hg[(1, -1)], z3], axis=2),
            jnp.concatenate([zc, hg[(0, 1)], gh, hg[(0, -1)], zc], axis=2),
            jnp.concatenate([z3, hg[(-1, 1)], hg[(-1, 0)], hg[(-1, -1)], z3], axis=2),
        ],
        axis=1,
    )
    width = cells_y + 2 * LPAD
    g_b = jnp.broadcast_to(gh_ext[0][:, :, None], (cells_x + 2 * h, width, columns))
    h_rows = gh_ext[1][jnp.array([0] + [h + TS * t for t in range(tiles_x)] + [h + cells_x])]
    h_b = jnp.broadcast_to(h_rows[:, :, None], (tiles_x + 2, width, columns))

    cheb_three, squares = run_stencil(detail, cm0, m0, halos, g_b, h_b, nw, nn)
    inv = 1.0 / jnp.sqrt(squares / total_cells + EPSILON)
    return scale_rows(cheb_three, inv)


def solution(mesh):
    in_specs = (
        P("wide", "narrow", None),
        P("wide", "narrow", None),
        P("wide", "narrow"),
        P("wide", "narrow"),
        P("wide", "narrow"),
    )
    out_specs = P("wide", "narrow", None)
    return jax.shard_map(local, mesh=mesh, in_specs=in_specs, out_specs=out_specs, check_vma=False)
```

```python
import functools

import jax
import jax.numpy as jnp
from jax import lax
from jax.experimental import pallas as pl
from jax.experimental.pallas import tpu as pltpu
from jax.sharding import PartitionSpec as P

TS = 8
CENTER = 7.5
HALF_WIDTH = 4.5
EPSILON = 1e-06

HALO = 3
LPAD = 8
RING = 16
ROWS = 8
SCALE_ROWS = 32


def shift_pairs(dw, dn, nw, nn):
    pairs = []
    for w in range(nw):
        for n in range(nn):
            tw, tn = w + dw, n + dn
            if 0 <= tw < nw and 0 <= tn < nn:
                pairs.append((w * nn + n, tw * nn + tn))
    return pairs


def exchange(pieces, dw, dn, nw, nn):
    flat = jnp.concatenate([p.reshape(-1) for p in pieces])
    got = lax.ppermute(flat, ("wide", "narrow"), shift_pairs(dw, dn, nw, nn))
    out, at = [], 0
    for p in pieces:
        out.append(got[at : at + p.size].reshape(p.shape))
        at += p.size
    return out


def stencil_kernel(nw, nn, det_ref, cm_ref, m_ref, top_ref, bot_ref, left_ref, right_ref,
                   tl_ref, tr_ref, bl_ref, br_ref, g_ref, h_ref, out_ref, sq_ref, r0, r1, r2, ss_ref,
                   part1, part2, q1, q2, s1, p1, s2, p2):
    i = pl.program_id(0)
    me_w = lax.axis_index("wide")
    me_n = lax.axis_index("narrow")
    mesh_id = pl.DeviceIdType.MESH
    barrier = pltpu.get_barrier_semaphore()
    cx = det_ref.shape[0]
    width = g_ref.shape[1]
    ext_rows = g_ref.shape[0]
    cy = det_ref.shape[1]

    def c0_row(x):
        s = x % RING
        zero = jnp.zeros((width, det_ref.shape[2]), jnp.float32)

        @pl.when(x < HALO)
        def _():
            j = jnp.minimum(x, HALO - 1)
            r0[s] = zero
            r0[s, LPAD - HALO:LPAD] = tl_ref[j]
            r0[s, LPAD:LPAD + cy] = top_ref[j]
            r0[s, LPAD + cy:LPAD + cy + HALO] = tr_ref[j]

        @pl.when(x >= HALO + cx)
        def _():
            j = jnp.clip(x - HALO - cx, 0, HALO - 1)
            r0[s] = zero
            r0[s, LPAD - HALO:LPAD] = bl_ref[j]
            r0[s, LPAD:LPAD + cy] = bot_ref[j]
            r0[s, LPAD + cy:LPAD + cy + HALO] = br_ref[j]

        @pl.when(jnp.logical_and(x >= HALO, x < HALO + cx))
        def _():
            b = jnp.clip(x - HALO, 0, cx - 1)
            t = b // TS
            r0[s, 0:LPAD] = zero[0:LPAD]
            for p in range(HALO):
                r0[s, pl.ds(LPAD - HALO + p, 1)] = left_ref[p, pl.ds(b, 1)]
            r0[s, LPAD:LPAD + cy] = cm_ref[t] + m_ref[t] * det_ref[b].astype(jnp.float32)
            r0[s, LPAD + cy:width] = zero[0:width - LPAD - cy]
            for p in range(HALO):
                r0[s, pl.ds(LPAD + cy + p, 1)] = right_ref[p, pl.ds(b, 1)]

    def apply_b(src, x):
        v = src[x % RING]
        nb = src[(x + 1) % RING] + src[(x + RING - 1) % RING]
        nb = nb + pltpu.roll(v, width - 1, 0) + pltpu.roll(v, 1, 0)
        return g_ref[x] * v - h_ref[(x + TS - HALO) // TS] * nb

    def c1_row(x):
        r1[x % RING] = apply_b(r0, x)

    def c2_row(x):
        r2[x % RING] = 2.0 * apply_b(r1, x) - r0[x % RING]

    def c3_row(x):
        c3 = 2.0 * apply_b(r2, x) - r1[x % RING]
        c3 = c3[LPAD:LPAD + cy]
        out_ref[x - HALO - ROWS * i] = c3
        sq = c3 * c3
        ss_ref[...] += jnp.sum(sq.reshape(cy // 8, 8, sq.shape[-1]), axis=0)

    def rows(fn, lo, n):
        def body(k, carry):
            fn(lo + k)
            return carry
        lax.fori_loop(0, n, body, 0)

    @pl.when(i == 0)
    def _():
        for k in range(1, nn):
            pl.semaphore_signal(barrier, inc=1, device_id=(me_w, (me_n + k) % nn), device_id_type=mesh_id)
        for k in range(1, nw):
            pl.semaphore_signal(barrier, inc=1, device_id=((me_w + k) % nw, me_n), device_id_type=mesh_id)
        ss_ref[...] = jnp.zeros_like(ss_ref)
        rows(c0_row, 0, 2 * HALO)
        rows(c1_row, 1, 2 * HALO - 2)
        rows(c2_row, 2, 2 * HALO - 4)

    base = ROWS * i
    rows(c0_row, base + 2 * HALO, ROWS)
    rows(c1_row, base + 2 * HALO - 1, ROWS)
    rows(c2_row, base + 2 * HALO - 2, ROWS)
    rows(c3_row, base + HALO, ROWS)

    @pl.when(i == pl.num_programs(0) - 1)
    def _():
        pl.semaphore_wait(barrier, nn - 1 + nw - 1)
        part1[...] = jnp.sum(ss_ref[...], axis=0, keepdims=True)
        part2[...] = exchange_sum(part1, q1, s1, p1, me_n, nn, lambda j: (me_w, j))
        sq_ref[...] = exchange_sum(part2, q2, s2, p2, me_w, nw, lambda j: (j, me_n))


def exchange_sum(src, slots, send, recv, me, n, peer_of):
    mesh_id = pl.DeviceIdType.MESH
    copies = []
    for k in range(1, n):
        c = pltpu.make_async_remote_copy(
            src_ref=src, dst_ref=slots.at[me], send_sem=send.at[k], recv_sem=recv.at[me],
            device_id=peer_of((me + k) % n), device_id_type=mesh_id)
        c.start()
        copies.append(c)
    slots[me] = src[...]
    for k in range(1, n):
        other = (me + k) % n
        pltpu.make_async_remote_copy(
            src_ref=src, dst_ref=slots.at[other], send_sem=send.at[k], recv_sem=recv.at[other],
            device_id=peer_of(other), device_id_type=mesh_id).wait_recv()
    for c in copies:
        c.wait_send()
    return jnp.sum(slots[...], axis=0)


def run_stencil(det, cm, m, halos, g, h, nw, nn):
    cx, cy, k = det.shape
    width = g.shape[1]
    steps = cx // ROWS
    vmem = pl.BlockSpec(memory_space=pltpu.VMEM)
    ops = cx * cy * k * 3 * 12
    return pl.pallas_call(
        functools.partial(stencil_kernel, nw, nn),
        grid=(steps,),
        in_specs=[vmem] * 13,
        out_specs=[
            pl.BlockSpec((ROWS, cy, k), lambda i: (i, 0, 0)),
            pl.BlockSpec((1, k), lambda i: (0, 0)),
        ],
        out_shape=[
            jax.ShapeDtypeStruct((cx, cy, k), jnp.float32),
            jax.ShapeDtypeStruct((1, k), jnp.float32),
        ],
        scratch_shapes=[pltpu.VMEM((RING, width, k), jnp.float32) for _ in range(3)] + [
            pltpu.VMEM((8, k), jnp.float32),
            pltpu.VMEM((1, k), jnp.float32),
            pltpu.VMEM((1, k), jnp.float32),
            pltpu.VMEM((nn, 1, k), jnp.float32),
            pltpu.VMEM((nw, 1, k), jnp.float32),
            pltpu.SemaphoreType.DMA((nn,)),
            pltpu.SemaphoreType.DMA((nn,)),
            pltpu.SemaphoreType.DMA((nw,)),
            pltpu.SemaphoreType.DMA((nw,)),
        ],
        compiler_params=pltpu.CompilerParams(
            dimension_semantics=("arbitrary",), vmem_limit_bytes=56 * 1024 * 1024,
            collective_id=0, has_side_effects=True,
        ),
        cost_estimate=pl.CostEstimate(
            flops=ops, transcendentals=0, bytes_accessed=det.size * 2 + cx * cy * k * 4 + g.size * 4
        ),
    )(det, cm, m, *halos, g, h)


def gather_kernel(nn, cols, par_ref, ct_ref, o_ref, pslots, stage, tslots, ps, pq, ts, tq):
    me_w = lax.axis_index("wide")
    me_n = lax.axis_index("narrow")
    mesh_id = pl.DeviceIdType.MESH
    barrier = pltpu.get_barrier_semaphore()
    for k in range(1, nn):
        pl.semaphore_signal(barrier, inc=1, device_id=(me_w, (me_n + k) % nn), device_id_type=mesh_id)
    pl.semaphore_wait(barrier, nn - 1)

    def par_copy(k, other, slot):
        return pltpu.make_async_remote_copy(
            src_ref=par_ref, dst_ref=pslots.at[slot], send_sem=ps.at[k], recv_sem=pq.at[slot],
            device_id=(me_w, other), device_id_type=mesh_id)

    sent = []
    for k in range(1, nn):
        c = par_copy(k, (me_n + k) % nn, me_n)
        c.start()
        sent.append(c)

    local_cells = ct_ref.shape[0]
    ncols = local_cells // cols

    def contribution(par):
        col = par % (ncols * nn)
        idx = (par // (ncols * nn)) * ncols + col % ncols
        idx = jnp.where(col // ncols == me_n, idx, -1)
        rows = lax.broadcasted_iota(jnp.int32, (local_cells, par.shape[-1]), 0)
        onehot = (rows == idx).astype(jnp.bfloat16)
        got = lax.dot_general(ct_ref[...], onehot, (((0,), (0,)), ((), ())),
                              preferred_element_type=jnp.float32)
        return got.astype(jnp.bfloat16)

    tslots[me_n] = contribution(par_ref[...])
    out_copies = []
    for k in range(1, nn):
        other = (me_n + k) % nn
        par_copy(k, other, other).wait_recv()
        stage[k] = contribution(pslots[other])
        c = pltpu.make_async_remote_copy(
            src_ref=stage.at[k], dst_ref=tslots.at[me_n], send_sem=ts.at[k], recv_sem=tq.at[me_n],
            device_id=(me_w, other), device_id_type=mesh_id)
        c.start()
        out_copies.append(c)
    for k in range(1, nn):
        other = (me_n + k) % nn
        pltpu.make_async_remote_copy(
            src_ref=stage.at[k], dst_ref=tslots.at[other], send_sem=ts.at[k], recv_sem=tq.at[other],
            device_id=(me_w, other), device_id_type=mesh_id).wait_recv()
    for c in sent + out_copies:
        c.wait_send()
    total = tslots[0].astype(jnp.float32)
    for j in range(1, nn):
        total = total + tslots[j].astype(jnp.float32)
    o_ref[...] = total


def gather_tiles(parents, coarse, nn):
    ccx, ccy, k = coarse.shape
    par = parents.reshape(1, -1)
    n_t = par.shape[-1]
    ct = coarse.reshape(ccx * ccy, k)
    vmem = pl.BlockSpec(memory_space=pltpu.VMEM)
    return pl.pallas_call(
        functools.partial(gather_kernel, nn, ccx),
        in_specs=[vmem, vmem],
        out_specs=vmem,
        out_shape=jax.ShapeDtypeStruct((k, n_t), jnp.float32),
        scratch_shapes=[
            pltpu.VMEM((nn, 1, n_t), jnp.int32),
            pltpu.VMEM((nn, k, n_t), jnp.bfloat16),
            pltpu.VMEM((nn, k, n_t), jnp.bfloat16),
            pltpu.SemaphoreType.DMA((nn,)),
            pltpu.SemaphoreType.DMA((nn,)),
            pltpu.SemaphoreType.DMA((nn,)),
            pltpu.SemaphoreType.DMA((nn,)),
        ],
        compiler_params=pltpu.CompilerParams(collective_id=1, has_side_effects=True),
    )(par, ct)


DIRS = ((1, 0), (-1, 0), (0, 1), (0, -1), (1, 1), (1, -1), (-1, 1), (-1, -1))


def halo_kernel(nw, nn, *refs):
    nd = len(DIRS)
    ins, outs = refs[:2 * nd], refs[2 * nd:4 * nd]
    send, recv = refs[4 * nd], refs[4 * nd + 1]
    me_w = lax.axis_index("wide")
    me_n = lax.axis_index("narrow")
    mesh_id = pl.DeviceIdType.MESH

    def inside(dw, dn, sign):
        w, n = me_w + sign * dw, me_n + sign * dn
        return jnp.logical_and(jnp.logical_and(w >= 0, w < nw), jnp.logical_and(n >= 0, n < nn))

    def clamp(v, n):
        return jnp.clip(v, 0, n - 1)

    barrier = pltpu.get_barrier_semaphore()
    count = 0
    for dw, dn in DIRS:
        ok = inside(dw, dn, 1)

        @pl.when(ok)
        def _():
            pl.semaphore_signal(barrier, inc=1, device_id=(clamp(me_w + dw, nw), clamp(me_n + dn, nn)),
                                device_id_type=mesh_id)
        count = count + ok.astype(jnp.int32)
    pl.semaphore_wait(barrier, count)

    def copy(d, p, sign):
        dw, dn = DIRS[d]
        j = 2 * d + p
        return pltpu.make_async_remote_copy(
            src_ref=ins[j], dst_ref=outs[j], send_sem=send.at[j], recv_sem=recv.at[j],
            device_id=(clamp(me_w + sign * dw, nw), clamp(me_n + sign * dn, nn)), device_id_type=mesh_id)

    for d, (dw, dn) in enumerate(DIRS):
        @pl.when(inside(dw, dn, 1))
        def _():
            for p in range(2):
                copy(d, p, 1).start()

    for d, (dw, dn) in enumerate(DIRS):
        src_ok = inside(dw, dn, -1)

        @pl.when(src_ok)
        def _():
            for p in range(2):
                copy(d, p, -1).wait_recv()

        @pl.when(jnp.logical_not(src_ok))
        def _():
            for p in range(2):
                outs[2 * d + p][...] = jnp.zeros(outs[2 * d + p].shape, outs[2 * d + p].dtype)

    for d, (dw, dn) in enumerate(DIRS):
        @pl.when(inside(dw, dn, 1))
        def _():
            for p in range(2):
                copy(d, p, 1).wait_send()


def exchange_halos(pieces, nw, nn):
    vmem = pl.BlockSpec(memory_space=pltpu.VMEM)
    n = len(pieces)
    return pl.pallas_call(
        functools.partial(halo_kernel, nw, nn),
        in_specs=[vmem] * n,
        out_specs=[vmem] * n,
        out_shape=[jax.ShapeDtypeStruct(p.shape, p.dtype) for p in pieces],
        scratch_shapes=[pltpu.SemaphoreType.DMA((n,)), pltpu.SemaphoreType.DMA((n,))],
        compiler_params=pltpu.CompilerParams(collective_id=2, has_side_effects=True),
    )(*pieces)


def scale_kernel(x_ref, s_ref, o_ref):
    o_ref[...] = x_ref[...] * s_ref[...]


def scale_rows(x, inv):
    cx, cy, k = x.shape
    return pl.pallas_call(
        scale_kernel,
        grid=(cx // SCALE_ROWS,),
        in_specs=[pl.BlockSpec((SCALE_ROWS, cy, k), lambda i: (i, 0, 0)), pl.BlockSpec((1, k), lambda i: (0, 0))],
        out_specs=pl.BlockSpec((SCALE_ROWS, cy, k), lambda i: (i, 0, 0)),
        out_shape=jax.ShapeDtypeStruct(x.shape, x.dtype),
        cost_estimate=pl.CostEstimate(flops=x.size, transcendentals=0, bytes_accessed=x.size * 8),
    )(x, inv)


def local(detail, coarse, diagonal, parents, tile_mask):
    tiles_x, tiles_y = parents.shape
    cells_x, cells_y, columns = detail.shape
    nw, nn = lax.axis_size("wide"), lax.axis_size("narrow")
    total_cells = cells_x * nw * cells_y * nn
    mask_float = tile_mask.astype(jnp.float32)

    tile_values = gather_tiles(parents, coarse, nn).T
    tv = tile_values.reshape(tiles_x, tiles_y, columns)

    m_rows = jnp.repeat(mask_float, TS, axis=1)
    m0 = jnp.broadcast_to(m_rows[:, :, None], (tiles_x, cells_y, columns))
    cm0 = m0 * jnp.repeat(tv, TS, axis=1)

    h = HALO
    c0_top = cm0[0][None] + m0[0][None] * detail[:h].astype(jnp.float32)
    c0_bot = cm0[-1][None] + m0[-1][None] * detail[-h:].astype(jnp.float32)
    cm_rep = jnp.repeat(cm0, TS, axis=0)
    m_rep = jnp.repeat(m0, TS, axis=0)
    c0_left = cm_rep[:, :h] + m_rep[:, :h] * detail[:, :h].astype(jnp.float32)
    c0_right = cm_rep[:, -h:] + m_rep[:, -h:] * detail[:, -h:].astype(jnp.float32)

    cell_mask = jnp.repeat(jnp.repeat(mask_float, TS, axis=0), TS, axis=1)
    g_own = (cell_mask * (4.0 + diagonal) - CENTER) / HALF_WIDTH
    h_own = cell_mask / HALF_WIDTH
    gh = jnp.stack([g_own, h_own])

    def edge(a, dw, dn, rows_axis, cols_axis):
        idx = [slice(None)] * a.ndim
        if dw == 1:
            idx[rows_axis] = slice(a.shape[rows_axis] - h, None)
        elif dw == -1:
            idx[rows_axis] = slice(0, h)
        if dn == 1:
            idx[cols_axis] = slice(a.shape[cols_axis] - h, None)
        elif dn == -1:
            idx[cols_axis] = slice(0, h)
        return a[tuple(idx)]

    c0_pieces = {
        (1, 0): c0_bot, (-1, 0): c0_top,
        (0, 1): c0_right.transpose(1, 0, 2), (0, -1): c0_left.transpose(1, 0, 2),
        (1, 1): c0_bot[:, -h:], (1, -1): c0_bot[:, :h], (-1, 1): c0_top[:, -h:], (-1, -1): c0_top[:, :h],
    }
    pieces = []
    for dw, dn in DIRS:
        pieces.append(c0_pieces[(dw, dn)])
        e = edge(gh, dw, dn, 1, 2)
        pieces.append(e.transpose(0, 2, 1) if dw == 0 else e)
    got = exchange_halos(pieces, nw, nn)
    hc = {dirn: got[2 * k] for k, dirn in enumerate(DIRS)}
    hg = {dirn: got[2 * k + 1] for k, dirn in enumerate(DIRS)}
    for dirn in ((0, 1), (0, -1)):
        hg[dirn] = hg[dirn].transpose(0, 2, 1)
    halos = [hc[(1, 0)], hc[(-1, 0)], hc[(0, 1)], hc[(0, -1)],
             hc[(1, 1)], hc[(1, -1)], hc[(-1, 1)], hc[(-1, -1)]]

    rpad = LPAD - h
    z3 = jnp.zeros((2, h, rpad), jnp.float32)
    zc = jnp.zeros((2, cells_x, rpad), jnp.float32)
    gh_ext = jnp.concatenate(
        [
            jnp.concatenate([z3, hg[(1, 1)], hg[(1, 0)], hg[(1, -1)], z3], axis=2),
            jnp.concatenate([zc, hg[(0, 1)], gh, hg[(0, -1)], zc], axis=2),
            jnp.concatenate([z3, hg[(-1, 1)], hg[(-1, 0)], hg[(-1, -1)], z3], axis=2),
        ],
        axis=1,
    )
    width = cells_y + 2 * LPAD
    g_b = jnp.broadcast_to(gh_ext[0][:, :, None], (cells_x + 2 * h, width, columns))
    h_rows = gh_ext[1][jnp.array([0] + [h + TS * t for t in range(tiles_x)] + [h + cells_x])]
    h_b = jnp.broadcast_to(h_rows[:, :, None], (tiles_x + 2, width, columns))

    cheb_three, squares = run_stencil(detail, cm0, m0, halos, g_b, h_b, nw, nn)
    inv = 1.0 / jnp.sqrt(squares / total_cells + EPSILON)
    return scale_rows(cheb_three, inv)


def solution(mesh):
    in_specs = (
        P("wide", "narrow", None),
        P("wide", "narrow", None),
        P("wide", "narrow"),
        P("wide", "narrow"),
        P("wide", "narrow"),
    )
    out_specs = P("wide", "narrow", None)
    return jax.shard_map(local, mesh=mesh, in_specs=in_specs, out_specs=out_specs, check_vma=False)
```

```python
import functools

import jax
import jax.numpy as jnp
from jax import lax
from jax.experimental import pallas as pl
from jax.experimental.pallas import tpu as pltpu
from jax.sharding import PartitionSpec as P

TS = 8
CENTER = 7.5
HALF_WIDTH = 4.5
EPSILON = 1e-06

HALO = 3
LPAD = 8
RING = 16
ROWS = 8
SCALE_ROWS = 32
DIRS = ((1, 0), (-1, 0), (0, 1), (0, -1), (1, 1), (1, -1), (-1, 1), (-1, -1))
DIAGONALS = DIRS[4:]
VERTICAL = ((1, 0), (-1, 0)) + DIAGONALS


def inside(me_w, me_n, dw, dn, nw, nn):
    w, n = me_w + dw, me_n + dn
    return jnp.logical_and(jnp.logical_and(w >= 0, w < nw), jnp.logical_and(n >= 0, n < nn))


def signal_others(barrier, me_w, me_n, nw, nn, dirs):
    count = 0
    for dw, dn in dirs:
        ok = inside(me_w, me_n, dw, dn, nw, nn)

        @pl.when(ok)
        def _():
            pl.semaphore_signal(barrier, inc=1, device_id=(jnp.clip(me_w + dw, 0, nw - 1),
                                jnp.clip(me_n + dn, 0, nn - 1)), device_id_type=pl.DeviceIdType.MESH)
        count = count + ok.astype(jnp.int32)
    return count


def halo_copy(ins, outs, send, recv, d, sign, me_w, me_n, nw, nn):
    dw, dn = DIRS[d]
    return pltpu.make_async_remote_copy(
        src_ref=ins[d], dst_ref=outs[d], send_sem=send.at[d], recv_sem=recv.at[d],
        device_id=(jnp.clip(me_w + sign * dw, 0, nw - 1), jnp.clip(me_n + sign * dn, 0, nn - 1)),
        device_id_type=pl.DeviceIdType.MESH)


def halo_start(ins, outs, send, recv, me_w, me_n, nw, nn):
    for d, (dw, dn) in enumerate(DIRS):
        @pl.when(inside(me_w, me_n, dw, dn, nw, nn))
        def _():
            halo_copy(ins, outs, send, recv, d, 1, me_w, me_n, nw, nn).start()


def halo_finish(ins, outs, send, recv, me_w, me_n, nw, nn):
    for d, (dw, dn) in enumerate(DIRS):
        src_ok = inside(me_w, me_n, -dw, -dn, nw, nn)

        @pl.when(src_ok)
        def _():
            halo_copy(ins, outs, send, recv, d, -1, me_w, me_n, nw, nn).wait_recv()

        @pl.when(jnp.logical_not(src_ok))
        def _():
            outs[d][...] = jnp.zeros(outs[d].shape, outs[d].dtype)

    for d, (dw, dn) in enumerate(DIRS):
        @pl.when(inside(me_w, me_n, dw, dn, nw, nn))
        def _():
            halo_copy(ins, outs, send, recv, d, 1, me_w, me_n, nw, nn).wait_send()


def shift_pairs(dw, dn, nw, nn):
    pairs = []
    for w in range(nw):
        for n in range(nn):
            tw, tn = w + dw, n + dn
            if 0 <= tw < nw and 0 <= tn < nn:
                pairs.append((w * nn + n, tw * nn + tn))
    return pairs


def exchange(pieces, dw, dn, nw, nn):
    flat = jnp.concatenate([p.reshape(-1) for p in pieces])
    got = lax.ppermute(flat, ("wide", "narrow"), shift_pairs(dw, dn, nw, nn))
    out, at = [], 0
    for p in pieces:
        out.append(got[at : at + p.size].reshape(p.shape))
        at += p.size
    return out


def stencil_kernel(nw, nn, *refs):
    nd = len(DIRS)
    det_ref, cm_ref, m_ref = refs[:3]
    sends = refs[3:3 + nd]
    g_ref, h_ref, out_ref, sq_ref, r0, r1, r2, ss_ref, part1, part2, q1, q2, s1, p1, s2, p2 = \
        refs[3 + nd:19 + nd]
    halos = refs[19 + nd:19 + 2 * nd]
    hs, hr = refs[19 + 2 * nd:]
    top_ref, bot_ref, left_ref, right_ref, tl_ref, tr_ref, bl_ref, br_ref = halos
    i = pl.program_id(0)
    me_w = lax.axis_index("wide")
    me_n = lax.axis_index("narrow")
    mesh_id = pl.DeviceIdType.MESH
    barrier = pltpu.get_barrier_semaphore()
    cx = det_ref.shape[0]
    width = g_ref.shape[1]
    ext_rows = g_ref.shape[0]
    cy = det_ref.shape[1]

    def c0_row(x):
        s = x % RING
        zero = jnp.zeros((width, det_ref.shape[2]), jnp.float32)

        @pl.when(x < HALO)
        def _():
            j = jnp.minimum(x, HALO - 1)
            r0[s] = zero
            r0[s, LPAD - HALO:LPAD] = tl_ref[j]
            r0[s, LPAD:LPAD + cy] = top_ref[j]
            r0[s, LPAD + cy:LPAD + cy + HALO] = tr_ref[j]

        @pl.when(x >= HALO + cx)
        def _():
            j = jnp.clip(x - HALO - cx, 0, HALO - 1)
            r0[s] = zero
            r0[s, LPAD - HALO:LPAD] = bl_ref[j]
            r0[s, LPAD:LPAD + cy] = bot_ref[j]
            r0[s, LPAD + cy:LPAD + cy + HALO] = br_ref[j]

        @pl.when(jnp.logical_and(x >= HALO, x < HALO + cx))
        def _():
            b = jnp.clip(x - HALO, 0, cx - 1)
            t = b // TS
            r0[s, 0:LPAD] = zero[0:LPAD]
            for p in range(HALO):
                r0[s, pl.ds(LPAD - HALO + p, 1)] = left_ref[p, pl.ds(b, 1)]
            r0[s, LPAD:LPAD + cy] = cm_ref[t] + m_ref[t] * det_ref[b].astype(jnp.float32)
            r0[s, LPAD + cy:width] = zero[0:width - LPAD - cy]
            for p in range(HALO):
                r0[s, pl.ds(LPAD + cy + p, 1)] = right_ref[p, pl.ds(b, 1)]

    def apply_b(src, x):
        v = src[x % RING]
        nb = src[(x + 1) % RING] + src[(x + RING - 1) % RING]
        nb = nb + pltpu.roll(v, width - 1, 0) + pltpu.roll(v, 1, 0)
        return g_ref[x] * v - h_ref[(x + TS - HALO) // TS] * nb

    def c1_row(x):
        r1[x % RING] = apply_b(r0, x)

    def c2_row(x):
        r2[x % RING] = 2.0 * apply_b(r1, x) - r0[x % RING]

    def c3_row(x):
        c3 = 2.0 * apply_b(r2, x) - r1[x % RING]
        c3 = c3[LPAD:LPAD + cy]
        out_ref[x - HALO - ROWS * i] = c3
        sq = c3 * c3
        ss_ref[...] += jnp.sum(sq.reshape(cy // 8, 8, sq.shape[-1]), axis=0)

    def rows(fn, lo, n):
        def body(k, carry):
            fn(lo + k)
            return carry
        lax.fori_loop(0, n, body, 0)

    @pl.when(i == 0)
    def _():
        for k in range(1, nn):
            pl.semaphore_signal(barrier, inc=1, device_id=(me_w, (me_n + k) % nn), device_id_type=mesh_id)
        for k in range(1, nw):
            pl.semaphore_signal(barrier, inc=1, device_id=((me_w + k) % nw, me_n), device_id_type=mesh_id)
        diag = signal_others(barrier, me_w, me_n, nw, nn, DIAGONALS)
        pl.semaphore_wait(barrier, nn - 1 + nw - 1 + diag)
        halo_start(sends, halos, hs, hr, me_w, me_n, nw, nn)
        halo_finish(sends, halos, hs, hr, me_w, me_n, nw, nn)
        ss_ref[...] = jnp.zeros_like(ss_ref)
        rows(c0_row, 0, 2 * HALO)
        rows(c1_row, 1, 2 * HALO - 2)
        rows(c2_row, 2, 2 * HALO - 4)

    base = ROWS * i
    rows(c0_row, base + 2 * HALO, ROWS)
    rows(c1_row, base + 2 * HALO - 1, ROWS)
    rows(c2_row, base + 2 * HALO - 2, ROWS)
    rows(c3_row, base + HALO, ROWS)

    @pl.when(i == pl.num_programs(0) - 1)
    def _():
        part1[...] = jnp.sum(ss_ref[...], axis=0, keepdims=True)
        part2[...] = exchange_sum(part1, q1, s1, p1, me_n, nn, lambda j: (me_w, j))
        sq_ref[...] = exchange_sum(part2, q2, s2, p2, me_w, nw, lambda j: (j, me_n))


def exchange_sum(src, slots, send, recv, me, n, peer_of):
    mesh_id = pl.DeviceIdType.MESH
    copies = []
    for k in range(1, n):
        c = pltpu.make_async_remote_copy(
            src_ref=src, dst_ref=slots.at[me], send_sem=send.at[k], recv_sem=recv.at[me],
            device_id=peer_of((me + k) % n), device_id_type=mesh_id)
        c.start()
        copies.append(c)
    slots[me] = src[...]
    for k in range(1, n):
        other = (me + k) % n
        pltpu.make_async_remote_copy(
            src_ref=src, dst_ref=slots.at[other], send_sem=send.at[k], recv_sem=recv.at[other],
            device_id=peer_of(other), device_id_type=mesh_id).wait_recv()
    for c in copies:
        c.wait_send()
    return jnp.sum(slots[...], axis=0)


def run_stencil(det, cm, m, sends, g, h, nw, nn):
    cx, cy, k = det.shape
    width = g.shape[1]
    steps = cx // ROWS
    vmem = pl.BlockSpec(memory_space=pltpu.VMEM)
    ops = cx * cy * k * 3 * 12
    return pl.pallas_call(
        functools.partial(stencil_kernel, nw, nn),
        grid=(steps,),
        in_specs=[vmem] * (5 + len(sends)),
        out_specs=[
            pl.BlockSpec((ROWS, cy, k), lambda i: (i, 0, 0)),
            pl.BlockSpec((1, k), lambda i: (0, 0)),
        ],
        out_shape=[
            jax.ShapeDtypeStruct((cx, cy, k), jnp.float32),
            jax.ShapeDtypeStruct((1, k), jnp.float32),
        ],
        scratch_shapes=[pltpu.VMEM((RING, width, k), jnp.float32) for _ in range(3)] + [
            pltpu.VMEM((8, k), jnp.float32),
            pltpu.VMEM((1, k), jnp.float32),
            pltpu.VMEM((1, k), jnp.float32),
            pltpu.VMEM((nn, 1, k), jnp.float32),
            pltpu.VMEM((nw, 1, k), jnp.float32),
            pltpu.SemaphoreType.DMA((nn,)),
            pltpu.SemaphoreType.DMA((nn,)),
            pltpu.SemaphoreType.DMA((nw,)),
            pltpu.SemaphoreType.DMA((nw,)),
        ] + [pltpu.VMEM(p.shape, p.dtype) for p in sends] + [
            pltpu.SemaphoreType.DMA((len(sends),)),
            pltpu.SemaphoreType.DMA((len(sends),)),
        ],
        compiler_params=pltpu.CompilerParams(
            dimension_semantics=("arbitrary",), vmem_limit_bytes=56 * 1024 * 1024,
            collective_id=0, has_side_effects=True,
        ),
        cost_estimate=pl.CostEstimate(
            flops=ops, transcendentals=0, bytes_accessed=det.size * 2 + cx * cy * k * 4 + g.size * 4
        ),
    )(det, cm, m, *sends, g, h)


def gather_kernel(nw, nn, cols, *refs):
    nd = len(DIRS)
    par_ref, ct_ref = refs[:2]
    gh_in = refs[2:2 + nd]
    o_ref = refs[2 + nd]
    gh_out = refs[3 + nd:3 + 2 * nd]
    pslots, stage, tslots, ps, pq, ts, tq, hs, hr = refs[3 + 2 * nd:]
    me_w = lax.axis_index("wide")
    me_n = lax.axis_index("narrow")
    mesh_id = pl.DeviceIdType.MESH
    barrier = pltpu.get_barrier_semaphore()
    for k in range(1, nn):
        pl.semaphore_signal(barrier, inc=1, device_id=(me_w, (me_n + k) % nn), device_id_type=mesh_id)
    extra = signal_others(barrier, me_w, me_n, nw, nn, VERTICAL)
    pl.semaphore_wait(barrier, nn - 1 + extra)
    halo_start(gh_in, gh_out, hs, hr, me_w, me_n, nw, nn)

    def par_copy(k, other, slot):
        return pltpu.make_async_remote_copy(
            src_ref=par_ref, dst_ref=pslots.at[slot], send_sem=ps.at[k], recv_sem=pq.at[slot],
            device_id=(me_w, other), device_id_type=mesh_id)

    sent = []
    for k in range(1, nn):
        c = par_copy(k, (me_n + k) % nn, me_n)
        c.start()
        sent.append(c)

    local_cells = ct_ref.shape[0]
    ncols = local_cells // cols

    def contribution(par):
        col = par % (ncols * nn)
        idx = (par // (ncols * nn)) * ncols + col % ncols
        idx = jnp.where(col // ncols == me_n, idx, -1)
        rows = lax.broadcasted_iota(jnp.int32, (local_cells, par.shape[-1]), 0)
        onehot = (rows == idx).astype(jnp.bfloat16)
        got = lax.dot_general(ct_ref[...], onehot, (((0,), (0,)), ((), ())),
                              preferred_element_type=jnp.float32)
        return got.astype(jnp.bfloat16)

    tslots[me_n] = contribution(par_ref[...])
    out_copies = []
    for k in range(1, nn):
        other = (me_n + k) % nn
        par_copy(k, other, other).wait_recv()
        stage[k] = contribution(pslots[other])
        c = pltpu.make_async_remote_copy(
            src_ref=stage.at[k], dst_ref=tslots.at[me_n], send_sem=ts.at[k], recv_sem=tq.at[me_n],
            device_id=(me_w, other), device_id_type=mesh_id)
        c.start()
        out_copies.append(c)
    for k in range(1, nn):
        other = (me_n + k) % nn
        pltpu.make_async_remote_copy(
            src_ref=stage.at[k], dst_ref=tslots.at[other], send_sem=ts.at[k], recv_sem=tq.at[other],
            device_id=(me_w, other), device_id_type=mesh_id).wait_recv()
    for c in sent + out_copies:
        c.wait_send()
    halo_finish(gh_in, gh_out, hs, hr, me_w, me_n, nw, nn)
    total = tslots[0].astype(jnp.float32)
    for j in range(1, nn):
        total = total + tslots[j].astype(jnp.float32)
    o_ref[...] = total


def gather_tiles(parents, coarse, gh_pieces, nw, nn):
    ccx, ccy, k = coarse.shape
    par = parents.reshape(1, -1)
    n_t = par.shape[-1]
    ct = coarse.reshape(ccx * ccy, k)
    vmem = pl.BlockSpec(memory_space=pltpu.VMEM)
    return pl.pallas_call(
        functools.partial(gather_kernel, nw, nn, ccx),
        in_specs=[vmem] * (2 + len(gh_pieces)),
        out_specs=[vmem] * (1 + len(gh_pieces)),
        out_shape=[jax.ShapeDtypeStruct((k, n_t), jnp.float32)]
        + [jax.ShapeDtypeStruct(p.shape, p.dtype) for p in gh_pieces],
        scratch_shapes=[
            pltpu.VMEM((nn, 1, n_t), jnp.int32),
            pltpu.VMEM((nn, k, n_t), jnp.bfloat16),
            pltpu.VMEM((nn, k, n_t), jnp.bfloat16),
            pltpu.SemaphoreType.DMA((nn,)),
            pltpu.SemaphoreType.DMA((nn,)),
            pltpu.SemaphoreType.DMA((nn,)),
            pltpu.SemaphoreType.DMA((nn,)),
            pltpu.SemaphoreType.DMA((len(gh_pieces),)),
            pltpu.SemaphoreType.DMA((len(gh_pieces),)),
        ],
        compiler_params=pltpu.CompilerParams(collective_id=1, has_side_effects=True),
    )(par, ct, *gh_pieces)


def scale_kernel(x_ref, s_ref, o_ref):
    o_ref[...] = x_ref[...] * s_ref[...]


def scale_rows(x, inv):
    cx, cy, k = x.shape
    return pl.pallas_call(
        scale_kernel,
        grid=(cx // SCALE_ROWS,),
        in_specs=[pl.BlockSpec((SCALE_ROWS, cy, k), lambda i: (i, 0, 0)), pl.BlockSpec((1, k), lambda i: (0, 0))],
        out_specs=pl.BlockSpec((SCALE_ROWS, cy, k), lambda i: (i, 0, 0)),
        out_shape=jax.ShapeDtypeStruct(x.shape, x.dtype),
        cost_estimate=pl.CostEstimate(flops=x.size, transcendentals=0, bytes_accessed=x.size * 8),
    )(x, inv)


def local(detail, coarse, diagonal, parents, tile_mask):
    tiles_x, tiles_y = parents.shape
    cells_x, cells_y, columns = detail.shape
    nw, nn = lax.axis_size("wide"), lax.axis_size("narrow")
    total_cells = cells_x * nw * cells_y * nn
    mask_float = tile_mask.astype(jnp.float32)

    h = HALO
    cell_mask = jnp.repeat(jnp.repeat(mask_float, TS, axis=0), TS, axis=1)
    g_own = (cell_mask * (4.0 + diagonal) - CENTER) / HALF_WIDTH
    h_own = cell_mask / HALF_WIDTH
    gh = jnp.stack([g_own, h_own])

    def edge(a, dw, dn, rows_axis, cols_axis):
        idx = [slice(None)] * a.ndim
        if dw == 1:
            idx[rows_axis] = slice(a.shape[rows_axis] - h, None)
        elif dw == -1:
            idx[rows_axis] = slice(0, h)
        if dn == 1:
            idx[cols_axis] = slice(a.shape[cols_axis] - h, None)
        elif dn == -1:
            idx[cols_axis] = slice(0, h)
        return a[tuple(idx)]

    gh_pieces = []
    for dw, dn in DIRS:
        e = edge(gh, dw, dn, 1, 2)
        gh_pieces.append(e.transpose(0, 2, 1) if dw == 0 else e)
    got = gather_tiles(parents, coarse, gh_pieces, nw, nn)
    tile_values = got[0].T
    hg = {dirn: got[1 + k] for k, dirn in enumerate(DIRS)}
    for dirn in ((0, 1), (0, -1)):
        hg[dirn] = hg[dirn].transpose(0, 2, 1)
    tv = tile_values.reshape(tiles_x, tiles_y, columns)

    m_rows = jnp.repeat(mask_float, TS, axis=1)
    m0 = jnp.broadcast_to(m_rows[:, :, None], (tiles_x, cells_y, columns))
    cm0 = m0 * jnp.repeat(tv, TS, axis=1)

    c0_top = cm0[0][None] + m0[0][None] * detail[:h].astype(jnp.float32)
    c0_bot = cm0[-1][None] + m0[-1][None] * detail[-h:].astype(jnp.float32)
    cm_rep = jnp.repeat(cm0, TS, axis=0)
    m_rep = jnp.repeat(m0, TS, axis=0)
    c0_left = cm_rep[:, :h] + m_rep[:, :h] * detail[:, :h].astype(jnp.float32)
    c0_right = cm_rep[:, -h:] + m_rep[:, -h:] * detail[:, -h:].astype(jnp.float32)
    c0_pieces = {
        (1, 0): c0_bot, (-1, 0): c0_top,
        (0, 1): c0_right.transpose(1, 0, 2), (0, -1): c0_left.transpose(1, 0, 2),
        (1, 1): c0_bot[:, -h:], (1, -1): c0_bot[:, :h], (-1, 1): c0_top[:, -h:], (-1, -1): c0_top[:, :h],
    }
    sends = [c0_pieces[dirn] for dirn in DIRS]

    rpad = LPAD - h
    z3 = jnp.zeros((2, h, rpad), jnp.float32)
    zc = jnp.zeros((2, cells_x, rpad), jnp.float32)
    gh_ext = jnp.concatenate(
        [
            jnp.concatenate([z3, hg[(1, 1)], hg[(1, 0)], hg[(1, -1)], z3], axis=2),
            jnp.concatenate([zc, hg[(0, 1)], gh, hg[(0, -1)], zc], axis=2),
            jnp.concatenate([z3, hg[(-1, 1)], hg[(-1, 0)], hg[(-1, -1)], z3], axis=2),
        ],
        axis=1,
    )
    width = cells_y + 2 * LPAD
    g_b = jnp.broadcast_to(gh_ext[0][:, :, None], (cells_x + 2 * h, width, columns))
    h_rows = gh_ext[1][jnp.array([0] + [h + TS * t for t in range(tiles_x)] + [h + cells_x])]
    h_b = jnp.broadcast_to(h_rows[:, :, None], (tiles_x + 2, width, columns))

    cheb_three, squares = run_stencil(detail, cm0, m0, sends, g_b, h_b, nw, nn)
    inv = 1.0 / jnp.sqrt(squares / total_cells + EPSILON)
    return scale_rows(cheb_three, inv)


def solution(mesh):
    in_specs = (
        P("wide", "narrow", None),
        P("wide", "narrow", None),
        P("wide", "narrow"),
        P("wide", "narrow"),
        P("wide", "narrow"),
    )
    out_specs = P("wide", "narrow", None)
    return jax.shard_map(local, mesh=mesh, in_specs=in_specs, out_specs=out_specs, check_vma=False)
```

```python
import functools

import jax
import jax.numpy as jnp
from jax import lax
from jax.experimental import pallas as pl
from jax.experimental.pallas import tpu as pltpu
from jax.sharding import PartitionSpec as P

TS = 8
CENTER = 7.5
HALF_WIDTH = 4.5
EPSILON = 1e-06

HALO = 3
LPAD = 8
RING = 16
ROWS = 8
SCALE_ROWS = 64
DIRS = ((1, 0), (-1, 0), (0, 1), (0, -1), (1, 1), (1, -1), (-1, 1), (-1, -1))
DIAGONALS = DIRS[4:]
VERTICAL = ((1, 0), (-1, 0)) + DIAGONALS


def inside(me_w, me_n, dw, dn, nw, nn):
    w, n = me_w + dw, me_n + dn
    return jnp.logical_and(jnp.logical_and(w >= 0, w < nw), jnp.logical_and(n >= 0, n < nn))


def signal_others(barrier, me_w, me_n, nw, nn, dirs):
    count = 0
    for dw, dn in dirs:
        ok = inside(me_w, me_n, dw, dn, nw, nn)

        @pl.when(ok)
        def _():
            pl.semaphore_signal(barrier, inc=1, device_id=(jnp.clip(me_w + dw, 0, nw - 1),
                                jnp.clip(me_n + dn, 0, nn - 1)), device_id_type=pl.DeviceIdType.MESH)
        count = count + ok.astype(jnp.int32)
    return count


def halo_copy(ins, outs, send, recv, d, sign, me_w, me_n, nw, nn):
    dw, dn = DIRS[d]
    return pltpu.make_async_remote_copy(
        src_ref=ins[d], dst_ref=outs[d], send_sem=send.at[d], recv_sem=recv.at[d],
        device_id=(jnp.clip(me_w + sign * dw, 0, nw - 1), jnp.clip(me_n + sign * dn, 0, nn - 1)),
        device_id_type=pl.DeviceIdType.MESH)


def halo_start(ins, outs, send, recv, me_w, me_n, nw, nn):
    for d, (dw, dn) in enumerate(DIRS):
        @pl.when(inside(me_w, me_n, dw, dn, nw, nn))
        def _():
            halo_copy(ins, outs, send, recv, d, 1, me_w, me_n, nw, nn).start()


def halo_finish(ins, outs, send, recv, me_w, me_n, nw, nn):
    for d, (dw, dn) in enumerate(DIRS):
        src_ok = inside(me_w, me_n, -dw, -dn, nw, nn)

        @pl.when(src_ok)
        def _():
            halo_copy(ins, outs, send, recv, d, -1, me_w, me_n, nw, nn).wait_recv()

        @pl.when(jnp.logical_not(src_ok))
        def _():
            outs[d][...] = jnp.zeros(outs[d].shape, outs[d].dtype)

    for d, (dw, dn) in enumerate(DIRS):
        @pl.when(inside(me_w, me_n, dw, dn, nw, nn))
        def _():
            halo_copy(ins, outs, send, recv, d, 1, me_w, me_n, nw, nn).wait_send()


def shift_pairs(dw, dn, nw, nn):
    pairs = []
    for w in range(nw):
        for n in range(nn):
            tw, tn = w + dw, n + dn
            if 0 <= tw < nw and 0 <= tn < nn:
                pairs.append((w * nn + n, tw * nn + tn))
    return pairs


def exchange(pieces, dw, dn, nw, nn):
    flat = jnp.concatenate([p.reshape(-1) for p in pieces])
    got = lax.ppermute(flat, ("wide", "narrow"), shift_pairs(dw, dn, nw, nn))
    out, at = [], 0
    for p in pieces:
        out.append(got[at : at + p.size].reshape(p.shape))
        at += p.size
    return out


def stencil_kernel(nw, nn, *refs):
    nd = len(DIRS)
    det_ref, cm_ref, m_ref = refs[:3]
    sends = refs[3:3 + nd]
    g_ref, h_ref, out_ref, sq_ref, r0, r1, r2, ss_ref, part1, part2, q1, q2, s1, p1, s2, p2 = \
        refs[3 + nd:19 + nd]
    halos = refs[19 + nd:19 + 2 * nd]
    hs, hr = refs[19 + 2 * nd:]
    top_ref, bot_ref, left_ref, right_ref, tl_ref, tr_ref, bl_ref, br_ref = halos
    i = pl.program_id(0)
    me_w = lax.axis_index("wide")
    me_n = lax.axis_index("narrow")
    mesh_id = pl.DeviceIdType.MESH
    barrier = pltpu.get_barrier_semaphore()
    cx = det_ref.shape[0]
    width = g_ref.shape[1]
    ext_rows = g_ref.shape[0]
    cy = det_ref.shape[1]

    def c0_row(x):
        s = x % RING
        zero = jnp.zeros((width, det_ref.shape[2]), jnp.float32)

        @pl.when(x < HALO)
        def _():
            j = jnp.minimum(x, HALO - 1)
            r0[s] = zero
            r0[s, LPAD - HALO:LPAD] = tl_ref[j]
            r0[s, LPAD:LPAD + cy] = top_ref[j]
            r0[s, LPAD + cy:LPAD + cy + HALO] = tr_ref[j]

        @pl.when(x >= HALO + cx)
        def _():
            j = jnp.clip(x - HALO - cx, 0, HALO - 1)
            r0[s] = zero
            r0[s, LPAD - HALO:LPAD] = bl_ref[j]
            r0[s, LPAD:LPAD + cy] = bot_ref[j]
            r0[s, LPAD + cy:LPAD + cy + HALO] = br_ref[j]

        @pl.when(jnp.logical_and(x >= HALO, x < HALO + cx))
        def _():
            b = jnp.clip(x - HALO, 0, cx - 1)
            t = b // TS
            r0[s, 0:LPAD] = zero[0:LPAD]
            for p in range(HALO):
                r0[s, pl.ds(LPAD - HALO + p, 1)] = left_ref[p, pl.ds(b, 1)]
            r0[s, LPAD:LPAD + cy] = cm_ref[t] + m_ref[t] * det_ref[b].astype(jnp.float32)
            r0[s, LPAD + cy:width] = zero[0:width - LPAD - cy]
            for p in range(HALO):
                r0[s, pl.ds(LPAD + cy + p, 1)] = right_ref[p, pl.ds(b, 1)]

    def apply_b(src, x):
        v = src[x % RING]
        nb = src[(x + 1) % RING] + src[(x + RING - 1) % RING]
        nb = nb + pltpu.roll(v, width - 1, 0) + pltpu.roll(v, 1, 0)
        return g_ref[x] * v - h_ref[(x + TS - HALO) // TS] * nb

    def c1_row(x):
        r1[x % RING] = apply_b(r0, x)

    def c2_row(x):
        r2[x % RING] = 2.0 * apply_b(r1, x) - r0[x % RING]

    def c3_row(x):
        c3 = 2.0 * apply_b(r2, x) - r1[x % RING]
        c3 = c3[LPAD:LPAD + cy]
        out_ref[x - HALO - ROWS * i] = c3
        sq = c3 * c3
        ss_ref[...] += jnp.sum(sq.reshape(cy // 8, 8, sq.shape[-1]), axis=0)

    def rows(fn, lo, n):
        def body(k, carry):
            fn(lo + k)
            return carry
        lax.fori_loop(0, n, body, 0)

    @pl.when(i == 0)
    def _():
        for k in range(1, nn):
            pl.semaphore_signal(barrier, inc=1, device_id=(me_w, (me_n + k) % nn), device_id_type=mesh_id)
        for k in range(1, nw):
            pl.semaphore_signal(barrier, inc=1, device_id=((me_w + k) % nw, me_n), device_id_type=mesh_id)
        diag = signal_others(barrier, me_w, me_n, nw, nn, DIAGONALS)
        pl.semaphore_wait(barrier, nn - 1 + nw - 1 + diag)
        halo_start(sends, halos, hs, hr, me_w, me_n, nw, nn)
        halo_finish(sends, halos, hs, hr, me_w, me_n, nw, nn)
        ss_ref[...] = jnp.zeros_like(ss_ref)
        rows(c0_row, 0, 2 * HALO)
        rows(c1_row, 1, 2 * HALO - 2)
        rows(c2_row, 2, 2 * HALO - 4)

    base = ROWS * i
    rows(c0_row, base + 2 * HALO, ROWS)
    rows(c1_row, base + 2 * HALO - 1, ROWS)
    rows(c2_row, base + 2 * HALO - 2, ROWS)
    rows(c3_row, base + HALO, ROWS)

    @pl.when(i == pl.num_programs(0) - 1)
    def _():
        part1[...] = jnp.sum(ss_ref[...], axis=0, keepdims=True)
        part2[...] = exchange_sum(part1, q1, s1, p1, me_n, nn, lambda j: (me_w, j))
        sq_ref[...] = exchange_sum(part2, q2, s2, p2, me_w, nw, lambda j: (j, me_n))


def exchange_sum(src, slots, send, recv, me, n, peer_of):
    mesh_id = pl.DeviceIdType.MESH
    copies = []
    for k in range(1, n):
        c = pltpu.make_async_remote_copy(
            src_ref=src, dst_ref=slots.at[me], send_sem=send.at[k], recv_sem=recv.at[me],
            device_id=peer_of((me + k) % n), device_id_type=mesh_id)
        c.start()
        copies.append(c)
    slots[me] = src[...]
    for k in range(1, n):
        other = (me + k) % n
        pltpu.make_async_remote_copy(
            src_ref=src, dst_ref=slots.at[other], send_sem=send.at[k], recv_sem=recv.at[other],
            device_id=peer_of(other), device_id_type=mesh_id).wait_recv()
    for c in copies:
        c.wait_send()
    return jnp.sum(slots[...], axis=0)


def run_stencil(det, cm, m, sends, g, h, nw, nn):
    cx, cy, k = det.shape
    width = g.shape[1]
    steps = cx // ROWS
    vmem = pl.BlockSpec(memory_space=pltpu.VMEM)
    ops = cx * cy * k * 3 * 12
    return pl.pallas_call(
        functools.partial(stencil_kernel, nw, nn),
        grid=(steps,),
        in_specs=[vmem] * (5 + len(sends)),
        out_specs=[
            pl.BlockSpec((ROWS, cy, k), lambda i: (i, 0, 0)),
            pl.BlockSpec((1, k), lambda i: (0, 0)),
        ],
        out_shape=[
            jax.ShapeDtypeStruct((cx, cy, k), jnp.float32),
            jax.ShapeDtypeStruct((1, k), jnp.float32),
        ],
        scratch_shapes=[pltpu.VMEM((RING, width, k), jnp.float32) for _ in range(3)] + [
            pltpu.VMEM((8, k), jnp.float32),
            pltpu.VMEM((1, k), jnp.float32),
            pltpu.VMEM((1, k), jnp.float32),
            pltpu.VMEM((nn, 1, k), jnp.float32),
            pltpu.VMEM((nw, 1, k), jnp.float32),
            pltpu.SemaphoreType.DMA((nn,)),
            pltpu.SemaphoreType.DMA((nn,)),
            pltpu.SemaphoreType.DMA((nw,)),
            pltpu.SemaphoreType.DMA((nw,)),
        ] + [pltpu.VMEM(p.shape, p.dtype) for p in sends] + [
            pltpu.SemaphoreType.DMA((len(sends),)),
            pltpu.SemaphoreType.DMA((len(sends),)),
        ],
        compiler_params=pltpu.CompilerParams(
            dimension_semantics=("arbitrary",), vmem_limit_bytes=56 * 1024 * 1024,
            collective_id=0, has_side_effects=True,
        ),
        cost_estimate=pl.CostEstimate(
            flops=ops, transcendentals=0, bytes_accessed=det.size * 2 + cx * cy * k * 4 + g.size * 4
        ),
    )(det, cm, m, *sends, g, h)


def gather_kernel(nw, nn, cols, *refs):
    nd = len(DIRS)
    par_ref, ct_ref = refs[:2]
    gh_in = refs[2:2 + nd]
    o_ref = refs[2 + nd]
    gh_out = refs[3 + nd:3 + 2 * nd]
    pslots, stage, tslots, ps, pq, ts, tq, hs, hr = refs[3 + 2 * nd:]
    me_w = lax.axis_index("wide")
    me_n = lax.axis_index("narrow")
    mesh_id = pl.DeviceIdType.MESH
    barrier = pltpu.get_barrier_semaphore()
    for k in range(1, nn):
        pl.semaphore_signal(barrier, inc=1, device_id=(me_w, (me_n + k) % nn), device_id_type=mesh_id)
    extra = signal_others(barrier, me_w, me_n, nw, nn, VERTICAL)
    pl.semaphore_wait(barrier, nn - 1 + extra)
    halo_start(gh_in, gh_out, hs, hr, me_w, me_n, nw, nn)

    def par_copy(k, other, slot):
        return pltpu.make_async_remote_copy(
            src_ref=par_ref, dst_ref=pslots.at[slot], send_sem=ps.at[k], recv_sem=pq.at[slot],
            device_id=(me_w, other), device_id_type=mesh_id)

    sent = []
    for k in range(1, nn):
        c = par_copy(k, (me_n + k) % nn, me_n)
        c.start()
        sent.append(c)

    local_cells = ct_ref.shape[0]
    ncols = local_cells // cols

    def contribution(par):
        col = par % (ncols * nn)
        idx = (par // (ncols * nn)) * ncols + col % ncols
        idx = jnp.where(col // ncols == me_n, idx, -1)
        rows = lax.broadcasted_iota(jnp.int32, (local_cells, par.shape[-1]), 0)
        onehot = (rows == idx).astype(jnp.bfloat16)
        got = lax.dot_general(ct_ref[...], onehot, (((0,), (0,)), ((), ())),
                              preferred_element_type=jnp.float32)
        return got.astype(jnp.bfloat16)

    tslots[me_n] = contribution(par_ref[...])
    out_copies = []
    for k in range(1, nn):
        other = (me_n + k) % nn
        par_copy(k, other, other).wait_recv()
        stage[k] = contribution(pslots[other])
        c = pltpu.make_async_remote_copy(
            src_ref=stage.at[k], dst_ref=tslots.at[me_n], send_sem=ts.at[k], recv_sem=tq.at[me_n],
            device_id=(me_w, other), device_id_type=mesh_id)
        c.start()
        out_copies.append(c)
    for k in range(1, nn):
        other = (me_n + k) % nn
        pltpu.make_async_remote_copy(
            src_ref=stage.at[k], dst_ref=tslots.at[other], send_sem=ts.at[k], recv_sem=tq.at[other],
            device_id=(me_w, other), device_id_type=mesh_id).wait_recv()
    for c in sent + out_copies:
        c.wait_send()
    halo_finish(gh_in, gh_out, hs, hr, me_w, me_n, nw, nn)
    total = tslots[0].astype(jnp.float32)
    for j in range(1, nn):
        total = total + tslots[j].astype(jnp.float32)
    o_ref[...] = total


def gather_tiles(parents, coarse, gh_pieces, nw, nn):
    ccx, ccy, k = coarse.shape
    par = parents.reshape(1, -1)
    n_t = par.shape[-1]
    ct = coarse.reshape(ccx * ccy, k)
    vmem = pl.BlockSpec(memory_space=pltpu.VMEM)
    return pl.pallas_call(
        functools.partial(gather_kernel, nw, nn, ccx),
        in_specs=[vmem] * (2 + len(gh_pieces)),
        out_specs=[vmem] * (1 + len(gh_pieces)),
        out_shape=[jax.ShapeDtypeStruct((k, n_t), jnp.float32)]
        + [jax.ShapeDtypeStruct(p.shape, p.dtype) for p in gh_pieces],
        scratch_shapes=[
            pltpu.VMEM((nn, 1, n_t), jnp.int32),
            pltpu.VMEM((nn, k, n_t), jnp.bfloat16),
            pltpu.VMEM((nn, k, n_t), jnp.bfloat16),
            pltpu.SemaphoreType.DMA((nn,)),
            pltpu.SemaphoreType.DMA((nn,)),
            pltpu.SemaphoreType.DMA((nn,)),
            pltpu.SemaphoreType.DMA((nn,)),
            pltpu.SemaphoreType.DMA((len(gh_pieces),)),
            pltpu.SemaphoreType.DMA((len(gh_pieces),)),
        ],
        compiler_params=pltpu.CompilerParams(collective_id=1, has_side_effects=True),
    )(par, ct, *gh_pieces)


def scale_kernel(x_ref, s_ref, o_ref):
    o_ref[...] = x_ref[...] * s_ref[...]


def scale_rows(x, inv):
    cx, cy, k = x.shape
    return pl.pallas_call(
        scale_kernel,
        grid=(cx // SCALE_ROWS,),
        in_specs=[pl.BlockSpec((SCALE_ROWS, cy, k), lambda i: (i, 0, 0)), pl.BlockSpec((1, k), lambda i: (0, 0))],
        out_specs=pl.BlockSpec((SCALE_ROWS, cy, k), lambda i: (i, 0, 0)),
        out_shape=jax.ShapeDtypeStruct(x.shape, x.dtype),
        cost_estimate=pl.CostEstimate(flops=x.size, transcendentals=0, bytes_accessed=x.size * 8),
    )(x, inv)


def local(detail, coarse, diagonal, parents, tile_mask):
    tiles_x, tiles_y = parents.shape
    cells_x, cells_y, columns = detail.shape
    nw, nn = lax.axis_size("wide"), lax.axis_size("narrow")
    total_cells = cells_x * nw * cells_y * nn
    mask_float = tile_mask.astype(jnp.float32)

    h = HALO
    cell_mask = jnp.repeat(jnp.repeat(mask_float, TS, axis=0), TS, axis=1)
    g_own = (cell_mask * (4.0 + diagonal) - CENTER) / HALF_WIDTH
    h_own = cell_mask / HALF_WIDTH
    gh = jnp.stack([g_own, h_own])

    def edge(a, dw, dn, rows_axis, cols_axis):
        idx = [slice(None)] * a.ndim
        if dw == 1:
            idx[rows_axis] = slice(a.shape[rows_axis] - h, None)
        elif dw == -1:
            idx[rows_axis] = slice(0, h)
        if dn == 1:
            idx[cols_axis] = slice(a.shape[cols_axis] - h, None)
        elif dn == -1:
            idx[cols_axis] = slice(0, h)
        return a[tuple(idx)]

    gh_t = gh.transpose(0, 2, 1)
    gh_pieces = []
    for dw, dn in DIRS:
        gh_pieces.append(edge(gh_t, dn, dw, 1, 2) if dw == 0 else edge(gh, dw, dn, 1, 2))
    got = gather_tiles(parents, coarse, gh_pieces, nw, nn)
    tile_values = got[0].T
    hg = {dirn: got[1 + k] for k, dirn in enumerate(DIRS)}
    tv = tile_values.reshape(tiles_x, tiles_y, columns)

    m_rows = jnp.repeat(mask_float, TS, axis=1)
    m0 = jnp.broadcast_to(m_rows[:, :, None], (tiles_x, cells_y, columns))
    cm0 = m0 * jnp.repeat(tv, TS, axis=1)

    c0_top = cm0[0][None] + m0[0][None] * detail[:h].astype(jnp.float32)
    c0_bot = cm0[-1][None] + m0[-1][None] * detail[-h:].astype(jnp.float32)
    cm_rep = jnp.repeat(cm0, TS, axis=0)
    m_rep = jnp.repeat(m0, TS, axis=0)
    c0_left = cm_rep[:, :h] + m_rep[:, :h] * detail[:, :h].astype(jnp.float32)
    c0_right = cm_rep[:, -h:] + m_rep[:, -h:] * detail[:, -h:].astype(jnp.float32)
    c0_pieces = {
        (1, 0): c0_bot, (-1, 0): c0_top,
        (0, 1): c0_right.transpose(1, 0, 2), (0, -1): c0_left.transpose(1, 0, 2),
        (1, 1): c0_bot[:, -h:], (1, -1): c0_bot[:, :h], (-1, 1): c0_top[:, -h:], (-1, -1): c0_top[:, :h],
    }
    sends = [c0_pieces[dirn] for dirn in DIRS]

    rpad = LPAD - h
    z3 = jnp.zeros((2, h, rpad), jnp.float32)
    zc = jnp.zeros((2, cells_x, rpad), jnp.float32)
    gh_ext = jnp.concatenate(
        [
            jnp.concatenate([z3, hg[(1, 1)], hg[(1, 0)], hg[(1, -1)], z3], axis=2),
            jnp.concatenate([zc.transpose(0, 2, 1), hg[(0, 1)], gh_t, hg[(0, -1)], zc.transpose(0, 2, 1)],
                            axis=1).transpose(0, 2, 1),
            jnp.concatenate([z3, hg[(-1, 1)], hg[(-1, 0)], hg[(-1, -1)], z3], axis=2),
        ],
        axis=1,
    )
    width = cells_y + 2 * LPAD
    g_b = jnp.broadcast_to(gh_ext[0][:, :, None], (cells_x + 2 * h, width, columns))
    h_rows = gh_ext[1][jnp.array([0] + [h + TS * t for t in range(tiles_x)] + [h + cells_x])]
    h_b = jnp.broadcast_to(h_rows[:, :, None], (tiles_x + 2, width, columns))

    cheb_three, squares = run_stencil(detail, cm0, m0, sends, g_b, h_b, nw, nn)
    inv = 1.0 / jnp.sqrt(squares / total_cells + EPSILON)
    return scale_rows(cheb_three, inv)


def solution(mesh):
    in_specs = (
        P("wide", "narrow", None),
        P("wide", "narrow", None),
        P("wide", "narrow"),
        P("wide", "narrow"),
        P("wide", "narrow"),
    )
    out_specs = P("wide", "narrow", None)
    return jax.shard_map(local, mesh=mesh, in_specs=in_specs, out_specs=out_specs, check_vma=False)
```

```python
import functools

import jax
import jax.numpy as jnp
from jax import lax
from jax.experimental import pallas as pl
from jax.experimental.pallas import tpu as pltpu
from jax.sharding import PartitionSpec as P

TS = 8
CENTER = 7.5
HALF_WIDTH = 4.5
EPSILON = 1e-06

HALO = 3
LPAD = 8
RING = 16
ROWS = 8
SCALE_ROWS = 64
DIRS = ((1, 0), (-1, 0), (0, 1), (0, -1), (1, 1), (1, -1), (-1, 1), (-1, -1))
DIAGONALS = DIRS[4:]
VERTICAL = ((1, 0), (-1, 0)) + DIAGONALS


def inside(me_w, me_n, dw, dn, nw, nn):
    w, n = me_w + dw, me_n + dn
    return jnp.logical_and(jnp.logical_and(w >= 0, w < nw), jnp.logical_and(n >= 0, n < nn))


def signal_others(barrier, me_w, me_n, nw, nn, dirs):
    count = 0
    for dw, dn in dirs:
        ok = inside(me_w, me_n, dw, dn, nw, nn)

        @pl.when(ok)
        def _():
            pl.semaphore_signal(barrier, inc=1, device_id=(jnp.clip(me_w + dw, 0, nw - 1),
                                jnp.clip(me_n + dn, 0, nn - 1)), device_id_type=pl.DeviceIdType.MESH)
        count = count + ok.astype(jnp.int32)
    return count


def halo_copy(ins, outs, send, recv, d, sign, me_w, me_n, nw, nn):
    dw, dn = DIRS[d]
    return pltpu.make_async_remote_copy(
        src_ref=ins[d], dst_ref=outs[d], send_sem=send.at[d], recv_sem=recv.at[d],
        device_id=(jnp.clip(me_w + sign * dw, 0, nw - 1), jnp.clip(me_n + sign * dn, 0, nn - 1)),
        device_id_type=pl.DeviceIdType.MESH)


def halo_start(ins, outs, send, recv, me_w, me_n, nw, nn):
    for d, (dw, dn) in enumerate(DIRS):
        @pl.when(inside(me_w, me_n, dw, dn, nw, nn))
        def _():
            halo_copy(ins, outs, send, recv, d, 1, me_w, me_n, nw, nn).start()


def halo_finish(ins, outs, send, recv, me_w, me_n, nw, nn):
    for d, (dw, dn) in enumerate(DIRS):
        src_ok = inside(me_w, me_n, -dw, -dn, nw, nn)

        @pl.when(src_ok)
        def _():
            halo_copy(ins, outs, send, recv, d, -1, me_w, me_n, nw, nn).wait_recv()

        @pl.when(jnp.logical_not(src_ok))
        def _():
            outs[d][...] = jnp.zeros(outs[d].shape, outs[d].dtype)

    for d, (dw, dn) in enumerate(DIRS):
        @pl.when(inside(me_w, me_n, dw, dn, nw, nn))
        def _():
            halo_copy(ins, outs, send, recv, d, 1, me_w, me_n, nw, nn).wait_send()


def shift_pairs(dw, dn, nw, nn):
    pairs = []
    for w in range(nw):
        for n in range(nn):
            tw, tn = w + dw, n + dn
            if 0 <= tw < nw and 0 <= tn < nn:
                pairs.append((w * nn + n, tw * nn + tn))
    return pairs


def exchange(pieces, dw, dn, nw, nn):
    flat = jnp.concatenate([p.reshape(-1) for p in pieces])
    got = lax.ppermute(flat, ("wide", "narrow"), shift_pairs(dw, dn, nw, nn))
    out, at = [], 0
    for p in pieces:
        out.append(got[at : at + p.size].reshape(p.shape))
        at += p.size
    return out


def stencil_kernel(nw, nn, total_cells, *refs):
    nd = len(DIRS)
    det_ref, cm_ref, m_ref = refs[:3]
    sends = refs[3:3 + nd]
    g_ref, h_ref, out_ref, sq_ref, r0, r1, r2, ss_ref, part1, part2, q1, q2, s1, p1, s2, p2 = \
        refs[3 + nd:19 + nd]
    halos = refs[19 + nd:19 + 2 * nd]
    hs, hr = refs[19 + 2 * nd:]
    top_ref, bot_ref, left_ref, right_ref, tl_ref, tr_ref, bl_ref, br_ref = halos
    i = pl.program_id(0)
    me_w = lax.axis_index("wide")
    me_n = lax.axis_index("narrow")
    mesh_id = pl.DeviceIdType.MESH
    barrier = pltpu.get_barrier_semaphore()
    cx = det_ref.shape[0]
    width = g_ref.shape[1]
    ext_rows = g_ref.shape[0]
    cy = det_ref.shape[1]

    def c0_row(x):
        s = x % RING
        zero = jnp.zeros((width, det_ref.shape[2]), jnp.float32)

        @pl.when(x < HALO)
        def _():
            j = jnp.minimum(x, HALO - 1)
            r0[s] = zero
            r0[s, LPAD - HALO:LPAD] = tl_ref[j]
            r0[s, LPAD:LPAD + cy] = top_ref[j]
            r0[s, LPAD + cy:LPAD + cy + HALO] = tr_ref[j]

        @pl.when(x >= HALO + cx)
        def _():
            j = jnp.clip(x - HALO - cx, 0, HALO - 1)
            r0[s] = zero
            r0[s, LPAD - HALO:LPAD] = bl_ref[j]
            r0[s, LPAD:LPAD + cy] = bot_ref[j]
            r0[s, LPAD + cy:LPAD + cy + HALO] = br_ref[j]

        @pl.when(jnp.logical_and(x >= HALO, x < HALO + cx))
        def _():
            b = jnp.clip(x - HALO, 0, cx - 1)
            t = b // TS
            r0[s, 0:LPAD] = zero[0:LPAD]
            for p in range(HALO):
                r0[s, pl.ds(LPAD - HALO + p, 1)] = left_ref[p, pl.ds(b, 1)]
            r0[s, LPAD:LPAD + cy] = cm_ref[t] + m_ref[t] * det_ref[b].astype(jnp.float32)
            r0[s, LPAD + cy:width] = zero[0:width - LPAD - cy]
            for p in range(HALO):
                r0[s, pl.ds(LPAD + cy + p, 1)] = right_ref[p, pl.ds(b, 1)]

    def apply_b(src, x):
        v = src[x % RING]
        nb = src[(x + 1) % RING] + src[(x + RING - 1) % RING]
        nb = nb + pltpu.roll(v, width - 1, 0) + pltpu.roll(v, 1, 0)
        return g_ref[x] * v - h_ref[(x + TS - HALO) // TS] * nb

    def c1_row(x):
        r1[x % RING] = apply_b(r0, x)

    def c2_row(x):
        r2[x % RING] = 2.0 * apply_b(r1, x) - r0[x % RING]

    def c3_row(x):
        c3 = 2.0 * apply_b(r2, x) - r1[x % RING]
        c3 = c3[LPAD:LPAD + cy]
        out_ref[x - HALO - ROWS * i] = c3
        sq = c3 * c3
        ss_ref[...] += jnp.sum(sq.reshape(cy // 8, 8, sq.shape[-1]), axis=0)

    def rows(fn, lo, n):
        def body(k, carry):
            fn(lo + k)
            return carry
        lax.fori_loop(0, n, body, 0)

    @pl.when(i == 0)
    def _():
        for k in range(1, nn):
            pl.semaphore_signal(barrier, inc=1, device_id=(me_w, (me_n + k) % nn), device_id_type=mesh_id)
        for k in range(1, nw):
            pl.semaphore_signal(barrier, inc=1, device_id=((me_w + k) % nw, me_n), device_id_type=mesh_id)
        diag = signal_others(barrier, me_w, me_n, nw, nn, DIAGONALS)
        pl.semaphore_wait(barrier, nn - 1 + nw - 1 + diag)
        halo_start(sends, halos, hs, hr, me_w, me_n, nw, nn)
        halo_finish(sends, halos, hs, hr, me_w, me_n, nw, nn)
        ss_ref[...] = jnp.zeros_like(ss_ref)
        rows(c0_row, 0, 2 * HALO)
        rows(c1_row, 1, 2 * HALO - 2)
        rows(c2_row, 2, 2 * HALO - 4)

    base = ROWS * i
    rows(c0_row, base + 2 * HALO, ROWS)
    rows(c1_row, base + 2 * HALO - 1, ROWS)
    rows(c2_row, base + 2 * HALO - 2, ROWS)
    rows(c3_row, base + HALO, ROWS)

    @pl.when(i == pl.num_programs(0) - 1)
    def _():
        part1[...] = jnp.sum(ss_ref[...], axis=0, keepdims=True)
        part2[...] = exchange_sum(part1, q1, s1, p1, me_n, nn, lambda j: (me_w, j))
        squares = exchange_sum(part2, q2, s2, p2, me_w, nw, lambda j: (j, me_n))
        sq_ref[...] = 1.0 / jnp.sqrt(squares / total_cells + EPSILON)


def exchange_sum(src, slots, send, recv, me, n, peer_of):
    mesh_id = pl.DeviceIdType.MESH
    copies = []
    for k in range(1, n):
        c = pltpu.make_async_remote_copy(
            src_ref=src, dst_ref=slots.at[me], send_sem=send.at[k], recv_sem=recv.at[me],
            device_id=peer_of((me + k) % n), device_id_type=mesh_id)
        c.start()
        copies.append(c)
    slots[me] = src[...]
    for k in range(1, n):
        other = (me + k) % n
        pltpu.make_async_remote_copy(
            src_ref=src, dst_ref=slots.at[other], send_sem=send.at[k], recv_sem=recv.at[other],
            device_id=peer_of(other), device_id_type=mesh_id).wait_recv()
    for c in copies:
        c.wait_send()
    return jnp.sum(slots[...], axis=0)


def run_stencil(det, cm, m, sends, g, h, nw, nn, total_cells):
    cx, cy, k = det.shape
    width = g.shape[1]
    steps = cx // ROWS
    vmem = pl.BlockSpec(memory_space=pltpu.VMEM)
    ops = cx * cy * k * 3 * 12
    return pl.pallas_call(
        functools.partial(stencil_kernel, nw, nn, float(total_cells)),
        grid=(steps,),
        in_specs=[vmem] * (5 + len(sends)),
        out_specs=[
            pl.BlockSpec((ROWS, cy, k), lambda i: (i, 0, 0)),
            pl.BlockSpec((1, k), lambda i: (0, 0)),
        ],
        out_shape=[
            jax.ShapeDtypeStruct((cx, cy, k), jnp.float32),
            jax.ShapeDtypeStruct((1, k), jnp.float32),
        ],
        scratch_shapes=[pltpu.VMEM((RING, width, k), jnp.float32) for _ in range(3)] + [
            pltpu.VMEM((8, k), jnp.float32),
            pltpu.VMEM((1, k), jnp.float32),
            pltpu.VMEM((1, k), jnp.float32),
            pltpu.VMEM((nn, 1, k), jnp.float32),
            pltpu.VMEM((nw, 1, k), jnp.float32),
            pltpu.SemaphoreType.DMA((nn,)),
            pltpu.SemaphoreType.DMA((nn,)),
            pltpu.SemaphoreType.DMA((nw,)),
            pltpu.SemaphoreType.DMA((nw,)),
        ] + [pltpu.VMEM(p.shape, p.dtype) for p in sends] + [
            pltpu.SemaphoreType.DMA((len(sends),)),
            pltpu.SemaphoreType.DMA((len(sends),)),
        ],
        compiler_params=pltpu.CompilerParams(
            dimension_semantics=("arbitrary",), vmem_limit_bytes=56 * 1024 * 1024,
            collective_id=0, has_side_effects=True,
        ),
        cost_estimate=pl.CostEstimate(
            flops=ops, transcendentals=0, bytes_accessed=det.size * 2 + cx * cy * k * 4 + g.size * 4
        ),
    )(det, cm, m, *sends, g, h)


def gather_kernel(nw, nn, cols, *refs):
    nd = len(DIRS)
    par_ref, ct_ref = refs[:2]
    gh_in = refs[2:2 + nd]
    o_ref = refs[2 + nd]
    gh_out = refs[3 + nd:3 + 2 * nd]
    pslots, stage, tslots, ps, pq, ts, tq, hs, hr = refs[3 + 2 * nd:]
    me_w = lax.axis_index("wide")
    me_n = lax.axis_index("narrow")
    mesh_id = pl.DeviceIdType.MESH
    barrier = pltpu.get_barrier_semaphore()
    for k in range(1, nn):
        pl.semaphore_signal(barrier, inc=1, device_id=(me_w, (me_n + k) % nn), device_id_type=mesh_id)
    extra = signal_others(barrier, me_w, me_n, nw, nn, VERTICAL)
    pl.semaphore_wait(barrier, nn - 1 + extra)
    halo_start(gh_in, gh_out, hs, hr, me_w, me_n, nw, nn)

    def par_copy(k, other, slot):
        return pltpu.make_async_remote_copy(
            src_ref=par_ref, dst_ref=pslots.at[slot], send_sem=ps.at[k], recv_sem=pq.at[slot],
            device_id=(me_w, other), device_id_type=mesh_id)

    sent = []
    for k in range(1, nn):
        c = par_copy(k, (me_n + k) % nn, me_n)
        c.start()
        sent.append(c)

    local_cells = ct_ref.shape[0]
    ncols = local_cells // cols

    def contribution(par):
        col = par % (ncols * nn)
        idx = (par // (ncols * nn)) * ncols + col % ncols
        idx = jnp.where(col // ncols == me_n, idx, -1)
        rows = lax.broadcasted_iota(jnp.int32, (local_cells, par.shape[-1]), 0)
        onehot = (rows == idx).astype(jnp.bfloat16)
        got = lax.dot_general(ct_ref[...], onehot, (((0,), (0,)), ((), ())),
                              preferred_element_type=jnp.float32)
        return got.astype(jnp.bfloat16)

    tslots[me_n] = contribution(par_ref[...])
    out_copies = []
    for k in range(1, nn):
        other = (me_n + k) % nn
        par_copy(k, other, other).wait_recv()
        stage[k] = contribution(pslots[other])
        c = pltpu.make_async_remote_copy(
            src_ref=stage.at[k], dst_ref=tslots.at[me_n], send_sem=ts.at[k], recv_sem=tq.at[me_n],
            device_id=(me_w, other), device_id_type=mesh_id)
        c.start()
        out_copies.append(c)
    for k in range(1, nn):
        other = (me_n + k) % nn
        pltpu.make_async_remote_copy(
            src_ref=stage.at[k], dst_ref=tslots.at[other], send_sem=ts.at[k], recv_sem=tq.at[other],
            device_id=(me_w, other), device_id_type=mesh_id).wait_recv()
    for c in sent + out_copies:
        c.wait_send()
    halo_finish(gh_in, gh_out, hs, hr, me_w, me_n, nw, nn)
    total = tslots[0].astype(jnp.float32)
    for j in range(1, nn):
        total = total + tslots[j].astype(jnp.float32)
    o_ref[...] = total


def gather_tiles(parents, coarse, gh_pieces, nw, nn):
    ccx, ccy, k = coarse.shape
    par = parents.reshape(1, -1)
    n_t = par.shape[-1]
    ct = coarse.reshape(ccx * ccy, k)
    vmem = pl.BlockSpec(memory_space=pltpu.VMEM)
    return pl.pallas_call(
        functools.partial(gather_kernel, nw, nn, ccx),
        in_specs=[vmem] * (2 + len(gh_pieces)),
        out_specs=[vmem] * (1 + len(gh_pieces)),
        out_shape=[jax.ShapeDtypeStruct((k, n_t), jnp.float32)]
        + [jax.ShapeDtypeStruct(p.shape, p.dtype) for p in gh_pieces],
        scratch_shapes=[
            pltpu.VMEM((nn, 1, n_t), jnp.int32),
            pltpu.VMEM((nn, k, n_t), jnp.bfloat16),
            pltpu.VMEM((nn, k, n_t), jnp.bfloat16),
            pltpu.SemaphoreType.DMA((nn,)),
            pltpu.SemaphoreType.DMA((nn,)),
            pltpu.SemaphoreType.DMA((nn,)),
            pltpu.SemaphoreType.DMA((nn,)),
            pltpu.SemaphoreType.DMA((len(gh_pieces),)),
            pltpu.SemaphoreType.DMA((len(gh_pieces),)),
        ],
        compiler_params=pltpu.CompilerParams(collective_id=1, has_side_effects=True),
    )(par, ct, *gh_pieces)


def scale_kernel(x_ref, s_ref, o_ref):
    o_ref[...] = x_ref[...] * s_ref[...]


def scale_rows(x, inv):
    cx, cy, k = x.shape
    return pl.pallas_call(
        scale_kernel,
        grid=(cx // SCALE_ROWS,),
        in_specs=[pl.BlockSpec((SCALE_ROWS, cy, k), lambda i: (i, 0, 0)), pl.BlockSpec((1, k), lambda i: (0, 0))],
        out_specs=pl.BlockSpec((SCALE_ROWS, cy, k), lambda i: (i, 0, 0)),
        out_shape=jax.ShapeDtypeStruct(x.shape, x.dtype),
        cost_estimate=pl.CostEstimate(flops=x.size, transcendentals=0, bytes_accessed=x.size * 8),
    )(x, inv)


def local(detail, coarse, diagonal, parents, tile_mask):
    tiles_x, tiles_y = parents.shape
    cells_x, cells_y, columns = detail.shape
    nw, nn = lax.axis_size("wide"), lax.axis_size("narrow")
    total_cells = cells_x * nw * cells_y * nn
    mask_float = tile_mask.astype(jnp.float32)

    h = HALO
    cell_mask = jnp.repeat(jnp.repeat(mask_float, TS, axis=0), TS, axis=1)
    g_own = (cell_mask * (4.0 + diagonal) - CENTER) / HALF_WIDTH
    h_own = cell_mask / HALF_WIDTH
    gh = jnp.stack([g_own, h_own])

    def edge(a, dw, dn, rows_axis, cols_axis):
        idx = [slice(None)] * a.ndim
        if dw == 1:
            idx[rows_axis] = slice(a.shape[rows_axis] - h, None)
        elif dw == -1:
            idx[rows_axis] = slice(0, h)
        if dn == 1:
            idx[cols_axis] = slice(a.shape[cols_axis] - h, None)
        elif dn == -1:
            idx[cols_axis] = slice(0, h)
        return a[tuple(idx)]

    gh_t = gh.transpose(0, 2, 1)
    gh_pieces = []
    for dw, dn in DIRS:
        gh_pieces.append(edge(gh_t, dn, dw, 1, 2) if dw == 0 else edge(gh, dw, dn, 1, 2))
    got = gather_tiles(parents, coarse, gh_pieces, nw, nn)
    tile_values = got[0].T
    hg = {dirn: got[1 + k] for k, dirn in enumerate(DIRS)}
    tv = tile_values.reshape(tiles_x, tiles_y, columns)

    m_rows = jnp.repeat(mask_float, TS, axis=1)
    m0 = jnp.broadcast_to(m_rows[:, :, None], (tiles_x, cells_y, columns))
    cm0 = m0 * jnp.repeat(tv, TS, axis=1)

    c0_top = cm0[0][None] + m0[0][None] * detail[:h].astype(jnp.float32)
    c0_bot = cm0[-1][None] + m0[-1][None] * detail[-h:].astype(jnp.float32)
    cm_rep = jnp.repeat(cm0, TS, axis=0)
    m_rep = jnp.repeat(m0, TS, axis=0)
    c0_left = cm_rep[:, :h] + m_rep[:, :h] * detail[:, :h].astype(jnp.float32)
    c0_right = cm_rep[:, -h:] + m_rep[:, -h:] * detail[:, -h:].astype(jnp.float32)
    c0_pieces = {
        (1, 0): c0_bot, (-1, 0): c0_top,
        (0, 1): c0_right.transpose(1, 0, 2), (0, -1): c0_left.transpose(1, 0, 2),
        (1, 1): c0_bot[:, -h:], (1, -1): c0_bot[:, :h], (-1, 1): c0_top[:, -h:], (-1, -1): c0_top[:, :h],
    }
    sends = [c0_pieces[dirn] for dirn in DIRS]

    rpad = LPAD - h
    z3 = jnp.zeros((2, h, rpad), jnp.float32)
    zc = jnp.zeros((2, cells_x, rpad), jnp.float32)
    gh_ext = jnp.concatenate(
        [
            jnp.concatenate([z3, hg[(1, 1)], hg[(1, 0)], hg[(1, -1)], z3], axis=2),
            jnp.concatenate([zc.transpose(0, 2, 1), hg[(0, 1)], gh_t, hg[(0, -1)], zc.transpose(0, 2, 1)],
                            axis=1).transpose(0, 2, 1),
            jnp.concatenate([z3, hg[(-1, 1)], hg[(-1, 0)], hg[(-1, -1)], z3], axis=2),
        ],
        axis=1,
    )
    width = cells_y + 2 * LPAD
    g_b = jnp.broadcast_to(gh_ext[0][:, :, None], (cells_x + 2 * h, width, columns))
    h_rows = gh_ext[1][jnp.array([0] + [h + TS * t for t in range(tiles_x)] + [h + cells_x])]
    h_b = jnp.broadcast_to(h_rows[:, :, None], (tiles_x + 2, width, columns))

    cheb_three, inv = run_stencil(detail, cm0, m0, sends, g_b, h_b, nw, nn, total_cells)
    return scale_rows(cheb_three, inv)


def solution(mesh):
    in_specs = (
        P("wide", "narrow", None),
        P("wide", "narrow", None),
        P("wide", "narrow"),
        P("wide", "narrow"),
        P("wide", "narrow"),
    )
    out_specs = P("wide", "narrow", None)
    return jax.shard_map(local, mesh=mesh, in_specs=in_specs, out_specs=out_specs, check_vma=False)
```

```python
import functools

import jax
import jax.numpy as jnp
from jax import lax
from jax.experimental import pallas as pl
from jax.experimental.pallas import tpu as pltpu
from jax.sharding import PartitionSpec as P

TS = 8
CENTER = 7.5
HALF_WIDTH = 4.5
EPSILON = 1e-06

HALO = 3
LPAD = 8
RING = 16
ROWS = 8
SCALE_ROWS = 64
DIRS = ((1, 0), (-1, 0), (0, 1), (0, -1), (1, 1), (1, -1), (-1, 1), (-1, -1))
DIAGONALS = DIRS[4:]
VERTICAL = ((1, 0), (-1, 0)) + DIAGONALS


def inside(me_w, me_n, dw, dn, nw, nn):
    w, n = me_w + dw, me_n + dn
    return jnp.logical_and(jnp.logical_and(w >= 0, w < nw), jnp.logical_and(n >= 0, n < nn))


def signal_others(barrier, me_w, me_n, nw, nn, dirs):
    count = 0
    for dw, dn in dirs:
        ok = inside(me_w, me_n, dw, dn, nw, nn)

        @pl.when(ok)
        def _():
            pl.semaphore_signal(barrier, inc=1, device_id=(jnp.clip(me_w + dw, 0, nw - 1),
                                jnp.clip(me_n + dn, 0, nn - 1)), device_id_type=pl.DeviceIdType.MESH)
        count = count + ok.astype(jnp.int32)
    return count


def halo_copy(ins, outs, send, recv, d, sign, me_w, me_n, nw, nn):
    dw, dn = DIRS[d]
    return pltpu.make_async_remote_copy(
        src_ref=ins[d], dst_ref=outs[d], send_sem=send.at[d], recv_sem=recv.at[d],
        device_id=(jnp.clip(me_w + sign * dw, 0, nw - 1), jnp.clip(me_n + sign * dn, 0, nn - 1)),
        device_id_type=pl.DeviceIdType.MESH)


def halo_start(ins, outs, send, recv, me_w, me_n, nw, nn):
    for d, (dw, dn) in enumerate(DIRS):
        @pl.when(inside(me_w, me_n, dw, dn, nw, nn))
        def _():
            halo_copy(ins, outs, send, recv, d, 1, me_w, me_n, nw, nn).start()


def halo_finish(ins, outs, send, recv, me_w, me_n, nw, nn):
    for d, (dw, dn) in enumerate(DIRS):
        src_ok = inside(me_w, me_n, -dw, -dn, nw, nn)

        @pl.when(src_ok)
        def _():
            halo_copy(ins, outs, send, recv, d, -1, me_w, me_n, nw, nn).wait_recv()

        @pl.when(jnp.logical_not(src_ok))
        def _():
            outs[d][...] = jnp.zeros(outs[d].shape, outs[d].dtype)

    for d, (dw, dn) in enumerate(DIRS):
        @pl.when(inside(me_w, me_n, dw, dn, nw, nn))
        def _():
            halo_copy(ins, outs, send, recv, d, 1, me_w, me_n, nw, nn).wait_send()


def shift_pairs(dw, dn, nw, nn):
    pairs = []
    for w in range(nw):
        for n in range(nn):
            tw, tn = w + dw, n + dn
            if 0 <= tw < nw and 0 <= tn < nn:
                pairs.append((w * nn + n, tw * nn + tn))
    return pairs


def exchange(pieces, dw, dn, nw, nn):
    flat = jnp.concatenate([p.reshape(-1) for p in pieces])
    got = lax.ppermute(flat, ("wide", "narrow"), shift_pairs(dw, dn, nw, nn))
    out, at = [], 0
    for p in pieces:
        out.append(got[at : at + p.size].reshape(p.shape))
        at += p.size
    return out


def stencil_kernel(nw, nn, total_cells, *refs):
    nd = len(DIRS)
    det_ref, cm_ref = refs[:2]
    sends = refs[2:2 + nd]
    g_ref, h_ref, out_ref, sq_ref, r0, r1, r2, ss_ref, part1, part2, q1, q2, s1, p1, s2, p2 = \
        refs[2 + nd:18 + nd]
    halos = refs[18 + nd:18 + 2 * nd]
    hs, hr = refs[18 + 2 * nd:]
    top_ref, bot_ref, left_ref, right_ref, tl_ref, tr_ref, bl_ref, br_ref = halos
    i = pl.program_id(0)
    me_w = lax.axis_index("wide")
    me_n = lax.axis_index("narrow")
    mesh_id = pl.DeviceIdType.MESH
    barrier = pltpu.get_barrier_semaphore()
    cx = det_ref.shape[0]
    width = g_ref.shape[1]
    ext_rows = g_ref.shape[0]
    cy = det_ref.shape[1]

    def c0_row(x):
        s = x % RING
        zero = jnp.zeros((width, det_ref.shape[2]), jnp.float32)

        @pl.when(x < HALO)
        def _():
            j = jnp.minimum(x, HALO - 1)
            r0[s] = zero
            r0[s, LPAD - HALO:LPAD] = tl_ref[j]
            r0[s, LPAD:LPAD + cy] = top_ref[j]
            r0[s, LPAD + cy:LPAD + cy + HALO] = tr_ref[j]

        @pl.when(x >= HALO + cx)
        def _():
            j = jnp.clip(x - HALO - cx, 0, HALO - 1)
            r0[s] = zero
            r0[s, LPAD - HALO:LPAD] = bl_ref[j]
            r0[s, LPAD:LPAD + cy] = bot_ref[j]
            r0[s, LPAD + cy:LPAD + cy + HALO] = br_ref[j]

        @pl.when(jnp.logical_and(x >= HALO, x < HALO + cx))
        def _():
            b = jnp.clip(x - HALO, 0, cx - 1)
            t = b // TS
            r0[s, 0:LPAD] = zero[0:LPAD]
            for p in range(HALO):
                r0[s, pl.ds(LPAD - HALO + p, 1)] = left_ref[p, pl.ds(b, 1)]
            own = h_ref[t + 1, LPAD:LPAD + cy] > 0
            r0[s, LPAD:LPAD + cy] = cm_ref[t] + jnp.where(own, det_ref[b].astype(jnp.float32), 0.0)
            r0[s, LPAD + cy:width] = zero[0:width - LPAD - cy]
            for p in range(HALO):
                r0[s, pl.ds(LPAD + cy + p, 1)] = right_ref[p, pl.ds(b, 1)]

    def apply_b(src, x):
        v = src[x % RING]
        nb = src[(x + 1) % RING] + src[(x + RING - 1) % RING]
        nb = nb + pltpu.roll(v, width - 1, 0) + pltpu.roll(v, 1, 0)
        return g_ref[x] * v - h_ref[(x + TS - HALO) // TS] * nb

    def c1_row(x):
        r1[x % RING] = apply_b(r0, x)

    def c2_row(x):
        r2[x % RING] = 2.0 * apply_b(r1, x) - r0[x % RING]

    def c3_row(x):
        c3 = 2.0 * apply_b(r2, x) - r1[x % RING]
        c3 = c3[LPAD:LPAD + cy]
        out_ref[x - HALO - ROWS * i] = c3
        sq = c3 * c3
        ss_ref[...] += jnp.sum(sq.reshape(cy // 8, 8, sq.shape[-1]), axis=0)

    def rows(fn, lo, n):
        def body(k, carry):
            fn(lo + k)
            return carry
        lax.fori_loop(0, n, body, 0)

    @pl.when(i == 0)
    def _():
        for k in range(1, nn):
            pl.semaphore_signal(barrier, inc=1, device_id=(me_w, (me_n + k) % nn), device_id_type=mesh_id)
        for k in range(1, nw):
            pl.semaphore_signal(barrier, inc=1, device_id=((me_w + k) % nw, me_n), device_id_type=mesh_id)
        diag = signal_others(barrier, me_w, me_n, nw, nn, DIAGONALS)
        pl.semaphore_wait(barrier, nn - 1 + nw - 1 + diag)
        halo_start(sends, halos, hs, hr, me_w, me_n, nw, nn)
        halo_finish(sends, halos, hs, hr, me_w, me_n, nw, nn)
        ss_ref[...] = jnp.zeros_like(ss_ref)
        rows(c0_row, 0, 2 * HALO)
        rows(c1_row, 1, 2 * HALO - 2)
        rows(c2_row, 2, 2 * HALO - 4)

    base = ROWS * i
    rows(c0_row, base + 2 * HALO, ROWS)
    rows(c1_row, base + 2 * HALO - 1, ROWS)
    rows(c2_row, base + 2 * HALO - 2, ROWS)
    rows(c3_row, base + HALO, ROWS)

    @pl.when(i == pl.num_programs(0) - 1)
    def _():
        part1[...] = jnp.sum(ss_ref[...], axis=0, keepdims=True)
        part2[...] = exchange_sum(part1, q1, s1, p1, me_n, nn, lambda j: (me_w, j))
        squares = exchange_sum(part2, q2, s2, p2, me_w, nw, lambda j: (j, me_n))
        sq_ref[...] = 1.0 / jnp.sqrt(squares / total_cells + EPSILON)


def exchange_sum(src, slots, send, recv, me, n, peer_of):
    mesh_id = pl.DeviceIdType.MESH
    copies = []
    for k in range(1, n):
        c = pltpu.make_async_remote_copy(
            src_ref=src, dst_ref=slots.at[me], send_sem=send.at[k], recv_sem=recv.at[me],
            device_id=peer_of((me + k) % n), device_id_type=mesh_id)
        c.start()
        copies.append(c)
    slots[me] = src[...]
    for k in range(1, n):
        other = (me + k) % n
        pltpu.make_async_remote_copy(
            src_ref=src, dst_ref=slots.at[other], send_sem=send.at[k], recv_sem=recv.at[other],
            device_id=peer_of(other), device_id_type=mesh_id).wait_recv()
    for c in copies:
        c.wait_send()
    return jnp.sum(slots[...], axis=0)


def run_stencil(det, cm, sends, g, h, nw, nn, total_cells):
    cx, cy, k = det.shape
    width = g.shape[1]
    steps = cx // ROWS
    vmem = pl.BlockSpec(memory_space=pltpu.VMEM)
    ops = cx * cy * k * 3 * 12
    return pl.pallas_call(
        functools.partial(stencil_kernel, nw, nn, float(total_cells)),
        grid=(steps,),
        in_specs=[vmem] * (4 + len(sends)),
        out_specs=[
            pl.BlockSpec((ROWS, cy, k), lambda i: (i, 0, 0)),
            pl.BlockSpec((1, k), lambda i: (0, 0)),
        ],
        out_shape=[
            jax.ShapeDtypeStruct((cx, cy, k), jnp.float32),
            jax.ShapeDtypeStruct((1, k), jnp.float32),
        ],
        scratch_shapes=[pltpu.VMEM((RING, width, k), jnp.float32) for _ in range(3)] + [
            pltpu.VMEM((8, k), jnp.float32),
            pltpu.VMEM((1, k), jnp.float32),
            pltpu.VMEM((1, k), jnp.float32),
            pltpu.VMEM((nn, 1, k), jnp.float32),
            pltpu.VMEM((nw, 1, k), jnp.float32),
            pltpu.SemaphoreType.DMA((nn,)),
            pltpu.SemaphoreType.DMA((nn,)),
            pltpu.SemaphoreType.DMA((nw,)),
            pltpu.SemaphoreType.DMA((nw,)),
        ] + [pltpu.VMEM(p.shape, p.dtype) for p in sends] + [
            pltpu.SemaphoreType.DMA((len(sends),)),
            pltpu.SemaphoreType.DMA((len(sends),)),
        ],
        compiler_params=pltpu.CompilerParams(
            dimension_semantics=("arbitrary",), vmem_limit_bytes=56 * 1024 * 1024,
            collective_id=0, has_side_effects=True,
        ),
        cost_estimate=pl.CostEstimate(
            flops=ops, transcendentals=0, bytes_accessed=det.size * 2 + cx * cy * k * 4 + g.size * 4
        ),
    )(det, cm, *sends, g, h)


def gather_kernel(nw, nn, cols, *refs):
    nd = len(DIRS)
    par_ref, ct_ref = refs[:2]
    gh_in = refs[2:2 + nd]
    o_ref = refs[2 + nd]
    gh_out = refs[3 + nd:3 + 2 * nd]
    pslots, stage, tslots, ps, pq, ts, tq, hs, hr = refs[3 + 2 * nd:]
    me_w = lax.axis_index("wide")
    me_n = lax.axis_index("narrow")
    mesh_id = pl.DeviceIdType.MESH
    barrier = pltpu.get_barrier_semaphore()
    for k in range(1, nn):
        pl.semaphore_signal(barrier, inc=1, device_id=(me_w, (me_n + k) % nn), device_id_type=mesh_id)
    extra = signal_others(barrier, me_w, me_n, nw, nn, VERTICAL)
    pl.semaphore_wait(barrier, nn - 1 + extra)
    halo_start(gh_in, gh_out, hs, hr, me_w, me_n, nw, nn)

    def par_copy(k, other, slot):
        return pltpu.make_async_remote_copy(
            src_ref=par_ref, dst_ref=pslots.at[slot], send_sem=ps.at[k], recv_sem=pq.at[slot],
            device_id=(me_w, other), device_id_type=mesh_id)

    sent = []
    for k in range(1, nn):
        c = par_copy(k, (me_n + k) % nn, me_n)
        c.start()
        sent.append(c)

    local_cells = ct_ref.shape[0]
    ncols = local_cells // cols

    def contribution(par):
        col = par % (ncols * nn)
        idx = (par // (ncols * nn)) * ncols + col % ncols
        idx = jnp.where(col // ncols == me_n, idx, -1)
        rows = lax.broadcasted_iota(jnp.int32, (local_cells, par.shape[-1]), 0)
        onehot = (rows == idx).astype(jnp.bfloat16)
        got = lax.dot_general(ct_ref[...], onehot, (((0,), (0,)), ((), ())),
                              preferred_element_type=jnp.float32)
        return got.astype(jnp.bfloat16)

    tslots[me_n] = contribution(par_ref[...])
    out_copies = []
    for k in range(1, nn):
        other = (me_n + k) % nn
        par_copy(k, other, other).wait_recv()
        stage[k] = contribution(pslots[other])
        c = pltpu.make_async_remote_copy(
            src_ref=stage.at[k], dst_ref=tslots.at[me_n], send_sem=ts.at[k], recv_sem=tq.at[me_n],
            device_id=(me_w, other), device_id_type=mesh_id)
        c.start()
        out_copies.append(c)
    for k in range(1, nn):
        other = (me_n + k) % nn
        pltpu.make_async_remote_copy(
            src_ref=stage.at[k], dst_ref=tslots.at[other], send_sem=ts.at[k], recv_sem=tq.at[other],
            device_id=(me_w, other), device_id_type=mesh_id).wait_recv()
    for c in sent + out_copies:
        c.wait_send()
    halo_finish(gh_in, gh_out, hs, hr, me_w, me_n, nw, nn)
    total = tslots[0].astype(jnp.float32)
    for j in range(1, nn):
        total = total + tslots[j].astype(jnp.float32)
    o_ref[...] = total


def gather_tiles(parents, coarse, gh_pieces, nw, nn):
    ccx, ccy, k = coarse.shape
    par = parents.reshape(1, -1)
    n_t = par.shape[-1]
    ct = coarse.reshape(ccx * ccy, k)
    vmem = pl.BlockSpec(memory_space=pltpu.VMEM)
    return pl.pallas_call(
        functools.partial(gather_kernel, nw, nn, ccx),
        in_specs=[vmem] * (2 + len(gh_pieces)),
        out_specs=[vmem] * (1 + len(gh_pieces)),
        out_shape=[jax.ShapeDtypeStruct((k, n_t), jnp.float32)]
        + [jax.ShapeDtypeStruct(p.shape, p.dtype) for p in gh_pieces],
        scratch_shapes=[
            pltpu.VMEM((nn, 1, n_t), jnp.int32),
            pltpu.VMEM((nn, k, n_t), jnp.bfloat16),
            pltpu.VMEM((nn, k, n_t), jnp.bfloat16),
            pltpu.SemaphoreType.DMA((nn,)),
            pltpu.SemaphoreType.DMA((nn,)),
            pltpu.SemaphoreType.DMA((nn,)),
            pltpu.SemaphoreType.DMA((nn,)),
            pltpu.SemaphoreType.DMA((len(gh_pieces),)),
            pltpu.SemaphoreType.DMA((len(gh_pieces),)),
        ],
        compiler_params=pltpu.CompilerParams(collective_id=1, has_side_effects=True),
    )(par, ct, *gh_pieces)


def scale_kernel(x_ref, s_ref, o_ref):
    o_ref[...] = x_ref[...] * s_ref[...]


def scale_rows(x, inv):
    cx, cy, k = x.shape
    return pl.pallas_call(
        scale_kernel,
        grid=(cx // SCALE_ROWS,),
        in_specs=[pl.BlockSpec((SCALE_ROWS, cy, k), lambda i: (i, 0, 0)), pl.BlockSpec((1, k), lambda i: (0, 0))],
        out_specs=pl.BlockSpec((SCALE_ROWS, cy, k), lambda i: (i, 0, 0)),
        out_shape=jax.ShapeDtypeStruct(x.shape, x.dtype),
        cost_estimate=pl.CostEstimate(flops=x.size, transcendentals=0, bytes_accessed=x.size * 8),
    )(x, inv)


def local(detail, coarse, diagonal, parents, tile_mask):
    tiles_x, tiles_y = parents.shape
    cells_x, cells_y, columns = detail.shape
    nw, nn = lax.axis_size("wide"), lax.axis_size("narrow")
    total_cells = cells_x * nw * cells_y * nn
    mask_float = tile_mask.astype(jnp.float32)

    h = HALO
    cell_mask = jnp.repeat(jnp.repeat(mask_float, TS, axis=0), TS, axis=1)
    g_own = (cell_mask * (4.0 + diagonal) - CENTER) / HALF_WIDTH
    h_own = cell_mask / HALF_WIDTH
    gh = jnp.stack([g_own, h_own])

    def edge(a, dw, dn, rows_axis, cols_axis):
        idx = [slice(None)] * a.ndim
        if dw == 1:
            idx[rows_axis] = slice(a.shape[rows_axis] - h, None)
        elif dw == -1:
            idx[rows_axis] = slice(0, h)
        if dn == 1:
            idx[cols_axis] = slice(a.shape[cols_axis] - h, None)
        elif dn == -1:
            idx[cols_axis] = slice(0, h)
        return a[tuple(idx)]

    gh_t = gh.transpose(0, 2, 1)
    gh_pieces = []
    for dw, dn in DIRS:
        gh_pieces.append(edge(gh_t, dn, dw, 1, 2) if dw == 0 else edge(gh, dw, dn, 1, 2))
    got = gather_tiles(parents, coarse, gh_pieces, nw, nn)
    tile_values = got[0].T
    hg = {dirn: got[1 + k] for k, dirn in enumerate(DIRS)}
    tv = tile_values.reshape(tiles_x, tiles_y, columns)

    m_rows = jnp.repeat(mask_float, TS, axis=1)
    m0 = jnp.broadcast_to(m_rows[:, :, None], (tiles_x, cells_y, columns))
    cm0 = m0 * jnp.repeat(tv, TS, axis=1)

    c0_top = cm0[0][None] + m0[0][None] * detail[:h].astype(jnp.float32)
    c0_bot = cm0[-1][None] + m0[-1][None] * detail[-h:].astype(jnp.float32)
    cm_rep = jnp.repeat(cm0, TS, axis=0)
    m_rep = jnp.repeat(m0, TS, axis=0)
    c0_left = cm_rep[:, :h] + m_rep[:, :h] * detail[:, :h].astype(jnp.float32)
    c0_right = cm_rep[:, -h:] + m_rep[:, -h:] * detail[:, -h:].astype(jnp.float32)
    c0_pieces = {
        (1, 0): c0_bot, (-1, 0): c0_top,
        (0, 1): c0_right.transpose(1, 0, 2), (0, -1): c0_left.transpose(1, 0, 2),
        (1, 1): c0_bot[:, -h:], (1, -1): c0_bot[:, :h], (-1, 1): c0_top[:, -h:], (-1, -1): c0_top[:, :h],
    }
    sends = [c0_pieces[dirn] for dirn in DIRS]

    rpad = LPAD - h
    z3 = jnp.zeros((2, h, rpad), jnp.float32)
    zc = jnp.zeros((2, cells_x, rpad), jnp.float32)
    gh_ext = jnp.concatenate(
        [
            jnp.concatenate([z3, hg[(1, 1)], hg[(1, 0)], hg[(1, -1)], z3], axis=2),
            jnp.concatenate([zc.transpose(0, 2, 1), hg[(0, 1)], gh_t, hg[(0, -1)], zc.transpose(0, 2, 1)],
                            axis=1).transpose(0, 2, 1),
            jnp.concatenate([z3, hg[(-1, 1)], hg[(-1, 0)], hg[(-1, -1)], z3], axis=2),
        ],
        axis=1,
    )
    width = cells_y + 2 * LPAD
    g_b = jnp.broadcast_to(gh_ext[0][:, :, None], (cells_x + 2 * h, width, columns))
    h_rows = gh_ext[1][jnp.array([0] + [h + TS * t for t in range(tiles_x)] + [h + cells_x])]
    h_b = jnp.broadcast_to(h_rows[:, :, None], (tiles_x + 2, width, columns))

    cheb_three, inv = run_stencil(detail, cm0, sends, g_b, h_b, nw, nn, total_cells)
    return scale_rows(cheb_three, inv)


def solution(mesh):
    in_specs = (
        P("wide", "narrow", None),
        P("wide", "narrow", None),
        P("wide", "narrow"),
        P("wide", "narrow"),
        P("wide", "narrow"),
    )
    out_specs = P("wide", "narrow", None)
    return jax.shard_map(local, mesh=mesh, in_specs=in_specs, out_specs=out_specs, check_vma=False)
```

```python
import functools

import jax
import jax.numpy as jnp
from jax import lax
from jax.experimental import pallas as pl
from jax.experimental.pallas import tpu as pltpu
from jax.sharding import PartitionSpec as P

TS = 8
CENTER = 7.5
HALF_WIDTH = 4.5
EPSILON = 1e-06

HALO = 3
LPAD = 8
RING = 32
ROWS = 16
SCALE_ROWS = 64
DIRS = ((1, 0), (-1, 0), (0, 1), (0, -1), (1, 1), (1, -1), (-1, 1), (-1, -1))
DIAGONALS = DIRS[4:]
VERTICAL = ((1, 0), (-1, 0)) + DIAGONALS


def inside(me_w, me_n, dw, dn, nw, nn):
    w, n = me_w + dw, me_n + dn
    return jnp.logical_and(jnp.logical_and(w >= 0, w < nw), jnp.logical_and(n >= 0, n < nn))


def signal_others(barrier, me_w, me_n, nw, nn, dirs):
    count = 0
    for dw, dn in dirs:
        ok = inside(me_w, me_n, dw, dn, nw, nn)

        @pl.when(ok)
        def _():
            pl.semaphore_signal(barrier, inc=1, device_id=(jnp.clip(me_w + dw, 0, nw - 1),
                                jnp.clip(me_n + dn, 0, nn - 1)), device_id_type=pl.DeviceIdType.MESH)
        count = count + ok.astype(jnp.int32)
    return count


def halo_copy(ins, outs, send, recv, d, sign, me_w, me_n, nw, nn):
    dw, dn = DIRS[d]
    return pltpu.make_async_remote_copy(
        src_ref=ins[d], dst_ref=outs[d], send_sem=send.at[d], recv_sem=recv.at[d],
        device_id=(jnp.clip(me_w + sign * dw, 0, nw - 1), jnp.clip(me_n + sign * dn, 0, nn - 1)),
        device_id_type=pl.DeviceIdType.MESH)


def halo_start(ins, outs, send, recv, me_w, me_n, nw, nn):
    for d, (dw, dn) in enumerate(DIRS):
        @pl.when(inside(me_w, me_n, dw, dn, nw, nn))
        def _():
            halo_copy(ins, outs, send, recv, d, 1, me_w, me_n, nw, nn).start()


def halo_finish(ins, outs, send, recv, me_w, me_n, nw, nn):
    for d, (dw, dn) in enumerate(DIRS):
        src_ok = inside(me_w, me_n, -dw, -dn, nw, nn)

        @pl.when(src_ok)
        def _():
            halo_copy(ins, outs, send, recv, d, -1, me_w, me_n, nw, nn).wait_recv()

        @pl.when(jnp.logical_not(src_ok))
        def _():
            outs[d][...] = jnp.zeros(outs[d].shape, outs[d].dtype)

    for d, (dw, dn) in enumerate(DIRS):
        @pl.when(inside(me_w, me_n, dw, dn, nw, nn))
        def _():
            halo_copy(ins, outs, send, recv, d, 1, me_w, me_n, nw, nn).wait_send()


def shift_pairs(dw, dn, nw, nn):
    pairs = []
    for w in range(nw):
        for n in range(nn):
            tw, tn = w + dw, n + dn
            if 0 <= tw < nw and 0 <= tn < nn:
                pairs.append((w * nn + n, tw * nn + tn))
    return pairs


def exchange(pieces, dw, dn, nw, nn):
    flat = jnp.concatenate([p.reshape(-1) for p in pieces])
    got = lax.ppermute(flat, ("wide", "narrow"), shift_pairs(dw, dn, nw, nn))
    out, at = [], 0
    for p in pieces:
        out.append(got[at : at + p.size].reshape(p.shape))
        at += p.size
    return out


def stencil_kernel(nw, nn, total_cells, *refs):
    nd = len(DIRS)
    det_ref, cm_ref = refs[:2]
    sends = refs[2:2 + nd]
    g_ref, h_ref, out_ref, sq_ref, r0, r1, r2, ss_ref, part1, part2, q1, q2, s1, p1, s2, p2 = \
        refs[2 + nd:18 + nd]
    halos = refs[18 + nd:18 + 2 * nd]
    hs, hr = refs[18 + 2 * nd:]
    top_ref, bot_ref, left_ref, right_ref, tl_ref, tr_ref, bl_ref, br_ref = halos
    i = pl.program_id(0)
    me_w = lax.axis_index("wide")
    me_n = lax.axis_index("narrow")
    mesh_id = pl.DeviceIdType.MESH
    barrier = pltpu.get_barrier_semaphore()
    cx = det_ref.shape[0]
    width = g_ref.shape[1]
    ext_rows = g_ref.shape[0]
    cy = det_ref.shape[1]

    def c0_row(x):
        s = x % RING
        zero = jnp.zeros((width, det_ref.shape[2]), jnp.float32)

        @pl.when(x < HALO)
        def _():
            j = jnp.minimum(x, HALO - 1)
            r0[s] = zero
            r0[s, LPAD - HALO:LPAD] = tl_ref[j]
            r0[s, LPAD:LPAD + cy] = top_ref[j]
            r0[s, LPAD + cy:LPAD + cy + HALO] = tr_ref[j]

        @pl.when(x >= HALO + cx)
        def _():
            j = jnp.clip(x - HALO - cx, 0, HALO - 1)
            r0[s] = zero
            r0[s, LPAD - HALO:LPAD] = bl_ref[j]
            r0[s, LPAD:LPAD + cy] = bot_ref[j]
            r0[s, LPAD + cy:LPAD + cy + HALO] = br_ref[j]

        @pl.when(jnp.logical_and(x >= HALO, x < HALO + cx))
        def _():
            b = jnp.clip(x - HALO, 0, cx - 1)
            t = b // TS
            r0[s, 0:LPAD] = zero[0:LPAD]
            for p in range(HALO):
                r0[s, pl.ds(LPAD - HALO + p, 1)] = left_ref[p, pl.ds(b, 1)]
            own = h_ref[t + 1, LPAD:LPAD + cy] > 0
            r0[s, LPAD:LPAD + cy] = cm_ref[t] + jnp.where(own, det_ref[b].astype(jnp.float32), 0.0)
            r0[s, LPAD + cy:width] = zero[0:width - LPAD - cy]
            for p in range(HALO):
                r0[s, pl.ds(LPAD + cy + p, 1)] = right_ref[p, pl.ds(b, 1)]

    def apply_b(src, x):
        v = src[x % RING]
        nb = src[(x + 1) % RING] + src[(x + RING - 1) % RING]
        nb = nb + pltpu.roll(v, width - 1, 0) + pltpu.roll(v, 1, 0)
        return g_ref[x] * v - h_ref[(x + TS - HALO) // TS] * nb

    def c1_row(x):
        r1[x % RING] = apply_b(r0, x)

    def c2_row(x):
        r2[x % RING] = 2.0 * apply_b(r1, x) - r0[x % RING]

    def c3_row(x):
        c3 = 2.0 * apply_b(r2, x) - r1[x % RING]
        c3 = c3[LPAD:LPAD + cy]
        out_ref[x - HALO - ROWS * i] = c3
        sq = c3 * c3
        ss_ref[...] += jnp.sum(sq.reshape(cy // 8, 8, sq.shape[-1]), axis=0)

    def rows(fn, lo, n):
        def body(k, carry):
            fn(lo + k)
            return carry
        lax.fori_loop(0, n, body, 0)

    @pl.when(i == 0)
    def _():
        for k in range(1, nn):
            pl.semaphore_signal(barrier, inc=1, device_id=(me_w, (me_n + k) % nn), device_id_type=mesh_id)
        for k in range(1, nw):
            pl.semaphore_signal(barrier, inc=1, device_id=((me_w + k) % nw, me_n), device_id_type=mesh_id)
        diag = signal_others(barrier, me_w, me_n, nw, nn, DIAGONALS)
        pl.semaphore_wait(barrier, nn - 1 + nw - 1 + diag)
        halo_start(sends, halos, hs, hr, me_w, me_n, nw, nn)
        halo_finish(sends, halos, hs, hr, me_w, me_n, nw, nn)
        ss_ref[...] = jnp.zeros_like(ss_ref)
        rows(c0_row, 0, 2 * HALO)
        rows(c1_row, 1, 2 * HALO - 2)
        rows(c2_row, 2, 2 * HALO - 4)

    base = ROWS * i
    rows(c0_row, base + 2 * HALO, ROWS)
    rows(c1_row, base + 2 * HALO - 1, ROWS)
    rows(c2_row, base + 2 * HALO - 2, ROWS)
    rows(c3_row, base + HALO, ROWS)

    @pl.when(i == pl.num_programs(0) - 1)
    def _():
        part1[...] = jnp.sum(ss_ref[...], axis=0, keepdims=True)
        part2[...] = exchange_sum(part1, q1, s1, p1, me_n, nn, lambda j: (me_w, j))
        squares = exchange_sum(part2, q2, s2, p2, me_w, nw, lambda j: (j, me_n))
        sq_ref[...] = 1.0 / jnp.sqrt(squares / total_cells + EPSILON)


def exchange_sum(src, slots, send, recv, me, n, peer_of):
    mesh_id = pl.DeviceIdType.MESH
    copies = []
    for k in range(1, n):
        c = pltpu.make_async_remote_copy(
            src_ref=src, dst_ref=slots.at[me], send_sem=send.at[k], recv_sem=recv.at[me],
            device_id=peer_of((me + k) % n), device_id_type=mesh_id)
        c.start()
        copies.append(c)
    slots[me] = src[...]
    for k in range(1, n):
        other = (me + k) % n
        pltpu.make_async_remote_copy(
            src_ref=src, dst_ref=slots.at[other], send_sem=send.at[k], recv_sem=recv.at[other],
            device_id=peer_of(other), device_id_type=mesh_id).wait_recv()
    for c in copies:
        c.wait_send()
    return jnp.sum(slots[...], axis=0)


def run_stencil(det, cm, sends, g, h, nw, nn, total_cells):
    cx, cy, k = det.shape
    width = g.shape[1]
    steps = cx // ROWS
    vmem = pl.BlockSpec(memory_space=pltpu.VMEM)
    ops = cx * cy * k * 3 * 12
    return pl.pallas_call(
        functools.partial(stencil_kernel, nw, nn, float(total_cells)),
        grid=(steps,),
        in_specs=[vmem] * (4 + len(sends)),
        out_specs=[
            pl.BlockSpec((ROWS, cy, k), lambda i: (i, 0, 0)),
            pl.BlockSpec((1, k), lambda i: (0, 0)),
        ],
        out_shape=[
            jax.ShapeDtypeStruct((cx, cy, k), jnp.float32),
            jax.ShapeDtypeStruct((1, k), jnp.float32),
        ],
        scratch_shapes=[pltpu.VMEM((RING, width, k), jnp.float32) for _ in range(3)] + [
            pltpu.VMEM((8, k), jnp.float32),
            pltpu.VMEM((1, k), jnp.float32),
            pltpu.VMEM((1, k), jnp.float32),
            pltpu.VMEM((nn, 1, k), jnp.float32),
            pltpu.VMEM((nw, 1, k), jnp.float32),
            pltpu.SemaphoreType.DMA((nn,)),
            pltpu.SemaphoreType.DMA((nn,)),
            pltpu.SemaphoreType.DMA((nw,)),
            pltpu.SemaphoreType.DMA((nw,)),
        ] + [pltpu.VMEM(p.shape, p.dtype) for p in sends] + [
            pltpu.SemaphoreType.DMA((len(sends),)),
            pltpu.SemaphoreType.DMA((len(sends),)),
        ],
        compiler_params=pltpu.CompilerParams(
            dimension_semantics=("arbitrary",), vmem_limit_bytes=56 * 1024 * 1024,
            collective_id=0, has_side_effects=True,
        ),
        cost_estimate=pl.CostEstimate(
            flops=ops, transcendentals=0, bytes_accessed=det.size * 2 + cx * cy * k * 4 + g.size * 4
        ),
    )(det, cm, *sends, g, h)


def gather_kernel(nw, nn, cols, *refs):
    nd = len(DIRS)
    par_ref, ct_ref = refs[:2]
    gh_in = refs[2:2 + nd]
    o_ref = refs[2 + nd]
    gh_out = refs[3 + nd:3 + 2 * nd]
    pslots, stage, tslots, ps, pq, ts, tq, hs, hr = refs[3 + 2 * nd:]
    me_w = lax.axis_index("wide")
    me_n = lax.axis_index("narrow")
    mesh_id = pl.DeviceIdType.MESH
    barrier = pltpu.get_barrier_semaphore()
    for k in range(1, nn):
        pl.semaphore_signal(barrier, inc=1, device_id=(me_w, (me_n + k) % nn), device_id_type=mesh_id)
    extra = signal_others(barrier, me_w, me_n, nw, nn, VERTICAL)
    pl.semaphore_wait(barrier, nn - 1 + extra)
    halo_start(gh_in, gh_out, hs, hr, me_w, me_n, nw, nn)

    def par_copy(k, other, slot):
        return pltpu.make_async_remote_copy(
            src_ref=par_ref, dst_ref=pslots.at[slot], send_sem=ps.at[k], recv_sem=pq.at[slot],
            device_id=(me_w, other), device_id_type=mesh_id)

    sent = []
    for k in range(1, nn):
        c = par_copy(k, (me_n + k) % nn, me_n)
        c.start()
        sent.append(c)

    local_cells = ct_ref.shape[0]
    ncols = local_cells // cols

    def contribution(par):
        col = par % (ncols * nn)
        idx = (par // (ncols * nn)) * ncols + col % ncols
        idx = jnp.where(col // ncols == me_n, idx, -1)
        rows = lax.broadcasted_iota(jnp.int32, (local_cells, par.shape[-1]), 0)
        onehot = (rows == idx).astype(jnp.bfloat16)
        got = lax.dot_general(ct_ref[...], onehot, (((0,), (0,)), ((), ())),
                              preferred_element_type=jnp.float32)
        return got.astype(jnp.bfloat16)

    tslots[me_n] = contribution(par_ref[...])
    out_copies = []
    for k in range(1, nn):
        other = (me_n + k) % nn
        par_copy(k, other, other).wait_recv()
        stage[k] = contribution(pslots[other])
        c = pltpu.make_async_remote_copy(
            src_ref=stage.at[k], dst_ref=tslots.at[me_n], send_sem=ts.at[k], recv_sem=tq.at[me_n],
            device_id=(me_w, other), device_id_type=mesh_id)
        c.start()
        out_copies.append(c)
    for k in range(1, nn):
        other = (me_n + k) % nn
        pltpu.make_async_remote_copy(
            src_ref=stage.at[k], dst_ref=tslots.at[other], send_sem=ts.at[k], recv_sem=tq.at[other],
            device_id=(me_w, other), device_id_type=mesh_id).wait_recv()
    for c in sent + out_copies:
        c.wait_send()
    halo_finish(gh_in, gh_out, hs, hr, me_w, me_n, nw, nn)
    total = tslots[0].astype(jnp.float32)
    for j in range(1, nn):
        total = total + tslots[j].astype(jnp.float32)
    o_ref[...] = total


def gather_tiles(parents, coarse, gh_pieces, nw, nn):
    ccx, ccy, k = coarse.shape
    par = parents.reshape(1, -1)
    n_t = par.shape[-1]
    ct = coarse.reshape(ccx * ccy, k)
    vmem = pl.BlockSpec(memory_space=pltpu.VMEM)
    return pl.pallas_call(
        functools.partial(gather_kernel, nw, nn, ccx),
        in_specs=[vmem] * (2 + len(gh_pieces)),
        out_specs=[vmem] * (1 + len(gh_pieces)),
        out_shape=[jax.ShapeDtypeStruct((k, n_t), jnp.float32)]
        + [jax.ShapeDtypeStruct(p.shape, p.dtype) for p in gh_pieces],
        scratch_shapes=[
            pltpu.VMEM((nn, 1, n_t), jnp.int32),
            pltpu.VMEM((nn, k, n_t), jnp.bfloat16),
            pltpu.VMEM((nn, k, n_t), jnp.bfloat16),
            pltpu.SemaphoreType.DMA((nn,)),
            pltpu.SemaphoreType.DMA((nn,)),
            pltpu.SemaphoreType.DMA((nn,)),
            pltpu.SemaphoreType.DMA((nn,)),
            pltpu.SemaphoreType.DMA((len(gh_pieces),)),
            pltpu.SemaphoreType.DMA((len(gh_pieces),)),
        ],
        compiler_params=pltpu.CompilerParams(collective_id=1, has_side_effects=True),
    )(par, ct, *gh_pieces)


def scale_kernel(x_ref, s_ref, o_ref):
    o_ref[...] = x_ref[...] * s_ref[...]


def scale_rows(x, inv):
    cx, cy, k = x.shape
    return pl.pallas_call(
        scale_kernel,
        grid=(cx // SCALE_ROWS,),
        in_specs=[pl.BlockSpec((SCALE_ROWS, cy, k), lambda i: (i, 0, 0)), pl.BlockSpec((1, k), lambda i: (0, 0))],
        out_specs=pl.BlockSpec((SCALE_ROWS, cy, k), lambda i: (i, 0, 0)),
        out_shape=jax.ShapeDtypeStruct(x.shape, x.dtype),
        cost_estimate=pl.CostEstimate(flops=x.size, transcendentals=0, bytes_accessed=x.size * 8),
    )(x, inv)


def local(detail, coarse, diagonal, parents, tile_mask):
    tiles_x, tiles_y = parents.shape
    cells_x, cells_y, columns = detail.shape
    nw, nn = lax.axis_size("wide"), lax.axis_size("narrow")
    total_cells = cells_x * nw * cells_y * nn
    mask_float = tile_mask.astype(jnp.float32)

    h = HALO
    cell_mask = jnp.repeat(jnp.repeat(mask_float, TS, axis=0), TS, axis=1)
    g_own = (cell_mask * (4.0 + diagonal) - CENTER) / HALF_WIDTH
    h_own = cell_mask / HALF_WIDTH
    gh = jnp.stack([g_own, h_own])

    def edge(a, dw, dn, rows_axis, cols_axis):
        idx = [slice(None)] * a.ndim
        if dw == 1:
            idx[rows_axis] = slice(a.shape[rows_axis] - h, None)
        elif dw == -1:
            idx[rows_axis] = slice(0, h)
        if dn == 1:
            idx[cols_axis] = slice(a.shape[cols_axis] - h, None)
        elif dn == -1:
            idx[cols_axis] = slice(0, h)
        return a[tuple(idx)]

    gh_t = gh.transpose(0, 2, 1)
    gh_pieces = []
    for dw, dn in DIRS:
        gh_pieces.append(edge(gh_t, dn, dw, 1, 2) if dw == 0 else edge(gh, dw, dn, 1, 2))
    got = gather_tiles(parents, coarse, gh_pieces, nw, nn)
    tile_values = got[0].T
    hg = {dirn: got[1 + k] for k, dirn in enumerate(DIRS)}
    tv = tile_values.reshape(tiles_x, tiles_y, columns)

    m_rows = jnp.repeat(mask_float, TS, axis=1)
    m0 = jnp.broadcast_to(m_rows[:, :, None], (tiles_x, cells_y, columns))
    cm0 = m0 * jnp.repeat(tv, TS, axis=1)

    c0_top = cm0[0][None] + m0[0][None] * detail[:h].astype(jnp.float32)
    c0_bot = cm0[-1][None] + m0[-1][None] * detail[-h:].astype(jnp.float32)
    cm_rep = jnp.repeat(cm0, TS, axis=0)
    m_rep = jnp.repeat(m0, TS, axis=0)
    c0_left = cm_rep[:, :h] + m_rep[:, :h] * detail[:, :h].astype(jnp.float32)
    c0_right = cm_rep[:, -h:] + m_rep[:, -h:] * detail[:, -h:].astype(jnp.float32)
    c0_pieces = {
        (1, 0): c0_bot, (-1, 0): c0_top,
        (0, 1): c0_right.transpose(1, 0, 2), (0, -1): c0_left.transpose(1, 0, 2),
        (1, 1): c0_bot[:, -h:], (1, -1): c0_bot[:, :h], (-1, 1): c0_top[:, -h:], (-1, -1): c0_top[:, :h],
    }
    sends = [c0_pieces[dirn] for dirn in DIRS]

    rpad = LPAD - h
    z3 = jnp.zeros((2, h, rpad), jnp.float32)
    zc = jnp.zeros((2, cells_x, rpad), jnp.float32)
    gh_ext = jnp.concatenate(
        [
            jnp.concatenate([z3, hg[(1, 1)], hg[(1, 0)], hg[(1, -1)], z3], axis=2),
            jnp.concatenate([zc.transpose(0, 2, 1), hg[(0, 1)], gh_t, hg[(0, -1)], zc.transpose(0, 2, 1)],
                            axis=1).transpose(0, 2, 1),
            jnp.concatenate([z3, hg[(-1, 1)], hg[(-1, 0)], hg[(-1, -1)], z3], axis=2),
        ],
        axis=1,
    )
    width = cells_y + 2 * LPAD
    g_b = jnp.broadcast_to(gh_ext[0][:, :, None], (cells_x + 2 * h, width, columns))
    h_rows = gh_ext[1][jnp.array([0] + [h + TS * t for t in range(tiles_x)] + [h + cells_x])]
    h_b = jnp.broadcast_to(h_rows[:, :, None], (tiles_x + 2, width, columns))

    cheb_three, inv = run_stencil(detail, cm0, sends, g_b, h_b, nw, nn, total_cells)
    return scale_rows(cheb_three, inv)


def solution(mesh):
    in_specs = (
        P("wide", "narrow", None),
        P("wide", "narrow", None),
        P("wide", "narrow"),
        P("wide", "narrow"),
        P("wide", "narrow"),
    )
    out_specs = P("wide", "narrow", None)
    return jax.shard_map(local, mesh=mesh, in_specs=in_specs, out_specs=out_specs, check_vma=False)
```

```python
import functools

import jax
import jax.numpy as jnp
from jax import lax
from jax.experimental import pallas as pl
from jax.experimental.pallas import tpu as pltpu
from jax.sharding import PartitionSpec as P

TS = 8
CENTER = 7.5
HALF_WIDTH = 4.5
EPSILON = 1e-06

HALO = 3
LPAD = 8
RING = 32
ROWS = 16
SCALE_ROWS = 64
DIRS = ((1, 0), (-1, 0), (0, 1), (0, -1), (1, 1), (1, -1), (-1, 1), (-1, -1))
DIAGONALS = DIRS[4:]
VERTICAL = ((1, 0), (-1, 0)) + DIAGONALS


def inside(me_w, me_n, dw, dn, nw, nn):
    w, n = me_w + dw, me_n + dn
    return jnp.logical_and(jnp.logical_and(w >= 0, w < nw), jnp.logical_and(n >= 0, n < nn))


def signal_others(barrier, me_w, me_n, nw, nn, dirs):
    count = 0
    for dw, dn in dirs:
        ok = inside(me_w, me_n, dw, dn, nw, nn)

        @pl.when(ok)
        def _():
            pl.semaphore_signal(barrier, inc=1, device_id=(jnp.clip(me_w + dw, 0, nw - 1),
                                jnp.clip(me_n + dn, 0, nn - 1)), device_id_type=pl.DeviceIdType.MESH)
        count = count + ok.astype(jnp.int32)
    return count


def halo_copy(ins, outs, send, recv, d, sign, me_w, me_n, nw, nn):
    dw, dn = DIRS[d]
    return pltpu.make_async_remote_copy(
        src_ref=ins[d], dst_ref=outs[d], send_sem=send.at[d], recv_sem=recv.at[d],
        device_id=(jnp.clip(me_w + sign * dw, 0, nw - 1), jnp.clip(me_n + sign * dn, 0, nn - 1)),
        device_id_type=pl.DeviceIdType.MESH)


def halo_start(ins, outs, send, recv, me_w, me_n, nw, nn):
    for d, (dw, dn) in enumerate(DIRS):
        @pl.when(inside(me_w, me_n, dw, dn, nw, nn))
        def _():
            halo_copy(ins, outs, send, recv, d, 1, me_w, me_n, nw, nn).start()


def halo_finish(ins, outs, send, recv, me_w, me_n, nw, nn):
    for d, (dw, dn) in enumerate(DIRS):
        src_ok = inside(me_w, me_n, -dw, -dn, nw, nn)

        @pl.when(src_ok)
        def _():
            halo_copy(ins, outs, send, recv, d, -1, me_w, me_n, nw, nn).wait_recv()

        @pl.when(jnp.logical_not(src_ok))
        def _():
            outs[d][...] = jnp.zeros(outs[d].shape, outs[d].dtype)

    for d, (dw, dn) in enumerate(DIRS):
        @pl.when(inside(me_w, me_n, dw, dn, nw, nn))
        def _():
            halo_copy(ins, outs, send, recv, d, 1, me_w, me_n, nw, nn).wait_send()


def shift_pairs(dw, dn, nw, nn):
    pairs = []
    for w in range(nw):
        for n in range(nn):
            tw, tn = w + dw, n + dn
            if 0 <= tw < nw and 0 <= tn < nn:
                pairs.append((w * nn + n, tw * nn + tn))
    return pairs


def exchange(pieces, dw, dn, nw, nn):
    flat = jnp.concatenate([p.reshape(-1) for p in pieces])
    got = lax.ppermute(flat, ("wide", "narrow"), shift_pairs(dw, dn, nw, nn))
    out, at = [], 0
    for p in pieces:
        out.append(got[at : at + p.size].reshape(p.shape))
        at += p.size
    return out


def stencil_kernel(nw, nn, total_cells, *refs):
    nd = len(DIRS)
    det_ref, cm_ref = refs[:2]
    sends = refs[2:2 + nd]
    g_ref, h_ref, out_ref, sq_ref, r0, r1, r2, ss_ref, part1, part2, q1, q2, s1, p1, s2, p2 = \
        refs[2 + nd:18 + nd]
    halos = refs[18 + nd:18 + 2 * nd]
    hs, hr = refs[18 + 2 * nd:]
    top_ref, bot_ref, left_ref, right_ref, tl_ref, tr_ref, bl_ref, br_ref = halos
    i = pl.program_id(0)
    me_w = lax.axis_index("wide")
    me_n = lax.axis_index("narrow")
    mesh_id = pl.DeviceIdType.MESH
    barrier = pltpu.get_barrier_semaphore()
    cx = det_ref.shape[0]
    width = g_ref.shape[1]
    ext_rows = g_ref.shape[0]
    cy = det_ref.shape[1]

    def c0_row(x):
        s = x % RING
        zero = jnp.zeros((width, det_ref.shape[2]), jnp.float32)

        @pl.when(x < HALO)
        def _():
            j = jnp.minimum(x, HALO - 1)
            r0[s] = zero
            r0[s, LPAD - HALO:LPAD] = tl_ref[j]
            r0[s, LPAD:LPAD + cy] = top_ref[j]
            r0[s, LPAD + cy:LPAD + cy + HALO] = tr_ref[j]

        @pl.when(x >= HALO + cx)
        def _():
            j = jnp.clip(x - HALO - cx, 0, HALO - 1)
            r0[s] = zero
            r0[s, LPAD - HALO:LPAD] = bl_ref[j]
            r0[s, LPAD:LPAD + cy] = bot_ref[j]
            r0[s, LPAD + cy:LPAD + cy + HALO] = br_ref[j]

        @pl.when(jnp.logical_and(x >= HALO, x < HALO + cx))
        def _():
            b = jnp.clip(x - HALO, 0, cx - 1)
            t = b // TS
            r0[s, 0:LPAD] = zero[0:LPAD]
            for p in range(HALO):
                r0[s, pl.ds(LPAD - HALO + p, 1)] = left_ref[p, pl.ds(b, 1)]
            own = h_ref[t + 1, LPAD:LPAD + cy] > 0
            r0[s, LPAD:LPAD + cy] = cm_ref[t] + jnp.where(own, det_ref[b].astype(jnp.float32), 0.0)
            r0[s, LPAD + cy:width] = zero[0:width - LPAD - cy]
            for p in range(HALO):
                r0[s, pl.ds(LPAD + cy + p, 1)] = right_ref[p, pl.ds(b, 1)]

    def apply_b(src, x):
        v = src[x % RING]
        nb = src[(x + 1) % RING] + src[(x + RING - 1) % RING]
        nb = nb + pltpu.roll(v, width - 1, 0) + pltpu.roll(v, 1, 0)
        return g_ref[x] * v - h_ref[(x + TS - HALO) // TS] * nb

    def c1_row(x):
        r1[x % RING] = apply_b(r0, x)

    def c2_row(x):
        r2[x % RING] = 2.0 * apply_b(r1, x) - r0[x % RING]

    def c3_row(x):
        c3 = 2.0 * apply_b(r2, x) - r1[x % RING]
        c3 = c3[LPAD:LPAD + cy]
        out_ref[x - HALO - ROWS * i] = c3
        sq = c3 * c3
        ss_ref[...] += jnp.sum(sq.reshape(cy // 8, 8, sq.shape[-1]), axis=0)

    def rows(fn, lo, n):
        def body(k, carry):
            fn(lo + k)
            return carry
        lax.fori_loop(0, n, body, 0)

    @pl.when(i == 0)
    def _():
        for k in range(1, nn):
            pl.semaphore_signal(barrier, inc=1, device_id=(me_w, (me_n + k) % nn), device_id_type=mesh_id)
        for k in range(1, nw):
            pl.semaphore_signal(barrier, inc=1, device_id=((me_w + k) % nw, me_n), device_id_type=mesh_id)
        diag = signal_others(barrier, me_w, me_n, nw, nn, DIAGONALS)
        pl.semaphore_wait(barrier, nn - 1 + nw - 1 + diag)
        halo_start(sends, halos, hs, hr, me_w, me_n, nw, nn)
        halo_finish(sends, halos, hs, hr, me_w, me_n, nw, nn)
        ss_ref[...] = jnp.zeros_like(ss_ref)
        rows(c0_row, 0, 2 * HALO)
        rows(c1_row, 1, 2 * HALO - 2)
        rows(c2_row, 2, 2 * HALO - 4)

    base = ROWS * i
    rows(c0_row, base + 2 * HALO, ROWS)
    rows(c1_row, base + 2 * HALO - 1, ROWS)
    rows(c2_row, base + 2 * HALO - 2, ROWS)
    rows(c3_row, base + HALO, ROWS)

    @pl.when(i == pl.num_programs(0) - 1)
    def _():
        part1[...] = jnp.sum(ss_ref[...], axis=0, keepdims=True)
        part2[...] = exchange_sum(part1, q1, s1, p1, me_n, nn, lambda j: (me_w, j))
        squares = exchange_sum(part2, q2, s2, p2, me_w, nw, lambda j: (j, me_n))
        sq_ref[...] = 1.0 / jnp.sqrt(squares / total_cells + EPSILON)


def exchange_sum(src, slots, send, recv, me, n, peer_of):
    mesh_id = pl.DeviceIdType.MESH
    copies = []
    for k in range(1, n):
        c = pltpu.make_async_remote_copy(
            src_ref=src, dst_ref=slots.at[me], send_sem=send.at[k], recv_sem=recv.at[me],
            device_id=peer_of((me + k) % n), device_id_type=mesh_id)
        c.start()
        copies.append(c)
    slots[me] = src[...]
    for k in range(1, n):
        other = (me + k) % n
        pltpu.make_async_remote_copy(
            src_ref=src, dst_ref=slots.at[other], send_sem=send.at[k], recv_sem=recv.at[other],
            device_id=peer_of(other), device_id_type=mesh_id).wait_recv()
    for c in copies:
        c.wait_send()
    return jnp.sum(slots[...], axis=0)


def run_stencil(det, cm, sends, g, h, nw, nn, total_cells):
    cx, cy, k = det.shape
    width = g.shape[1]
    steps = cx // ROWS
    vmem = pl.BlockSpec(memory_space=pltpu.VMEM)
    ops = cx * cy * k * 3 * 12
    return pl.pallas_call(
        functools.partial(stencil_kernel, nw, nn, float(total_cells)),
        grid=(steps,),
        in_specs=[vmem] * (4 + len(sends)),
        out_specs=[
            pl.BlockSpec((ROWS, cy, k), lambda i: (i, 0, 0)),
            pl.BlockSpec((1, k), lambda i: (0, 0)),
        ],
        out_shape=[
            jax.ShapeDtypeStruct((cx, cy, k), jnp.float32),
            jax.ShapeDtypeStruct((1, k), jnp.float32),
        ],
        scratch_shapes=[pltpu.VMEM((RING, width, k), jnp.float32) for _ in range(3)] + [
            pltpu.VMEM((8, k), jnp.float32),
            pltpu.VMEM((1, k), jnp.float32),
            pltpu.VMEM((1, k), jnp.float32),
            pltpu.VMEM((nn, 1, k), jnp.float32),
            pltpu.VMEM((nw, 1, k), jnp.float32),
            pltpu.SemaphoreType.DMA((nn,)),
            pltpu.SemaphoreType.DMA((nn,)),
            pltpu.SemaphoreType.DMA((nw,)),
            pltpu.SemaphoreType.DMA((nw,)),
        ] + [pltpu.VMEM(p.shape, p.dtype) for p in sends] + [
            pltpu.SemaphoreType.DMA((len(sends),)),
            pltpu.SemaphoreType.DMA((len(sends),)),
        ],
        compiler_params=pltpu.CompilerParams(
            dimension_semantics=("arbitrary",), vmem_limit_bytes=56 * 1024 * 1024,
            collective_id=0, has_side_effects=True,
        ),
        cost_estimate=pl.CostEstimate(
            flops=ops, transcendentals=0, bytes_accessed=det.size * 2 + cx * cy * k * 4 + g.size * 4
        ),
    )(det, cm, *sends, g, h)


def gather_kernel(nw, nn, cols, *refs):
    nd = len(DIRS)
    par_ref, ct_ref = refs[:2]
    gh_in = refs[2:2 + nd]
    o_ref = refs[2 + nd]
    gh_out = refs[3 + nd:3 + 2 * nd]
    pslots, stage, tslots, ps, pq, ts, tq, hs, hr = refs[3 + 2 * nd:]
    me_w = lax.axis_index("wide")
    me_n = lax.axis_index("narrow")
    mesh_id = pl.DeviceIdType.MESH
    barrier = pltpu.get_barrier_semaphore()
    for k in range(1, nn):
        pl.semaphore_signal(barrier, inc=1, device_id=(me_w, (me_n + k) % nn), device_id_type=mesh_id)
    extra = signal_others(barrier, me_w, me_n, nw, nn, VERTICAL)
    pl.semaphore_wait(barrier, nn - 1 + extra)
    halo_start(gh_in, gh_out, hs, hr, me_w, me_n, nw, nn)

    def par_copy(k, other, slot):
        return pltpu.make_async_remote_copy(
            src_ref=par_ref, dst_ref=pslots.at[slot], send_sem=ps.at[k], recv_sem=pq.at[slot],
            device_id=(me_w, other), device_id_type=mesh_id)

    sent = []
    for k in range(1, nn):
        c = par_copy(k, (me_n + k) % nn, me_n)
        c.start()
        sent.append(c)

    local_cells = ct_ref.shape[0]
    ncols = local_cells // cols

    def contribution(par):
        col = par % (ncols * nn)
        idx = (par // (ncols * nn)) * ncols + col % ncols
        idx = jnp.where(col // ncols == me_n, idx, -1)
        rows = lax.broadcasted_iota(jnp.int32, (local_cells, par.shape[-1]), 0)
        onehot = (rows == idx).astype(jnp.bfloat16)
        got = lax.dot_general(ct_ref[...], onehot, (((0,), (0,)), ((), ())),
                              preferred_element_type=jnp.float32)
        return got.astype(jnp.bfloat16)

    tslots[me_n] = contribution(par_ref[...])
    out_copies = []
    for k in range(1, nn):
        other = (me_n + k) % nn
        par_copy(k, other, other).wait_recv()
        stage[k] = contribution(pslots[other])
        c = pltpu.make_async_remote_copy(
            src_ref=stage.at[k], dst_ref=tslots.at[me_n], send_sem=ts.at[k], recv_sem=tq.at[me_n],
            device_id=(me_w, other), device_id_type=mesh_id)
        c.start()
        out_copies.append(c)
    for k in range(1, nn):
        other = (me_n + k) % nn
        pltpu.make_async_remote_copy(
            src_ref=stage.at[k], dst_ref=tslots.at[other], send_sem=ts.at[k], recv_sem=tq.at[other],
            device_id=(me_w, other), device_id_type=mesh_id).wait_recv()
    for c in sent + out_copies:
        c.wait_send()
    halo_finish(gh_in, gh_out, hs, hr, me_w, me_n, nw, nn)
    total = tslots[0].astype(jnp.float32)
    for j in range(1, nn):
        total = total + tslots[j].astype(jnp.float32)
    o_ref[...] = total


def gather_tiles(parents, coarse, gh_pieces, nw, nn):
    ccx, ccy, k = coarse.shape
    par = parents.reshape(1, -1)
    n_t = par.shape[-1]
    ct = coarse.reshape(ccx * ccy, k)
    vmem = pl.BlockSpec(memory_space=pltpu.VMEM)
    return pl.pallas_call(
        functools.partial(gather_kernel, nw, nn, ccx),
        in_specs=[vmem] * (2 + len(gh_pieces)),
        out_specs=[vmem] * (1 + len(gh_pieces)),
        out_shape=[jax.ShapeDtypeStruct((k, n_t), jnp.float32)]
        + [jax.ShapeDtypeStruct(p.shape, p.dtype) for p in gh_pieces],
        scratch_shapes=[
            pltpu.VMEM((nn, 1, n_t), jnp.int32),
            pltpu.VMEM((nn, k, n_t), jnp.bfloat16),
            pltpu.VMEM((nn, k, n_t), jnp.bfloat16),
            pltpu.SemaphoreType.DMA((nn,)),
            pltpu.SemaphoreType.DMA((nn,)),
            pltpu.SemaphoreType.DMA((nn,)),
            pltpu.SemaphoreType.DMA((nn,)),
            pltpu.SemaphoreType.DMA((len(gh_pieces),)),
            pltpu.SemaphoreType.DMA((len(gh_pieces),)),
        ],
        compiler_params=pltpu.CompilerParams(collective_id=1, has_side_effects=True),
    )(par, ct, *gh_pieces)


def scale_kernel(x_ref, s_ref, o_ref):
    o_ref[...] = x_ref[...] * s_ref[...]


def scale_rows(x, inv):
    cx, cy, k = x.shape
    return pl.pallas_call(
        scale_kernel,
        grid=(cx // SCALE_ROWS,),
        in_specs=[pl.BlockSpec((SCALE_ROWS, cy, k), lambda i: (i, 0, 0)), pl.BlockSpec((1, k), lambda i: (0, 0))],
        out_specs=pl.BlockSpec((SCALE_ROWS, cy, k), lambda i: (i, 0, 0)),
        out_shape=jax.ShapeDtypeStruct(x.shape, x.dtype),
        cost_estimate=pl.CostEstimate(flops=x.size, transcendentals=0, bytes_accessed=x.size * 8),
    )(x, inv)


def local(detail, coarse, diagonal, parents, tile_mask):
    tiles_x, tiles_y = parents.shape
    cells_x, cells_y, columns = detail.shape
    nw, nn = lax.axis_size("wide"), lax.axis_size("narrow")
    total_cells = cells_x * nw * cells_y * nn
    mask_float = tile_mask.astype(jnp.float32)

    h = HALO
    cell_mask = jnp.repeat(jnp.repeat(mask_float, TS, axis=0), TS, axis=1)
    g_own = (cell_mask * (4.0 + diagonal) - CENTER) / HALF_WIDTH
    h_own = cell_mask / HALF_WIDTH
    gh = jnp.stack([g_own, h_own])

    def edge(a, dw, dn, rows_axis, cols_axis):
        idx = [slice(None)] * a.ndim
        if dw == 1:
            idx[rows_axis] = slice(a.shape[rows_axis] - h, None)
        elif dw == -1:
            idx[rows_axis] = slice(0, h)
        if dn == 1:
            idx[cols_axis] = slice(a.shape[cols_axis] - h, None)
        elif dn == -1:
            idx[cols_axis] = slice(0, h)
        return a[tuple(idx)]

    gh_t = gh.transpose(0, 2, 1)
    gh_pieces = []
    for dw, dn in DIRS:
        gh_pieces.append(edge(gh_t, dn, dw, 1, 2) if dw == 0 else edge(gh, dw, dn, 1, 2))
    got = gather_tiles(parents, coarse, gh_pieces, nw, nn)
    tile_values = got[0].T
    hg = {dirn: got[1 + k] for k, dirn in enumerate(DIRS)}
    tv = tile_values.reshape(tiles_x, tiles_y, columns)

    m_rows = jnp.repeat(mask_float, TS, axis=1)
    m0 = jnp.broadcast_to(m_rows[:, :, None], (tiles_x, cells_y, columns))
    cm0 = m0 * jnp.repeat(tv, TS, axis=1)

    c0_top = cm0[0][None] + m0[0][None] * detail[:h].astype(jnp.float32)
    c0_bot = cm0[-1][None] + m0[-1][None] * detail[-h:].astype(jnp.float32)
    cm_rep = jnp.repeat(cm0, TS, axis=0)
    m_rep = jnp.repeat(m0, TS, axis=0)
    c0_left = cm_rep[:, :h] + m_rep[:, :h] * detail[:, :h].astype(jnp.float32)
    c0_right = cm_rep[:, -h:] + m_rep[:, -h:] * detail[:, -h:].astype(jnp.float32)
    c0_pieces = {
        (1, 0): c0_bot, (-1, 0): c0_top,
        (0, 1): c0_right.transpose(1, 0, 2), (0, -1): c0_left.transpose(1, 0, 2),
        (1, 1): c0_bot[:, -h:], (1, -1): c0_bot[:, :h], (-1, 1): c0_top[:, -h:], (-1, -1): c0_top[:, :h],
    }
    sends = [c0_pieces[dirn] for dirn in DIRS]

    rpad = LPAD - h
    width = cells_y + 2 * LPAD
    zc = jnp.zeros((2, cells_x, rpad), jnp.float32)
    gh_ext = jnp.concatenate(
        [
            (jnp.pad(hg[(1, 1)], ((0, 0), (0, 0), (rpad, width - LPAD))) + jnp.pad(hg[(1, 0)], ((0, 0), (0, 0), (LPAD, LPAD))) + jnp.pad(hg[(1, -1)], ((0, 0), (0, 0), (LPAD + cells_y, rpad)))),
            jnp.concatenate([zc.transpose(0, 2, 1), hg[(0, 1)], gh_t, hg[(0, -1)], zc.transpose(0, 2, 1)],
                            axis=1).transpose(0, 2, 1),
            (jnp.pad(hg[(-1, 1)], ((0, 0), (0, 0), (rpad, width - LPAD))) + jnp.pad(hg[(-1, 0)], ((0, 0), (0, 0), (LPAD, LPAD))) + jnp.pad(hg[(-1, -1)], ((0, 0), (0, 0), (LPAD + cells_y, rpad)))),
        ],
        axis=1,
    )
    g_b = jnp.broadcast_to(gh_ext[0][:, :, None], (cells_x + 2 * h, width, columns))
    h_rows = jnp.concatenate(
        [gh_ext[1][0:1], gh_ext[1][h:h + cells_x:TS], gh_ext[1][h + cells_x:h + cells_x + 1]], axis=0)
    h_b = jnp.broadcast_to(h_rows[:, :, None], (tiles_x + 2, width, columns))

    cheb_three, inv = run_stencil(detail, cm0, sends, g_b, h_b, nw, nn, total_cells)
    return scale_rows(cheb_three, inv)


def solution(mesh):
    in_specs = (
        P("wide", "narrow", None),
        P("wide", "narrow", None),
        P("wide", "narrow"),
        P("wide", "narrow"),
        P("wide", "narrow"),
    )
    out_specs = P("wide", "narrow", None)
    return jax.shard_map(local, mesh=mesh, in_specs=in_specs, out_specs=out_specs, check_vma=False)
```

```python
import functools

import jax
import jax.numpy as jnp
from jax import lax
from jax.experimental import pallas as pl
from jax.experimental.pallas import tpu as pltpu
from jax.sharding import PartitionSpec as P

TS = 8
CENTER = 7.5
HALF_WIDTH = 4.5
EPSILON = 1e-06

HALO = 3
LPAD = 8
RING = 32
ROWS = 16
SCALE_ROWS = 64
DIRS = ((1, 0), (-1, 0), (0, 1), (0, -1), (1, 1), (1, -1), (-1, 1), (-1, -1))
DIAGONALS = DIRS[4:]
VERTICAL = ((1, 0), (-1, 0)) + DIAGONALS


def inside(me_w, me_n, dw, dn, nw, nn):
    w, n = me_w + dw, me_n + dn
    return jnp.logical_and(jnp.logical_and(w >= 0, w < nw), jnp.logical_and(n >= 0, n < nn))


def signal_others(barrier, me_w, me_n, nw, nn, dirs):
    count = 0
    for dw, dn in dirs:
        ok = inside(me_w, me_n, dw, dn, nw, nn)

        @pl.when(ok)
        def _():
            pl.semaphore_signal(barrier, inc=1, device_id=(jnp.clip(me_w + dw, 0, nw - 1),
                                jnp.clip(me_n + dn, 0, nn - 1)), device_id_type=pl.DeviceIdType.MESH)
        count = count + ok.astype(jnp.int32)
    return count


def halo_copy(ins, outs, send, recv, d, sign, me_w, me_n, nw, nn):
    dw, dn = DIRS[d]
    return pltpu.make_async_remote_copy(
        src_ref=ins[d], dst_ref=outs[d], send_sem=send.at[d], recv_sem=recv.at[d],
        device_id=(jnp.clip(me_w + sign * dw, 0, nw - 1), jnp.clip(me_n + sign * dn, 0, nn - 1)),
        device_id_type=pl.DeviceIdType.MESH)


def halo_start(ins, outs, send, recv, me_w, me_n, nw, nn):
    for d, (dw, dn) in enumerate(DIRS):
        @pl.when(inside(me_w, me_n, dw, dn, nw, nn))
        def _():
            halo_copy(ins, outs, send, recv, d, 1, me_w, me_n, nw, nn).start()


def halo_finish(ins, outs, send, recv, me_w, me_n, nw, nn):
    for d, (dw, dn) in enumerate(DIRS):
        src_ok = inside(me_w, me_n, -dw, -dn, nw, nn)

        @pl.when(src_ok)
        def _():
            halo_copy(ins, outs, send, recv, d, -1, me_w, me_n, nw, nn).wait_recv()

        @pl.when(jnp.logical_not(src_ok))
        def _():
            outs[d][...] = jnp.zeros(outs[d].shape, outs[d].dtype)

    for d, (dw, dn) in enumerate(DIRS):
        @pl.when(inside(me_w, me_n, dw, dn, nw, nn))
        def _():
            halo_copy(ins, outs, send, recv, d, 1, me_w, me_n, nw, nn).wait_send()


def shift_pairs(dw, dn, nw, nn):
    pairs = []
    for w in range(nw):
        for n in range(nn):
            tw, tn = w + dw, n + dn
            if 0 <= tw < nw and 0 <= tn < nn:
                pairs.append((w * nn + n, tw * nn + tn))
    return pairs


def exchange(pieces, dw, dn, nw, nn):
    flat = jnp.concatenate([p.reshape(-1) for p in pieces])
    got = lax.ppermute(flat, ("wide", "narrow"), shift_pairs(dw, dn, nw, nn))
    out, at = [], 0
    for p in pieces:
        out.append(got[at : at + p.size].reshape(p.shape))
        at += p.size
    return out


def stencil_kernel(nw, nn, total_cells, *refs):
    nd = len(DIRS)
    det_ref, cm_ref = refs[:2]
    sends = refs[2:2 + nd]
    g_ref, h_ref, out_ref, sq_ref, r0, r1, r2, ss_ref, part1, part2, q1, q2, s1, p1, s2, p2 = \
        refs[2 + nd:18 + nd]
    halos = refs[18 + nd:18 + 2 * nd]
    hs, hr = refs[18 + 2 * nd:]
    top_ref, bot_ref, left_ref, right_ref, tl_ref, tr_ref, bl_ref, br_ref = halos
    i = pl.program_id(0)
    me_w = lax.axis_index("wide")
    me_n = lax.axis_index("narrow")
    mesh_id = pl.DeviceIdType.MESH
    barrier = pltpu.get_barrier_semaphore()
    cx = det_ref.shape[0]
    width = g_ref.shape[1]
    ext_rows = g_ref.shape[0]
    cy = det_ref.shape[1]

    def c0_row(x):
        s = x % RING
        zero = jnp.zeros((width, det_ref.shape[2]), jnp.float32)

        @pl.when(x < HALO)
        def _():
            j = jnp.minimum(x, HALO - 1)
            r0[s] = zero
            r0[s, LPAD - HALO:LPAD] = tl_ref[j]
            r0[s, LPAD:LPAD + cy] = top_ref[j]
            r0[s, LPAD + cy:LPAD + cy + HALO] = tr_ref[j]

        @pl.when(x >= HALO + cx)
        def _():
            j = jnp.clip(x - HALO - cx, 0, HALO - 1)
            r0[s] = zero
            r0[s, LPAD - HALO:LPAD] = bl_ref[j]
            r0[s, LPAD:LPAD + cy] = bot_ref[j]
            r0[s, LPAD + cy:LPAD + cy + HALO] = br_ref[j]

        @pl.when(jnp.logical_and(x >= HALO, x < HALO + cx))
        def _():
            b = jnp.clip(x - HALO, 0, cx - 1)
            t = b // TS
            r0[s, 0:LPAD] = zero[0:LPAD]
            for p in range(HALO):
                r0[s, pl.ds(LPAD - HALO + p, 1)] = left_ref[p, pl.ds(b, 1)]
            own = h_ref[t + 1, LPAD:LPAD + cy] > 0
            r0[s, LPAD:LPAD + cy] = cm_ref[t] + jnp.where(own, det_ref[b].astype(jnp.float32), 0.0)
            r0[s, LPAD + cy:width] = zero[0:width - LPAD - cy]
            for p in range(HALO):
                r0[s, pl.ds(LPAD + cy + p, 1)] = right_ref[p, pl.ds(b, 1)]

    def apply_b(src, x):
        v = src[x % RING]
        nb = src[(x + 1) % RING] + src[(x + RING - 1) % RING]
        nb = nb + pltpu.roll(v, width - 1, 0) + pltpu.roll(v, 1, 0)
        return g_ref[x] * v - h_ref[(x + TS - HALO) // TS] * nb

    def c1_row(x):
        r1[x % RING] = apply_b(r0, x)

    def c2_row(x):
        r2[x % RING] = 2.0 * apply_b(r1, x) - r0[x % RING]

    def c3_row(x):
        c3 = 2.0 * apply_b(r2, x) - r1[x % RING]
        c3 = c3[LPAD:LPAD + cy]
        out_ref[x - HALO - ROWS * i] = c3
        sq = c3 * c3
        ss_ref[...] += jnp.sum(sq.reshape(cy // 8, 8, sq.shape[-1]), axis=0)

    def rows(fn, lo, n):
        def body(k, carry):
            fn(lo + k)
            return carry
        lax.fori_loop(0, n, body, 0)

    @pl.when(i == 0)
    def _():
        for k in range(1, nn):
            pl.semaphore_signal(barrier, inc=1, device_id=(me_w, (me_n + k) % nn), device_id_type=mesh_id)
        for k in range(1, nw):
            pl.semaphore_signal(barrier, inc=1, device_id=((me_w + k) % nw, me_n), device_id_type=mesh_id)
        diag = signal_others(barrier, me_w, me_n, nw, nn, DIAGONALS)
        pl.semaphore_wait(barrier, nn - 1 + nw - 1 + diag)
        halo_start(sends, halos, hs, hr, me_w, me_n, nw, nn)
        halo_finish(sends, halos, hs, hr, me_w, me_n, nw, nn)
        ss_ref[...] = jnp.zeros_like(ss_ref)
        rows(c0_row, 0, 2 * HALO)
        rows(c1_row, 1, 2 * HALO - 2)
        rows(c2_row, 2, 2 * HALO - 4)

    base = ROWS * i
    rows(c0_row, base + 2 * HALO, ROWS)
    rows(c1_row, base + 2 * HALO - 1, ROWS)
    rows(c2_row, base + 2 * HALO - 2, ROWS)
    rows(c3_row, base + HALO, ROWS)

    @pl.when(i == pl.num_programs(0) - 1)
    def _():
        part1[...] = jnp.sum(ss_ref[...], axis=0, keepdims=True)
        part2[...] = exchange_sum(part1, q1, s1, p1, me_n, nn, lambda j: (me_w, j))
        squares = exchange_sum(part2, q2, s2, p2, me_w, nw, lambda j: (j, me_n))
        sq_ref[...] = 1.0 / jnp.sqrt(squares / total_cells + EPSILON)


def exchange_sum(src, slots, send, recv, me, n, peer_of):
    mesh_id = pl.DeviceIdType.MESH
    copies = []
    for k in range(1, n):
        c = pltpu.make_async_remote_copy(
            src_ref=src, dst_ref=slots.at[me], send_sem=send.at[k], recv_sem=recv.at[me],
            device_id=peer_of((me + k) % n), device_id_type=mesh_id)
        c.start()
        copies.append(c)
    slots[me] = src[...]
    for k in range(1, n):
        other = (me + k) % n
        pltpu.make_async_remote_copy(
            src_ref=src, dst_ref=slots.at[other], send_sem=send.at[k], recv_sem=recv.at[other],
            device_id=peer_of(other), device_id_type=mesh_id).wait_recv()
    for c in copies:
        c.wait_send()
    return jnp.sum(slots[...], axis=0)


def run_stencil(det, cm, sends, g, h, nw, nn, total_cells):
    cx, cy, k = det.shape
    width = g.shape[1]
    steps = cx // ROWS
    vmem = pl.BlockSpec(memory_space=pltpu.VMEM)
    ops = cx * cy * k * 3 * 12
    return pl.pallas_call(
        functools.partial(stencil_kernel, nw, nn, float(total_cells)),
        grid=(steps,),
        in_specs=[vmem] * (4 + len(sends)),
        out_specs=[
            pl.BlockSpec((ROWS, cy, k), lambda i: (i, 0, 0)),
            pl.BlockSpec((1, k), lambda i: (0, 0)),
        ],
        out_shape=[
            jax.ShapeDtypeStruct((cx, cy, k), jnp.float32),
            jax.ShapeDtypeStruct((1, k), jnp.float32),
        ],
        scratch_shapes=[pltpu.VMEM((RING, width, k), jnp.float32) for _ in range(3)] + [
            pltpu.VMEM((8, k), jnp.float32),
            pltpu.VMEM((1, k), jnp.float32),
            pltpu.VMEM((1, k), jnp.float32),
            pltpu.VMEM((nn, 1, k), jnp.float32),
            pltpu.VMEM((nw, 1, k), jnp.float32),
            pltpu.SemaphoreType.DMA((nn,)),
            pltpu.SemaphoreType.DMA((nn,)),
            pltpu.SemaphoreType.DMA((nw,)),
            pltpu.SemaphoreType.DMA((nw,)),
        ] + [pltpu.VMEM(p.shape, p.dtype) for p in sends] + [
            pltpu.SemaphoreType.DMA((len(sends),)),
            pltpu.SemaphoreType.DMA((len(sends),)),
        ],
        compiler_params=pltpu.CompilerParams(
            dimension_semantics=("arbitrary",), vmem_limit_bytes=56 * 1024 * 1024,
            collective_id=0, has_side_effects=True,
        ),
        cost_estimate=pl.CostEstimate(
            flops=ops, transcendentals=0, bytes_accessed=det.size * 2 + cx * cy * k * 4 + g.size * 4
        ),
    )(det, cm, *sends, g, h)


def gather_kernel(nw, nn, cols, *refs):
    nd = len(DIRS)
    par_ref, ct_ref = refs[:2]
    gh_in = refs[2:2 + nd]
    o_ref = refs[2 + nd]
    gh_out = refs[3 + nd:3 + 2 * nd]
    pslots, stage, tslots, ps, pq, ts, tq, hs, hr = refs[3 + 2 * nd:]
    me_w = lax.axis_index("wide")
    me_n = lax.axis_index("narrow")
    mesh_id = pl.DeviceIdType.MESH
    barrier = pltpu.get_barrier_semaphore()
    for k in range(1, nn):
        pl.semaphore_signal(barrier, inc=1, device_id=(me_w, (me_n + k) % nn), device_id_type=mesh_id)
    extra = signal_others(barrier, me_w, me_n, nw, nn, VERTICAL)
    pl.semaphore_wait(barrier, nn - 1 + extra)
    halo_start(gh_in, gh_out, hs, hr, me_w, me_n, nw, nn)

    def par_copy(k, other, slot):
        return pltpu.make_async_remote_copy(
            src_ref=par_ref, dst_ref=pslots.at[slot], send_sem=ps.at[k], recv_sem=pq.at[slot],
            device_id=(me_w, other), device_id_type=mesh_id)

    sent = []
    for k in range(1, nn):
        c = par_copy(k, (me_n + k) % nn, me_n)
        c.start()
        sent.append(c)

    local_cells = ct_ref.shape[0]
    ncols = local_cells // cols

    def contribution(par):
        col = par % (ncols * nn)
        idx = (par // (ncols * nn)) * ncols + col % ncols
        idx = jnp.where(col // ncols == me_n, idx, -1)
        rows = lax.broadcasted_iota(jnp.int32, (local_cells, par.shape[-1]), 0)
        onehot = (rows == idx).astype(jnp.bfloat16)
        got = lax.dot_general(ct_ref[...], onehot, (((0,), (0,)), ((), ())),
                              preferred_element_type=jnp.float32)
        return got.astype(jnp.bfloat16)

    tslots[me_n] = contribution(par_ref[...])
    out_copies = []
    for k in range(1, nn):
        other = (me_n + k) % nn
        par_copy(k, other, other).wait_recv()
        stage[k] = contribution(pslots[other])
        c = pltpu.make_async_remote_copy(
            src_ref=stage.at[k], dst_ref=tslots.at[me_n], send_sem=ts.at[k], recv_sem=tq.at[me_n],
            device_id=(me_w, other), device_id_type=mesh_id)
        c.start()
        out_copies.append(c)
    for k in range(1, nn):
        other = (me_n + k) % nn
        pltpu.make_async_remote_copy(
            src_ref=stage.at[k], dst_ref=tslots.at[other], send_sem=ts.at[k], recv_sem=tq.at[other],
            device_id=(me_w, other), device_id_type=mesh_id).wait_recv()
    for c in sent + out_copies:
        c.wait_send()
    halo_finish(gh_in, gh_out, hs, hr, me_w, me_n, nw, nn)
    total = tslots[0].astype(jnp.float32)
    for j in range(1, nn):
        total = total + tslots[j].astype(jnp.float32)
    o_ref[...] = total


def gather_tiles(parents, coarse, gh_pieces, nw, nn):
    ccx, ccy, k = coarse.shape
    par = parents.reshape(1, -1)
    n_t = par.shape[-1]
    ct = coarse.reshape(ccx * ccy, k)
    vmem = pl.BlockSpec(memory_space=pltpu.VMEM)
    return pl.pallas_call(
        functools.partial(gather_kernel, nw, nn, ccx),
        in_specs=[vmem] * (2 + len(gh_pieces)),
        out_specs=[vmem] * (1 + len(gh_pieces)),
        out_shape=[jax.ShapeDtypeStruct((k, n_t), jnp.float32)]
        + [jax.ShapeDtypeStruct(p.shape, p.dtype) for p in gh_pieces],
        scratch_shapes=[
            pltpu.VMEM((nn, 1, n_t), jnp.int32),
            pltpu.VMEM((nn, k, n_t), jnp.bfloat16),
            pltpu.VMEM((nn, k, n_t), jnp.bfloat16),
            pltpu.SemaphoreType.DMA((nn,)),
            pltpu.SemaphoreType.DMA((nn,)),
            pltpu.SemaphoreType.DMA((nn,)),
            pltpu.SemaphoreType.DMA((nn,)),
            pltpu.SemaphoreType.DMA((len(gh_pieces),)),
            pltpu.SemaphoreType.DMA((len(gh_pieces),)),
        ],
        compiler_params=pltpu.CompilerParams(collective_id=1, has_side_effects=True),
    )(par, ct, *gh_pieces)


def scale_kernel(x_ref, s_ref, o_ref):
    o_ref[...] = x_ref[...] * s_ref[...]


def scale_rows(x, inv):
    cx, cy, k = x.shape
    return pl.pallas_call(
        scale_kernel,
        grid=(cx // SCALE_ROWS,),
        in_specs=[pl.BlockSpec((SCALE_ROWS, cy, k), lambda i: (i, 0, 0)), pl.BlockSpec((1, k), lambda i: (0, 0))],
        out_specs=pl.BlockSpec((SCALE_ROWS, cy, k), lambda i: (i, 0, 0)),
        out_shape=jax.ShapeDtypeStruct(x.shape, x.dtype),
        cost_estimate=pl.CostEstimate(flops=x.size, transcendentals=0, bytes_accessed=x.size * 8),
    )(x, inv)


def local(detail, coarse, diagonal, parents, tile_mask):
    tiles_x, tiles_y = parents.shape
    cells_x, cells_y, columns = detail.shape
    nw, nn = lax.axis_size("wide"), lax.axis_size("narrow")
    total_cells = cells_x * nw * cells_y * nn
    mask_float = tile_mask.astype(jnp.float32)

    h = HALO
    cell_mask = jnp.repeat(jnp.repeat(mask_float, TS, axis=0), TS, axis=1)
    g_own = (cell_mask * (4.0 + diagonal) - CENTER) / HALF_WIDTH
    h_own = cell_mask / HALF_WIDTH
    gh = jnp.stack([g_own, h_own])

    def edge(a, dw, dn, rows_axis, cols_axis):
        idx = [slice(None)] * a.ndim
        if dw == 1:
            idx[rows_axis] = slice(a.shape[rows_axis] - h, None)
        elif dw == -1:
            idx[rows_axis] = slice(0, h)
        if dn == 1:
            idx[cols_axis] = slice(a.shape[cols_axis] - h, None)
        elif dn == -1:
            idx[cols_axis] = slice(0, h)
        return a[tuple(idx)]

    gh_t = gh.transpose(0, 2, 1)
    gh_pieces = []
    for dw, dn in DIRS:
        gh_pieces.append(edge(gh_t, dn, dw, 1, 2) if dw == 0 else edge(gh, dw, dn, 1, 2))
    got = gather_tiles(parents, coarse, gh_pieces, nw, nn)
    tile_values = got[0].T
    hg = {dirn: got[1 + k] for k, dirn in enumerate(DIRS)}
    tv = tile_values.reshape(tiles_x, tiles_y, columns)

    m_rows = jnp.repeat(mask_float, TS, axis=1)
    m0 = jnp.broadcast_to(m_rows[:, :, None], (tiles_x, cells_y, columns))
    cm0 = m0 * jnp.repeat(tv, TS, axis=1)

    c0_top = cm0[0][None] + m0[0][None] * detail[:h].astype(jnp.float32)
    c0_bot = cm0[-1][None] + m0[-1][None] * detail[-h:].astype(jnp.float32)
    cm_rep = jnp.repeat(cm0, TS, axis=0)
    m_rep = jnp.repeat(m0, TS, axis=0)
    c0_left = cm_rep[:, :h] + m_rep[:, :h] * detail[:, :h].astype(jnp.float32)
    c0_right = cm_rep[:, -h:] + m_rep[:, -h:] * detail[:, -h:].astype(jnp.float32)
    c0_pieces = {
        (1, 0): c0_bot, (-1, 0): c0_top,
        (0, 1): c0_right.transpose(1, 0, 2), (0, -1): c0_left.transpose(1, 0, 2),
        (1, 1): c0_bot[:, -h:], (1, -1): c0_bot[:, :h], (-1, 1): c0_top[:, -h:], (-1, -1): c0_top[:, :h],
    }
    sends = [c0_pieces[dirn] for dirn in DIRS]

    rpad = LPAD - h
    width = cells_y + 2 * LPAD
    zc = jnp.zeros((2, cells_x, rpad), jnp.float32)
    def cols(x, lo, hi):
        return jnp.pad(x, ((0, 0), (0, 0), (lo, hi)))

    def rows_of(x, lo, hi):
        return jnp.pad(x, ((0, 0), (lo, hi), (0, 0)))

    top = cols(hg[(1, 1)], rpad, width - LPAD) + cols(hg[(1, 0)], LPAD, LPAD) + cols(hg[(1, -1)], LPAD + cells_y, rpad)
    bot = cols(hg[(-1, 1)], rpad, width - LPAD) + cols(hg[(-1, 0)], LPAD, LPAD) + cols(hg[(-1, -1)], LPAD + cells_y, rpad)
    mid_t = rows_of(hg[(0, 1)], rpad, width - LPAD) + rows_of(gh_t, LPAD, LPAD) + rows_of(hg[(0, -1)], LPAD + cells_y, rpad)
    mid = mid_t.transpose(0, 2, 1)
    gh_ext = rows_of(top, 0, cells_x + h) + rows_of(mid, h, h) + rows_of(bot, cells_x + h, 0)
    g_b = jnp.broadcast_to(gh_ext[0][:, :, None], (cells_x + 2 * h, width, columns))
    h_rows = jnp.concatenate(
        [gh_ext[1][0:1], gh_ext[1][h:h + cells_x:TS], gh_ext[1][h + cells_x:h + cells_x + 1]], axis=0)
    h_b = jnp.broadcast_to(h_rows[:, :, None], (tiles_x + 2, width, columns))

    cheb_three, inv = run_stencil(detail, cm0, sends, g_b, h_b, nw, nn, total_cells)
    return scale_rows(cheb_three, inv)


def solution(mesh):
    in_specs = (
        P("wide", "narrow", None),
        P("wide", "narrow", None),
        P("wide", "narrow"),
        P("wide", "narrow"),
        P("wide", "narrow"),
    )
    out_specs = P("wide", "narrow", None)
    return jax.shard_map(local, mesh=mesh, in_specs=in_specs, out_specs=out_specs, check_vma=False)
```

```python
import functools

import jax
import jax.numpy as jnp
from jax import lax
from jax.experimental import pallas as pl
from jax.experimental.pallas import tpu as pltpu
from jax.sharding import PartitionSpec as P

TS = 8
CENTER = 7.5
HALF_WIDTH = 4.5
EPSILON = 1e-06

HALO = 3
LPAD = 8
RING = 32
ROWS = 16
SCALE_ROWS = 64
DIRS = ((1, 0), (-1, 0), (0, 1), (0, -1), (1, 1), (1, -1), (-1, 1), (-1, -1))
DIAGONALS = DIRS[4:]
VERTICAL = ((1, 0), (-1, 0)) + DIAGONALS


def inside(me_w, me_n, dw, dn, nw, nn):
    w, n = me_w + dw, me_n + dn
    return jnp.logical_and(jnp.logical_and(w >= 0, w < nw), jnp.logical_and(n >= 0, n < nn))


def signal_others(barrier, me_w, me_n, nw, nn, dirs):
    count = 0
    for dw, dn in dirs:
        ok = inside(me_w, me_n, dw, dn, nw, nn)

        @pl.when(ok)
        def _():
            pl.semaphore_signal(barrier, inc=1, device_id=(jnp.clip(me_w + dw, 0, nw - 1),
                                jnp.clip(me_n + dn, 0, nn - 1)), device_id_type=pl.DeviceIdType.MESH)
        count = count + ok.astype(jnp.int32)
    return count


def halo_copy(ins, outs, send, recv, d, sign, me_w, me_n, nw, nn):
    dw, dn = DIRS[d]
    return pltpu.make_async_remote_copy(
        src_ref=ins[d], dst_ref=outs[d], send_sem=send.at[d], recv_sem=recv.at[d],
        device_id=(jnp.clip(me_w + sign * dw, 0, nw - 1), jnp.clip(me_n + sign * dn, 0, nn - 1)),
        device_id_type=pl.DeviceIdType.MESH)


def halo_start(ins, outs, send, recv, me_w, me_n, nw, nn):
    for d, (dw, dn) in enumerate(DIRS):
        @pl.when(inside(me_w, me_n, dw, dn, nw, nn))
        def _():
            halo_copy(ins, outs, send, recv, d, 1, me_w, me_n, nw, nn).start()


def halo_finish(ins, outs, send, recv, me_w, me_n, nw, nn):
    for d, (dw, dn) in enumerate(DIRS):
        src_ok = inside(me_w, me_n, -dw, -dn, nw, nn)

        @pl.when(src_ok)
        def _():
            halo_copy(ins, outs, send, recv, d, -1, me_w, me_n, nw, nn).wait_recv()

        @pl.when(jnp.logical_not(src_ok))
        def _():
            outs[d][...] = jnp.zeros(outs[d].shape, outs[d].dtype)

    for d, (dw, dn) in enumerate(DIRS):
        @pl.when(inside(me_w, me_n, dw, dn, nw, nn))
        def _():
            halo_copy(ins, outs, send, recv, d, 1, me_w, me_n, nw, nn).wait_send()


def shift_pairs(dw, dn, nw, nn):
    pairs = []
    for w in range(nw):
        for n in range(nn):
            tw, tn = w + dw, n + dn
            if 0 <= tw < nw and 0 <= tn < nn:
                pairs.append((w * nn + n, tw * nn + tn))
    return pairs


def exchange(pieces, dw, dn, nw, nn):
    flat = jnp.concatenate([p.reshape(-1) for p in pieces])
    got = lax.ppermute(flat, ("wide", "narrow"), shift_pairs(dw, dn, nw, nn))
    out, at = [], 0
    for p in pieces:
        out.append(got[at : at + p.size].reshape(p.shape))
        at += p.size
    return out


def stencil_kernel(nw, nn, total_cells, *refs):
    nd = len(DIRS)
    det_ref, cm_ref = refs[:2]
    sends = refs[2:2 + nd]
    g_ref, h_ref, out_ref, sq_ref, r0, r1, r2, ss_ref, part1, part2, q1, q2, s1, p1, s2, p2 = \
        refs[2 + nd:18 + nd]
    halos = refs[18 + nd:18 + 2 * nd]
    hs, hr = refs[18 + 2 * nd:]
    top_ref, bot_ref, left_ref, right_ref, tl_ref, tr_ref, bl_ref, br_ref = halos
    i = pl.program_id(0)
    me_w = lax.axis_index("wide")
    me_n = lax.axis_index("narrow")
    mesh_id = pl.DeviceIdType.MESH
    barrier = pltpu.get_barrier_semaphore()
    cx = det_ref.shape[0]
    width = g_ref.shape[1]
    ext_rows = g_ref.shape[0]
    cy = det_ref.shape[1]

    def c0_row(x):
        s = x % RING
        zero = jnp.zeros((width, det_ref.shape[2]), jnp.float32)

        @pl.when(x < HALO)
        def _():
            j = jnp.minimum(x, HALO - 1)
            r0[s] = zero
            r0[s, LPAD - HALO:LPAD] = tl_ref[j]
            r0[s, LPAD:LPAD + cy] = top_ref[j]
            r0[s, LPAD + cy:LPAD + cy + HALO] = tr_ref[j]

        @pl.when(x >= HALO + cx)
        def _():
            j = jnp.clip(x - HALO - cx, 0, HALO - 1)
            r0[s] = zero
            r0[s, LPAD - HALO:LPAD] = bl_ref[j]
            r0[s, LPAD:LPAD + cy] = bot_ref[j]
            r0[s, LPAD + cy:LPAD + cy + HALO] = br_ref[j]

        @pl.when(jnp.logical_and(x >= HALO, x < HALO + cx))
        def _():
            b = jnp.clip(x - HALO, 0, cx - 1)
            t = b // TS
            r0[s, 0:LPAD] = zero[0:LPAD]
            for p in range(HALO):
                r0[s, pl.ds(LPAD - HALO + p, 1)] = left_ref[p, pl.ds(b, 1)]
            own = h_ref[t + 1, LPAD:LPAD + cy] > 0
            r0[s, LPAD:LPAD + cy] = cm_ref[t] + jnp.where(own, det_ref[b].astype(jnp.float32), 0.0)
            r0[s, LPAD + cy:width] = zero[0:width - LPAD - cy]
            for p in range(HALO):
                r0[s, pl.ds(LPAD + cy + p, 1)] = right_ref[p, pl.ds(b, 1)]

    def apply_b(src, x):
        v = src[x % RING]
        nb = src[(x + 1) % RING] + src[(x + RING - 1) % RING]
        nb = nb + pltpu.roll(v, width - 1, 0) + pltpu.roll(v, 1, 0)
        return g_ref[x] * v - h_ref[(x + TS - HALO) // TS] * nb

    def c1_row(x):
        r1[x % RING] = apply_b(r0, x)

    def c2_row(x):
        r2[x % RING] = 2.0 * apply_b(r1, x) - r0[x % RING]

    def c3_row(x):
        c3 = 2.0 * apply_b(r2, x) - r1[x % RING]
        c3 = c3[LPAD:LPAD + cy]
        out_ref[x - HALO - ROWS * i] = c3
        sq = c3 * c3
        ss_ref[...] += jnp.sum(sq.reshape(cy // 8, 8, sq.shape[-1]), axis=0)

    def rows(fn, lo, n):
        def body(k, carry):
            fn(lo + k)
            return carry
        lax.fori_loop(0, n, body, 0)

    @pl.when(i == 0)
    def _():
        for k in range(1, nn):
            pl.semaphore_signal(barrier, inc=1, device_id=(me_w, (me_n + k) % nn), device_id_type=mesh_id)
        for k in range(1, nw):
            pl.semaphore_signal(barrier, inc=1, device_id=((me_w + k) % nw, me_n), device_id_type=mesh_id)
        diag = signal_others(barrier, me_w, me_n, nw, nn, DIAGONALS)
        pl.semaphore_wait(barrier, nn - 1 + nw - 1 + diag)
        halo_start(sends, halos, hs, hr, me_w, me_n, nw, nn)
        halo_finish(sends, halos, hs, hr, me_w, me_n, nw, nn)
        ss_ref[...] = jnp.zeros_like(ss_ref)
        rows(c0_row, 0, 2 * HALO)
        rows(c1_row, 1, 2 * HALO - 2)
        rows(c2_row, 2, 2 * HALO - 4)

    base = ROWS * i
    rows(c0_row, base + 2 * HALO, ROWS)
    rows(c1_row, base + 2 * HALO - 1, ROWS)
    rows(c2_row, base + 2 * HALO - 2, ROWS)
    rows(c3_row, base + HALO, ROWS)

    @pl.when(i == pl.num_programs(0) - 1)
    def _():
        part1[...] = jnp.sum(ss_ref[...], axis=0, keepdims=True)
        part2[...] = exchange_sum(part1, q1, s1, p1, me_n, nn, lambda j: (me_w, j))
        squares = exchange_sum(part2, q2, s2, p2, me_w, nw, lambda j: (j, me_n))
        sq_ref[...] = 1.0 / jnp.sqrt(squares / total_cells + EPSILON)


def exchange_sum(src, slots, send, recv, me, n, peer_of):
    mesh_id = pl.DeviceIdType.MESH
    copies = []
    for k in range(1, n):
        c = pltpu.make_async_remote_copy(
            src_ref=src, dst_ref=slots.at[me], send_sem=send.at[k], recv_sem=recv.at[me],
            device_id=peer_of((me + k) % n), device_id_type=mesh_id)
        c.start()
        copies.append(c)
    slots[me] = src[...]
    for k in range(1, n):
        other = (me + k) % n
        pltpu.make_async_remote_copy(
            src_ref=src, dst_ref=slots.at[other], send_sem=send.at[k], recv_sem=recv.at[other],
            device_id=peer_of(other), device_id_type=mesh_id).wait_recv()
    for c in copies:
        c.wait_send()
    return jnp.sum(slots[...], axis=0)


def run_stencil(det, cm, sends, g, h, nw, nn, total_cells):
    cx, cy, k = det.shape
    width = g.shape[1]
    steps = cx // ROWS
    vmem = pl.BlockSpec(memory_space=pltpu.VMEM)
    ops = cx * cy * k * 3 * 12
    return pl.pallas_call(
        functools.partial(stencil_kernel, nw, nn, float(total_cells)),
        grid=(steps,),
        in_specs=[vmem] * (4 + len(sends)),
        out_specs=[
            pl.BlockSpec((ROWS, cy, k), lambda i: (i, 0, 0)),
            pl.BlockSpec((1, k), lambda i: (0, 0)),
        ],
        out_shape=[
            jax.ShapeDtypeStruct((cx, cy, k), jnp.float32),
            jax.ShapeDtypeStruct((1, k), jnp.float32),
        ],
        scratch_shapes=[pltpu.VMEM((RING, width, k), jnp.float32) for _ in range(3)] + [
            pltpu.VMEM((8, k), jnp.float32),
            pltpu.VMEM((1, k), jnp.float32),
            pltpu.VMEM((1, k), jnp.float32),
            pltpu.VMEM((nn, 1, k), jnp.float32),
            pltpu.VMEM((nw, 1, k), jnp.float32),
            pltpu.SemaphoreType.DMA((nn,)),
            pltpu.SemaphoreType.DMA((nn,)),
            pltpu.SemaphoreType.DMA((nw,)),
            pltpu.SemaphoreType.DMA((nw,)),
        ] + [pltpu.VMEM(p.shape, p.dtype) for p in sends] + [
            pltpu.SemaphoreType.DMA((len(sends),)),
            pltpu.SemaphoreType.DMA((len(sends),)),
        ],
        compiler_params=pltpu.CompilerParams(
            dimension_semantics=("arbitrary",), vmem_limit_bytes=56 * 1024 * 1024,
            collective_id=0, has_side_effects=True,
        ),
        cost_estimate=pl.CostEstimate(
            flops=ops, transcendentals=0, bytes_accessed=det.size * 2 + cx * cy * k * 4 + g.size * 4
        ),
    )(det, cm, *sends, g, h)


def gather_kernel(nw, nn, cols, *refs):
    nd = len(DIRS)
    par_ref, ct_ref = refs[:2]
    gh_in = refs[2:2 + nd]
    o_ref = refs[2 + nd]
    gh_out = refs[3 + nd:3 + 2 * nd]
    pslots, stage, tslots, ps, pq, ts, tq, hs, hr = refs[3 + 2 * nd:]
    me_w = lax.axis_index("wide")
    me_n = lax.axis_index("narrow")
    mesh_id = pl.DeviceIdType.MESH
    barrier = pltpu.get_barrier_semaphore()
    for k in range(1, nn):
        pl.semaphore_signal(barrier, inc=1, device_id=(me_w, (me_n + k) % nn), device_id_type=mesh_id)
    extra = signal_others(barrier, me_w, me_n, nw, nn, VERTICAL)
    pl.semaphore_wait(barrier, nn - 1 + extra)
    halo_start(gh_in, gh_out, hs, hr, me_w, me_n, nw, nn)

    def par_copy(k, other, slot):
        return pltpu.make_async_remote_copy(
            src_ref=par_ref, dst_ref=pslots.at[slot], send_sem=ps.at[k], recv_sem=pq.at[slot],
            device_id=(me_w, other), device_id_type=mesh_id)

    sent = []
    for k in range(1, nn):
        c = par_copy(k, (me_n + k) % nn, me_n)
        c.start()
        sent.append(c)

    local_cells = ct_ref.shape[0]
    ncols = local_cells // cols

    def contribution(par):
        col = par % (ncols * nn)
        idx = (par // (ncols * nn)) * ncols + col % ncols
        idx = jnp.where(col // ncols == me_n, idx, -1)
        rows = lax.broadcasted_iota(jnp.int32, (local_cells, par.shape[-1]), 0)
        onehot = (rows == idx).astype(jnp.bfloat16)
        got = lax.dot_general(ct_ref[...], onehot, (((0,), (0,)), ((), ())),
                              preferred_element_type=jnp.float32)
        return got.astype(jnp.bfloat16)

    tslots[me_n] = contribution(par_ref[...])
    out_copies = []
    for k in range(1, nn):
        other = (me_n + k) % nn
        par_copy(k, other, other).wait_recv()
        stage[k] = contribution(pslots[other])
        c = pltpu.make_async_remote_copy(
            src_ref=stage.at[k], dst_ref=tslots.at[me_n], send_sem=ts.at[k], recv_sem=tq.at[me_n],
            device_id=(me_w, other), device_id_type=mesh_id)
        c.start()
        out_copies.append(c)
    for k in range(1, nn):
        other = (me_n + k) % nn
        pltpu.make_async_remote_copy(
            src_ref=stage.at[k], dst_ref=tslots.at[other], send_sem=ts.at[k], recv_sem=tq.at[other],
            device_id=(me_w, other), device_id_type=mesh_id).wait_recv()
    for c in sent + out_copies:
        c.wait_send()
    halo_finish(gh_in, gh_out, hs, hr, me_w, me_n, nw, nn)
    total = tslots[0].astype(jnp.float32)
    for j in range(1, nn):
        total = total + tslots[j].astype(jnp.float32)
    o_ref[...] = total


def gather_tiles(parents, coarse, gh_pieces, nw, nn):
    ccx, ccy, k = coarse.shape
    par = parents.reshape(1, -1)
    n_t = par.shape[-1]
    ct = coarse.reshape(ccx * ccy, k)
    vmem = pl.BlockSpec(memory_space=pltpu.VMEM)
    return pl.pallas_call(
        functools.partial(gather_kernel, nw, nn, ccx),
        in_specs=[vmem] * (2 + len(gh_pieces)),
        out_specs=[vmem] * (1 + len(gh_pieces)),
        out_shape=[jax.ShapeDtypeStruct((k, n_t), jnp.float32)]
        + [jax.ShapeDtypeStruct(p.shape, p.dtype) for p in gh_pieces],
        scratch_shapes=[
            pltpu.VMEM((nn, 1, n_t), jnp.int32),
            pltpu.VMEM((nn, k, n_t), jnp.bfloat16),
            pltpu.VMEM((nn, k, n_t), jnp.bfloat16),
            pltpu.SemaphoreType.DMA((nn,)),
            pltpu.SemaphoreType.DMA((nn,)),
            pltpu.SemaphoreType.DMA((nn,)),
            pltpu.SemaphoreType.DMA((nn,)),
            pltpu.SemaphoreType.DMA((len(gh_pieces),)),
            pltpu.SemaphoreType.DMA((len(gh_pieces),)),
        ],
        compiler_params=pltpu.CompilerParams(collective_id=1, has_side_effects=True),
    )(par, ct, *gh_pieces)


def scale_kernel(x_ref, s_ref, o_ref):
    o_ref[...] = x_ref[...] * s_ref[...]


def scale_rows(x, inv):
    cx, cy, k = x.shape
    return pl.pallas_call(
        scale_kernel,
        grid=(cx // SCALE_ROWS,),
        in_specs=[pl.BlockSpec((SCALE_ROWS, cy, k), lambda i: (i, 0, 0)), pl.BlockSpec((1, k), lambda i: (0, 0))],
        out_specs=pl.BlockSpec((SCALE_ROWS, cy, k), lambda i: (i, 0, 0)),
        out_shape=jax.ShapeDtypeStruct(x.shape, x.dtype),
        cost_estimate=pl.CostEstimate(flops=x.size, transcendentals=0, bytes_accessed=x.size * 8),
    )(x, inv)


def local(detail, coarse, diagonal, parents, tile_mask):
    tiles_x, tiles_y = parents.shape
    cells_x, cells_y, columns = detail.shape
    nw, nn = lax.axis_size("wide"), lax.axis_size("narrow")
    total_cells = cells_x * nw * cells_y * nn
    mask_float = tile_mask.astype(jnp.float32)

    h = HALO
    cell_mask = jnp.repeat(jnp.repeat(mask_float, TS, axis=0), TS, axis=1)
    g_own = (cell_mask * (4.0 + diagonal) - CENTER) / HALF_WIDTH
    h_own = cell_mask / HALF_WIDTH
    gh = jnp.stack([g_own, h_own])

    def edge(a, dw, dn, rows_axis, cols_axis):
        idx = [slice(None)] * a.ndim
        if dw == 1:
            idx[rows_axis] = slice(a.shape[rows_axis] - h, None)
        elif dw == -1:
            idx[rows_axis] = slice(0, h)
        if dn == 1:
            idx[cols_axis] = slice(a.shape[cols_axis] - h, None)
        elif dn == -1:
            idx[cols_axis] = slice(0, h)
        return a[tuple(idx)]

    gh_t = gh.transpose(0, 2, 1)
    gh_pieces = []
    for dw, dn in DIRS:
        gh_pieces.append(edge(gh_t, dn, dw, 1, 2) if dw == 0 else edge(gh, dw, dn, 1, 2))
    got = gather_tiles(parents, coarse, gh_pieces, nw, nn)
    tile_values = got[0].T
    hg = {dirn: got[1 + k] for k, dirn in enumerate(DIRS)}
    tv = tile_values.reshape(tiles_x, tiles_y, columns)

    m_rows = jnp.repeat(mask_float, TS, axis=1)
    m0 = jnp.broadcast_to(m_rows[:, :, None], (tiles_x, cells_y, columns))
    cm0 = m0 * jnp.repeat(tv, TS, axis=1)

    c0_top = cm0[0][None] + m0[0][None] * detail[:h].astype(jnp.float32)
    c0_bot = cm0[-1][None] + m0[-1][None] * detail[-h:].astype(jnp.float32)

    def side_planes(cols_):
        planes = []
        for c in cols_:
            cm_c = jnp.repeat(cm0[:, c], TS, axis=0)
            m_c = jnp.repeat(m0[:, c], TS, axis=0)
            planes.append(cm_c + m_c * detail[:, c].astype(jnp.float32))
        return jnp.stack(planes)

    c0_left = side_planes(range(h))
    c0_right = side_planes(range(cells_y - h, cells_y))
    c0_pieces = {
        (1, 0): c0_bot, (-1, 0): c0_top,
        (0, 1): c0_right, (0, -1): c0_left,
        (1, 1): c0_bot[:, -h:], (1, -1): c0_bot[:, :h], (-1, 1): c0_top[:, -h:], (-1, -1): c0_top[:, :h],
    }
    sends = [c0_pieces[dirn] for dirn in DIRS]

    rpad = LPAD - h
    width = cells_y + 2 * LPAD
    zc = jnp.zeros((2, cells_x, rpad), jnp.float32)
    def cols(x, lo, hi):
        return jnp.pad(x, ((0, 0), (0, 0), (lo, hi)))

    def rows_of(x, lo, hi):
        return jnp.pad(x, ((0, 0), (lo, hi), (0, 0)))

    top = cols(hg[(1, 1)], rpad, width - LPAD) + cols(hg[(1, 0)], LPAD, LPAD) + cols(hg[(1, -1)], LPAD + cells_y, rpad)
    bot = cols(hg[(-1, 1)], rpad, width - LPAD) + cols(hg[(-1, 0)], LPAD, LPAD) + cols(hg[(-1, -1)], LPAD + cells_y, rpad)
    mid_t = rows_of(hg[(0, 1)], rpad, width - LPAD) + rows_of(gh_t, LPAD, LPAD) + rows_of(hg[(0, -1)], LPAD + cells_y, rpad)
    mid = mid_t.transpose(0, 2, 1)
    gh_ext = rows_of(top, 0, cells_x + h) + rows_of(mid, h, h) + rows_of(bot, cells_x + h, 0)
    g_b = jnp.broadcast_to(gh_ext[0][:, :, None], (cells_x + 2 * h, width, columns))
    h_rows = jnp.concatenate(
        [gh_ext[1][0:1], gh_ext[1][h:h + cells_x:TS], gh_ext[1][h + cells_x:h + cells_x + 1]], axis=0)
    h_b = jnp.broadcast_to(h_rows[:, :, None], (tiles_x + 2, width, columns))

    cheb_three, inv = run_stencil(detail, cm0, sends, g_b, h_b, nw, nn, total_cells)
    return scale_rows(cheb_three, inv)


def solution(mesh):
    in_specs = (
        P("wide", "narrow", None),
        P("wide", "narrow", None),
        P("wide", "narrow"),
        P("wide", "narrow"),
        P("wide", "narrow"),
    )
    out_specs = P("wide", "narrow", None)
    return jax.shard_map(local, mesh=mesh, in_specs=in_specs, out_specs=out_specs, check_vma=False)
```

```python
import functools

import jax
import jax.numpy as jnp
from jax import lax
from jax.experimental import pallas as pl
from jax.experimental.pallas import tpu as pltpu
from jax.sharding import PartitionSpec as P

TS = 8
CENTER = 7.5
HALF_WIDTH = 4.5
EPSILON = 1e-06

HALO = 3
LPAD = 8
RING = 32
ROWS = 16
SCALE_ROWS = 128
DIRS = ((1, 0), (-1, 0), (0, 1), (0, -1), (1, 1), (1, -1), (-1, 1), (-1, -1))
DIAGONALS = DIRS[4:]
VERTICAL = ((1, 0), (-1, 0)) + DIAGONALS


def inside(me_w, me_n, dw, dn, nw, nn):
    w, n = me_w + dw, me_n + dn
    return jnp.logical_and(jnp.logical_and(w >= 0, w < nw), jnp.logical_and(n >= 0, n < nn))


def signal_others(barrier, me_w, me_n, nw, nn, dirs):
    count = 0
    for dw, dn in dirs:
        ok = inside(me_w, me_n, dw, dn, nw, nn)

        @pl.when(ok)
        def _():
            pl.semaphore_signal(barrier, inc=1, device_id=(jnp.clip(me_w + dw, 0, nw - 1),
                                jnp.clip(me_n + dn, 0, nn - 1)), device_id_type=pl.DeviceIdType.MESH)
        count = count + ok.astype(jnp.int32)
    return count


def halo_copy(ins, outs, send, recv, d, sign, me_w, me_n, nw, nn):
    dw, dn = DIRS[d]
    return pltpu.make_async_remote_copy(
        src_ref=ins[d], dst_ref=outs[d], send_sem=send.at[d], recv_sem=recv.at[d],
        device_id=(jnp.clip(me_w + sign * dw, 0, nw - 1), jnp.clip(me_n + sign * dn, 0, nn - 1)),
        device_id_type=pl.DeviceIdType.MESH)


def halo_start(ins, outs, send, recv, me_w, me_n, nw, nn):
    for d, (dw, dn) in enumerate(DIRS):
        @pl.when(inside(me_w, me_n, dw, dn, nw, nn))
        def _():
            halo_copy(ins, outs, send, recv, d, 1, me_w, me_n, nw, nn).start()


def halo_finish(ins, outs, send, recv, me_w, me_n, nw, nn):
    for d, (dw, dn) in enumerate(DIRS):
        src_ok = inside(me_w, me_n, -dw, -dn, nw, nn)

        @pl.when(src_ok)
        def _():
            halo_copy(ins, outs, send, recv, d, -1, me_w, me_n, nw, nn).wait_recv()

        @pl.when(jnp.logical_not(src_ok))
        def _():
            outs[d][...] = jnp.zeros(outs[d].shape, outs[d].dtype)

    for d, (dw, dn) in enumerate(DIRS):
        @pl.when(inside(me_w, me_n, dw, dn, nw, nn))
        def _():
            halo_copy(ins, outs, send, recv, d, 1, me_w, me_n, nw, nn).wait_send()


def shift_pairs(dw, dn, nw, nn):
    pairs = []
    for w in range(nw):
        for n in range(nn):
            tw, tn = w + dw, n + dn
            if 0 <= tw < nw and 0 <= tn < nn:
                pairs.append((w * nn + n, tw * nn + tn))
    return pairs


def exchange(pieces, dw, dn, nw, nn):
    flat = jnp.concatenate([p.reshape(-1) for p in pieces])
    got = lax.ppermute(flat, ("wide", "narrow"), shift_pairs(dw, dn, nw, nn))
    out, at = [], 0
    for p in pieces:
        out.append(got[at : at + p.size].reshape(p.shape))
        at += p.size
    return out


def stencil_kernel(nw, nn, total_cells, *refs):
    nd = len(DIRS)
    det_ref, cm_ref = refs[:2]
    sends = refs[2:2 + nd]
    g_ref, h_ref, out_ref, sq_ref, r0, r1, r2, ss_ref, part1, part2, q1, q2, s1, p1, s2, p2 = \
        refs[2 + nd:18 + nd]
    halos = refs[18 + nd:18 + 2 * nd]
    hs, hr = refs[18 + 2 * nd:]
    top_ref, bot_ref, left_ref, right_ref, tl_ref, tr_ref, bl_ref, br_ref = halos
    i = pl.program_id(0)
    me_w = lax.axis_index("wide")
    me_n = lax.axis_index("narrow")
    mesh_id = pl.DeviceIdType.MESH
    barrier = pltpu.get_barrier_semaphore()
    cx = det_ref.shape[0]
    width = g_ref.shape[1]
    ext_rows = g_ref.shape[0]
    cy = det_ref.shape[1]

    def c0_row(x):
        s = x % RING
        zero = jnp.zeros((width, det_ref.shape[2]), jnp.float32)

        @pl.when(x < HALO)
        def _():
            j = jnp.minimum(x, HALO - 1)
            r0[s] = zero
            r0[s, LPAD - HALO:LPAD] = tl_ref[j]
            r0[s, LPAD:LPAD + cy] = top_ref[j]
            r0[s, LPAD + cy:LPAD + cy + HALO] = tr_ref[j]

        @pl.when(x >= HALO + cx)
        def _():
            j = jnp.clip(x - HALO - cx, 0, HALO - 1)
            r0[s] = zero
            r0[s, LPAD - HALO:LPAD] = bl_ref[j]
            r0[s, LPAD:LPAD + cy] = bot_ref[j]
            r0[s, LPAD + cy:LPAD + cy + HALO] = br_ref[j]

        @pl.when(jnp.logical_and(x >= HALO, x < HALO + cx))
        def _():
            b = jnp.clip(x - HALO, 0, cx - 1)
            t = b // TS
            r0[s, 0:LPAD] = zero[0:LPAD]
            for p in range(HALO):
                r0[s, pl.ds(LPAD - HALO + p, 1)] = left_ref[p, pl.ds(b, 1)]
            own = h_ref[t + 1, LPAD:LPAD + cy] > 0
            r0[s, LPAD:LPAD + cy] = cm_ref[t] + jnp.where(own, det_ref[b].astype(jnp.float32), 0.0)
            r0[s, LPAD + cy:width] = zero[0:width - LPAD - cy]
            for p in range(HALO):
                r0[s, pl.ds(LPAD + cy + p, 1)] = right_ref[p, pl.ds(b, 1)]

    def apply_b(src, x):
        v = src[x % RING]
        nb = src[(x + 1) % RING] + src[(x + RING - 1) % RING]
        nb = nb + pltpu.roll(v, width - 1, 0) + pltpu.roll(v, 1, 0)
        return g_ref[x] * v - h_ref[(x + TS - HALO) // TS] * nb

    def c1_row(x):
        r1[x % RING] = apply_b(r0, x)

    def c2_row(x):
        r2[x % RING] = 2.0 * apply_b(r1, x) - r0[x % RING]

    def c3_row(x):
        c3 = 2.0 * apply_b(r2, x) - r1[x % RING]
        c3 = c3[LPAD:LPAD + cy]
        out_ref[x - HALO - ROWS * i] = c3
        sq = c3 * c3
        ss_ref[...] += jnp.sum(sq.reshape(cy // 8, 8, sq.shape[-1]), axis=0)

    def rows(fn, lo, n):
        def body(k, carry):
            fn(lo + k)
            return carry
        lax.fori_loop(0, n, body, 0)

    @pl.when(i == 0)
    def _():
        for k in range(1, nn):
            pl.semaphore_signal(barrier, inc=1, device_id=(me_w, (me_n + k) % nn), device_id_type=mesh_id)
        for k in range(1, nw):
            pl.semaphore_signal(barrier, inc=1, device_id=((me_w + k) % nw, me_n), device_id_type=mesh_id)
        diag = signal_others(barrier, me_w, me_n, nw, nn, DIAGONALS)
        pl.semaphore_wait(barrier, nn - 1 + nw - 1 + diag)
        halo_start(sends, halos, hs, hr, me_w, me_n, nw, nn)
        halo_finish(sends, halos, hs, hr, me_w, me_n, nw, nn)
        ss_ref[...] = jnp.zeros_like(ss_ref)
        rows(c0_row, 0, 2 * HALO)
        rows(c1_row, 1, 2 * HALO - 2)
        rows(c2_row, 2, 2 * HALO - 4)

    base = ROWS * i
    rows(c0_row, base + 2 * HALO, ROWS)
    rows(c1_row, base + 2 * HALO - 1, ROWS)
    rows(c2_row, base + 2 * HALO - 2, ROWS)
    rows(c3_row, base + HALO, ROWS)

    @pl.when(i == pl.num_programs(0) - 1)
    def _():
        part1[...] = jnp.sum(ss_ref[...], axis=0, keepdims=True)
        part2[...] = exchange_sum(part1, q1, s1, p1, me_n, nn, lambda j: (me_w, j))
        squares = exchange_sum(part2, q2, s2, p2, me_w, nw, lambda j: (j, me_n))
        sq_ref[...] = 1.0 / jnp.sqrt(squares / total_cells + EPSILON)


def exchange_sum(src, slots, send, recv, me, n, peer_of):
    mesh_id = pl.DeviceIdType.MESH
    copies = []
    for k in range(1, n):
        c = pltpu.make_async_remote_copy(
            src_ref=src, dst_ref=slots.at[me], send_sem=send.at[k], recv_sem=recv.at[me],
            device_id=peer_of((me + k) % n), device_id_type=mesh_id)
        c.start()
        copies.append(c)
    slots[me] = src[...]
    for k in range(1, n):
        other = (me + k) % n
        pltpu.make_async_remote_copy(
            src_ref=src, dst_ref=slots.at[other], send_sem=send.at[k], recv_sem=recv.at[other],
            device_id=peer_of(other), device_id_type=mesh_id).wait_recv()
    for c in copies:
        c.wait_send()
    return jnp.sum(slots[...], axis=0)


def run_stencil(det, cm, sends, g, h, nw, nn, total_cells):
    cx, cy, k = det.shape
    width = g.shape[1]
    steps = cx // ROWS
    vmem = pl.BlockSpec(memory_space=pltpu.VMEM)
    ops = cx * cy * k * 3 * 12
    return pl.pallas_call(
        functools.partial(stencil_kernel, nw, nn, float(total_cells)),
        grid=(steps,),
        in_specs=[vmem] * (4 + len(sends)),
        out_specs=[
            pl.BlockSpec((ROWS, cy, k), lambda i: (i, 0, 0)),
            pl.BlockSpec((1, k), lambda i: (0, 0)),
        ],
        out_shape=[
            jax.ShapeDtypeStruct((cx, cy, k), jnp.float32),
            jax.ShapeDtypeStruct((1, k), jnp.float32),
        ],
        scratch_shapes=[pltpu.VMEM((RING, width, k), jnp.float32) for _ in range(3)] + [
            pltpu.VMEM((8, k), jnp.float32),
            pltpu.VMEM((1, k), jnp.float32),
            pltpu.VMEM((1, k), jnp.float32),
            pltpu.VMEM((nn, 1, k), jnp.float32),
            pltpu.VMEM((nw, 1, k), jnp.float32),
            pltpu.SemaphoreType.DMA((nn,)),
            pltpu.SemaphoreType.DMA((nn,)),
            pltpu.SemaphoreType.DMA((nw,)),
            pltpu.SemaphoreType.DMA((nw,)),
        ] + [pltpu.VMEM(p.shape, p.dtype) for p in sends] + [
            pltpu.SemaphoreType.DMA((len(sends),)),
            pltpu.SemaphoreType.DMA((len(sends),)),
        ],
        compiler_params=pltpu.CompilerParams(
            dimension_semantics=("arbitrary",), vmem_limit_bytes=56 * 1024 * 1024,
            collective_id=0, has_side_effects=True,
        ),
        cost_estimate=pl.CostEstimate(
            flops=ops, transcendentals=0, bytes_accessed=det.size * 2 + cx * cy * k * 4 + g.size * 4
        ),
    )(det, cm, *sends, g, h)


def gather_kernel(nw, nn, cols, *refs):
    nd = len(DIRS)
    par_ref, ct_ref = refs[:2]
    gh_in = refs[2:2 + nd]
    o_ref = refs[2 + nd]
    gh_out = refs[3 + nd:3 + 2 * nd]
    pslots, stage, tslots, ps, pq, ts, tq, hs, hr = refs[3 + 2 * nd:]
    me_w = lax.axis_index("wide")
    me_n = lax.axis_index("narrow")
    mesh_id = pl.DeviceIdType.MESH
    barrier = pltpu.get_barrier_semaphore()
    for k in range(1, nn):
        pl.semaphore_signal(barrier, inc=1, device_id=(me_w, (me_n + k) % nn), device_id_type=mesh_id)
    extra = signal_others(barrier, me_w, me_n, nw, nn, VERTICAL)
    pl.semaphore_wait(barrier, nn - 1 + extra)
    halo_start(gh_in, gh_out, hs, hr, me_w, me_n, nw, nn)

    def par_copy(k, other, slot):
        return pltpu.make_async_remote_copy(
            src_ref=par_ref, dst_ref=pslots.at[slot], send_sem=ps.at[k], recv_sem=pq.at[slot],
            device_id=(me_w, other), device_id_type=mesh_id)

    sent = []
    for k in range(1, nn):
        c = par_copy(k, (me_n + k) % nn, me_n)
        c.start()
        sent.append(c)

    local_cells = ct_ref.shape[0]
    ncols = local_cells // cols

    def contribution(par):
        col = par % (ncols * nn)
        idx = (par // (ncols * nn)) * ncols + col % ncols
        idx = jnp.where(col // ncols == me_n, idx, -1)
        rows = lax.broadcasted_iota(jnp.int32, (local_cells, par.shape[-1]), 0)
        onehot = (rows == idx).astype(jnp.bfloat16)
        got = lax.dot_general(ct_ref[...], onehot, (((0,), (0,)), ((), ())),
                              preferred_element_type=jnp.float32)
        return got.astype(jnp.bfloat16)

    tslots[me_n] = contribution(par_ref[...])
    out_copies = []
    for k in range(1, nn):
        other = (me_n + k) % nn
        par_copy(k, other, other).wait_recv()
        stage[k] = contribution(pslots[other])
        c = pltpu.make_async_remote_copy(
            src_ref=stage.at[k], dst_ref=tslots.at[me_n], send_sem=ts.at[k], recv_sem=tq.at[me_n],
            device_id=(me_w, other), device_id_type=mesh_id)
        c.start()
        out_copies.append(c)
    for k in range(1, nn):
        other = (me_n + k) % nn
        pltpu.make_async_remote_copy(
            src_ref=stage.at[k], dst_ref=tslots.at[other], send_sem=ts.at[k], recv_sem=tq.at[other],
            device_id=(me_w, other), device_id_type=mesh_id).wait_recv()
    for c in sent + out_copies:
        c.wait_send()
    halo_finish(gh_in, gh_out, hs, hr, me_w, me_n, nw, nn)
    total = tslots[0].astype(jnp.float32)
    for j in range(1, nn):
        total = total + tslots[j].astype(jnp.float32)
    o_ref[...] = total


def gather_tiles(parents, coarse, gh_pieces, nw, nn):
    ccx, ccy, k = coarse.shape
    par = parents.reshape(1, -1)
    n_t = par.shape[-1]
    ct = coarse.reshape(ccx * ccy, k)
    vmem = pl.BlockSpec(memory_space=pltpu.VMEM)
    return pl.pallas_call(
        functools.partial(gather_kernel, nw, nn, ccx),
        in_specs=[vmem] * (2 + len(gh_pieces)),
        out_specs=[vmem] * (1 + len(gh_pieces)),
        out_shape=[jax.ShapeDtypeStruct((k, n_t), jnp.float32)]
        + [jax.ShapeDtypeStruct(p.shape, p.dtype) for p in gh_pieces],
        scratch_shapes=[
            pltpu.VMEM((nn, 1, n_t), jnp.int32),
            pltpu.VMEM((nn, k, n_t), jnp.bfloat16),
            pltpu.VMEM((nn, k, n_t), jnp.bfloat16),
            pltpu.SemaphoreType.DMA((nn,)),
            pltpu.SemaphoreType.DMA((nn,)),
            pltpu.SemaphoreType.DMA((nn,)),
            pltpu.SemaphoreType.DMA((nn,)),
            pltpu.SemaphoreType.DMA((len(gh_pieces),)),
            pltpu.SemaphoreType.DMA((len(gh_pieces),)),
        ],
        compiler_params=pltpu.CompilerParams(collective_id=1, has_side_effects=True),
    )(par, ct, *gh_pieces)


def scale_kernel(x_ref, s_ref, o_ref):
    o_ref[...] = x_ref[...] * s_ref[...]


def scale_rows(x, inv):
    cx, cy, k = x.shape
    return pl.pallas_call(
        scale_kernel,
        grid=(cx // SCALE_ROWS,),
        in_specs=[pl.BlockSpec((SCALE_ROWS, cy, k), lambda i: (i, 0, 0)), pl.BlockSpec((1, k), lambda i: (0, 0))],
        out_specs=pl.BlockSpec((SCALE_ROWS, cy, k), lambda i: (i, 0, 0)),
        out_shape=jax.ShapeDtypeStruct(x.shape, x.dtype),
        cost_estimate=pl.CostEstimate(flops=x.size, transcendentals=0, bytes_accessed=x.size * 8),
    )(x, inv)


def local(detail, coarse, diagonal, parents, tile_mask):
    tiles_x, tiles_y = parents.shape
    cells_x, cells_y, columns = detail.shape
    nw, nn = lax.axis_size("wide"), lax.axis_size("narrow")
    total_cells = cells_x * nw * cells_y * nn
    mask_float = tile_mask.astype(jnp.float32)

    h = HALO
    cell_mask = jnp.repeat(jnp.repeat(mask_float, TS, axis=0), TS, axis=1)
    g_own = (cell_mask * (4.0 + diagonal) - CENTER) / HALF_WIDTH
    h_own = cell_mask / HALF_WIDTH
    gh = jnp.stack([g_own, h_own])

    def edge(a, dw, dn, rows_axis, cols_axis):
        idx = [slice(None)] * a.ndim
        if dw == 1:
            idx[rows_axis] = slice(a.shape[rows_axis] - h, None)
        elif dw == -1:
            idx[rows_axis] = slice(0, h)
        if dn == 1:
            idx[cols_axis] = slice(a.shape[cols_axis] - h, None)
        elif dn == -1:
            idx[cols_axis] = slice(0, h)
        return a[tuple(idx)]

    gh_t = gh.transpose(0, 2, 1)
    gh_pieces = []
    for dw, dn in DIRS:
        gh_pieces.append(edge(gh_t, dn, dw, 1, 2) if dw == 0 else edge(gh, dw, dn, 1, 2))
    got = gather_tiles(parents, coarse, gh_pieces, nw, nn)
    tile_values = got[0].T
    hg = {dirn: got[1 + k] for k, dirn in enumerate(DIRS)}
    tv = tile_values.reshape(tiles_x, tiles_y, columns)

    m_rows = jnp.repeat(mask_float, TS, axis=1)
    m0 = jnp.broadcast_to(m_rows[:, :, None], (tiles_x, cells_y, columns))
    cm0 = m0 * jnp.repeat(tv, TS, axis=1)

    c0_top = cm0[0][None] + m0[0][None] * detail[:h].astype(jnp.float32)
    c0_bot = cm0[-1][None] + m0[-1][None] * detail[-h:].astype(jnp.float32)
    cm_rep = jnp.repeat(cm0, TS, axis=0)
    m_rep = jnp.repeat(m0, TS, axis=0)
    c0_left = cm_rep[:, :h] + m_rep[:, :h] * detail[:, :h].astype(jnp.float32)
    c0_right = cm_rep[:, -h:] + m_rep[:, -h:] * detail[:, -h:].astype(jnp.float32)
    c0_pieces = {
        (1, 0): c0_bot, (-1, 0): c0_top,
        (0, 1): c0_right.transpose(1, 0, 2), (0, -1): c0_left.transpose(1, 0, 2),
        (1, 1): c0_bot[:, -h:], (1, -1): c0_bot[:, :h], (-1, 1): c0_top[:, -h:], (-1, -1): c0_top[:, :h],
    }
    sends = [c0_pieces[dirn] for dirn in DIRS]

    rpad = LPAD - h
    width = cells_y + 2 * LPAD
    zc = jnp.zeros((2, cells_x, rpad), jnp.float32)
    def cols(x, lo, hi):
        return jnp.pad(x, ((0, 0), (0, 0), (lo, hi)))

    def rows_of(x, lo, hi):
        return jnp.pad(x, ((0, 0), (lo, hi), (0, 0)))

    top = cols(hg[(1, 1)], rpad, width - LPAD) + cols(hg[(1, 0)], LPAD, LPAD) + cols(hg[(1, -1)], LPAD + cells_y, rpad)
    bot = cols(hg[(-1, 1)], rpad, width - LPAD) + cols(hg[(-1, 0)], LPAD, LPAD) + cols(hg[(-1, -1)], LPAD + cells_y, rpad)
    mid_t = rows_of(hg[(0, 1)], rpad, width - LPAD) + rows_of(gh_t, LPAD, LPAD) + rows_of(hg[(0, -1)], LPAD + cells_y, rpad)
    mid = mid_t.transpose(0, 2, 1)
    gh_ext = rows_of(top, 0, cells_x + h) + rows_of(mid, h, h) + rows_of(bot, cells_x + h, 0)
    g_b = jnp.broadcast_to(gh_ext[0][:, :, None], (cells_x + 2 * h, width, columns))
    h_rows = jnp.concatenate(
        [gh_ext[1][0:1], gh_ext[1][h:h + cells_x:TS], gh_ext[1][h + cells_x:h + cells_x + 1]], axis=0)
    h_b = jnp.broadcast_to(h_rows[:, :, None], (tiles_x + 2, width, columns))

    cheb_three, inv = run_stencil(detail, cm0, sends, g_b, h_b, nw, nn, total_cells)
    return scale_rows(cheb_three, inv)


def solution(mesh):
    in_specs = (
        P("wide", "narrow", None),
        P("wide", "narrow", None),
        P("wide", "narrow"),
        P("wide", "narrow"),
        P("wide", "narrow"),
    )
    out_specs = P("wide", "narrow", None)
    return jax.shard_map(local, mesh=mesh, in_specs=in_specs, out_specs=out_specs, check_vma=False)
```

```python
import functools

import jax
import jax.numpy as jnp
from jax import lax
from jax.experimental import pallas as pl
from jax.experimental.pallas import tpu as pltpu
from jax.sharding import PartitionSpec as P

TS = 8
CENTER = 7.5
HALF_WIDTH = 4.5
EPSILON = 1e-06

HALO = 3
LPAD = 8
RING = 32
ROWS = 16
SCALE_ROWS = 64
DIRS = ((1, 0), (-1, 0), (0, 1), (0, -1), (1, 1), (1, -1), (-1, 1), (-1, -1))
DIAGONALS = DIRS[4:]
VERTICAL = ((1, 0), (-1, 0)) + DIAGONALS


def inside(me_w, me_n, dw, dn, nw, nn):
    w, n = me_w + dw, me_n + dn
    return jnp.logical_and(jnp.logical_and(w >= 0, w < nw), jnp.logical_and(n >= 0, n < nn))


def signal_others(barrier, me_w, me_n, nw, nn, dirs):
    count = 0
    for dw, dn in dirs:
        ok = inside(me_w, me_n, dw, dn, nw, nn)

        @pl.when(ok)
        def _():
            pl.semaphore_signal(barrier, inc=1, device_id=(jnp.clip(me_w + dw, 0, nw - 1),
                                jnp.clip(me_n + dn, 0, nn - 1)), device_id_type=pl.DeviceIdType.MESH)
        count = count + ok.astype(jnp.int32)
    return count


def halo_copy(ins, outs, send, recv, d, sign, me_w, me_n, nw, nn):
    dw, dn = DIRS[d]
    return pltpu.make_async_remote_copy(
        src_ref=ins[d], dst_ref=outs[d], send_sem=send.at[d], recv_sem=recv.at[d],
        device_id=(jnp.clip(me_w + sign * dw, 0, nw - 1), jnp.clip(me_n + sign * dn, 0, nn - 1)),
        device_id_type=pl.DeviceIdType.MESH)


def halo_start(ins, outs, send, recv, me_w, me_n, nw, nn):
    for d, (dw, dn) in enumerate(DIRS):
        @pl.when(inside(me_w, me_n, dw, dn, nw, nn))
        def _():
            halo_copy(ins, outs, send, recv, d, 1, me_w, me_n, nw, nn).start()


def halo_finish(ins, outs, send, recv, me_w, me_n, nw, nn):
    for d, (dw, dn) in enumerate(DIRS):
        src_ok = inside(me_w, me_n, -dw, -dn, nw, nn)

        @pl.when(src_ok)
        def _():
            halo_copy(ins, outs, send, recv, d, -1, me_w, me_n, nw, nn).wait_recv()

        @pl.when(jnp.logical_not(src_ok))
        def _():
            outs[d][...] = jnp.zeros(outs[d].shape, outs[d].dtype)

    for d, (dw, dn) in enumerate(DIRS):
        @pl.when(inside(me_w, me_n, dw, dn, nw, nn))
        def _():
            halo_copy(ins, outs, send, recv, d, 1, me_w, me_n, nw, nn).wait_send()


def shift_pairs(dw, dn, nw, nn):
    pairs = []
    for w in range(nw):
        for n in range(nn):
            tw, tn = w + dw, n + dn
            if 0 <= tw < nw and 0 <= tn < nn:
                pairs.append((w * nn + n, tw * nn + tn))
    return pairs


def exchange(pieces, dw, dn, nw, nn):
    flat = jnp.concatenate([p.reshape(-1) for p in pieces])
    got = lax.ppermute(flat, ("wide", "narrow"), shift_pairs(dw, dn, nw, nn))
    out, at = [], 0
    for p in pieces:
        out.append(got[at : at + p.size].reshape(p.shape))
        at += p.size
    return out


def stencil_kernel(nw, nn, total_cells, *refs):
    nd = len(DIRS)
    det_ref, cm_ref = refs[:2]
    sends = refs[2:2 + nd]
    g_ref, h_ref, out_ref, sq_ref, r0, r1, r2, ss_ref, part1, part2, q1, q2, s1, p1, s2, p2 = \
        refs[2 + nd:18 + nd]
    halos = refs[18 + nd:18 + 2 * nd]
    hs, hr = refs[18 + 2 * nd:]
    top_ref, bot_ref, left_ref, right_ref, tl_ref, tr_ref, bl_ref, br_ref = halos
    i = pl.program_id(0)
    me_w = lax.axis_index("wide")
    me_n = lax.axis_index("narrow")
    mesh_id = pl.DeviceIdType.MESH
    barrier = pltpu.get_barrier_semaphore()
    cx = det_ref.shape[0]
    width = g_ref.shape[1]
    ext_rows = g_ref.shape[0]
    cy = det_ref.shape[1]

    def c0_row(x):
        s = x % RING
        zero = jnp.zeros((width, det_ref.shape[2]), jnp.float32)

        @pl.when(x < HALO)
        def _():
            j = jnp.minimum(x, HALO - 1)
            r0[s] = zero
            r0[s, LPAD - HALO:LPAD] = tl_ref[j]
            r0[s, LPAD:LPAD + cy] = top_ref[j]
            r0[s, LPAD + cy:LPAD + cy + HALO] = tr_ref[j]

        @pl.when(x >= HALO + cx)
        def _():
            j = jnp.clip(x - HALO - cx, 0, HALO - 1)
            r0[s] = zero
            r0[s, LPAD - HALO:LPAD] = bl_ref[j]
            r0[s, LPAD:LPAD + cy] = bot_ref[j]
            r0[s, LPAD + cy:LPAD + cy + HALO] = br_ref[j]

        @pl.when(jnp.logical_and(x >= HALO, x < HALO + cx))
        def _():
            b = jnp.clip(x - HALO, 0, cx - 1)
            t = b // TS
            r0[s, 0:LPAD] = zero[0:LPAD]
            for p in range(HALO):
                r0[s, pl.ds(LPAD - HALO + p, 1)] = left_ref[p, pl.ds(b, 1)]
            own = h_ref[t + 1, LPAD:LPAD + cy] > 0
            r0[s, LPAD:LPAD + cy] = cm_ref[t] + jnp.where(own, det_ref[b].astype(jnp.float32), 0.0)
            r0[s, LPAD + cy:width] = zero[0:width - LPAD - cy]
            for p in range(HALO):
                r0[s, pl.ds(LPAD + cy + p, 1)] = right_ref[p, pl.ds(b, 1)]

    def apply_b(src, x):
        v = src[x % RING]
        nb = src[(x + 1) % RING] + src[(x + RING - 1) % RING]
        nb = nb + pltpu.roll(v, width - 1, 0) + pltpu.roll(v, 1, 0)
        return g_ref[x] * v - h_ref[(x + TS - HALO) // TS] * nb

    def c1_row(x):
        r1[x % RING] = apply_b(r0, x)

    def c2_row(x):
        r2[x % RING] = 2.0 * apply_b(r1, x) - r0[x % RING]

    def c3_row(x):
        c3 = 2.0 * apply_b(r2, x) - r1[x % RING]
        c3 = c3[LPAD:LPAD + cy]
        out_ref[x - HALO - ROWS * i] = c3
        sq = c3 * c3
        ss_ref[...] += jnp.sum(sq.reshape(cy // 8, 8, sq.shape[-1]), axis=0)

    def rows(fn, lo, n):
        def body(k, carry):
            fn(lo + k)
            return carry
        lax.fori_loop(0, n, body, 0)

    @pl.when(i == 0)
    def _():
        for k in range(1, nn):
            pl.semaphore_signal(barrier, inc=1, device_id=(me_w, (me_n + k) % nn), device_id_type=mesh_id)
        for k in range(1, nw):
            pl.semaphore_signal(barrier, inc=1, device_id=((me_w + k) % nw, me_n), device_id_type=mesh_id)
        diag = signal_others(barrier, me_w, me_n, nw, nn, DIAGONALS)
        pl.semaphore_wait(barrier, nn - 1 + nw - 1 + diag)
        halo_start(sends, halos, hs, hr, me_w, me_n, nw, nn)
        halo_finish(sends, halos, hs, hr, me_w, me_n, nw, nn)
        ss_ref[...] = jnp.zeros_like(ss_ref)
        rows(c0_row, 0, 2 * HALO)
        rows(c1_row, 1, 2 * HALO - 2)
        rows(c2_row, 2, 2 * HALO - 4)

    base = ROWS * i
    rows(c0_row, base + 2 * HALO, ROWS)
    rows(c1_row, base + 2 * HALO - 1, ROWS)
    rows(c2_row, base + 2 * HALO - 2, ROWS)
    rows(c3_row, base + HALO, ROWS)

    @pl.when(i == pl.num_programs(0) - 1)
    def _():
        part1[...] = jnp.sum(ss_ref[...], axis=0, keepdims=True)
        part2[...] = exchange_sum(part1, q1, s1, p1, me_n, nn, lambda j: (me_w, j))
        squares = exchange_sum(part2, q2, s2, p2, me_w, nw, lambda j: (j, me_n))
        sq_ref[...] = 1.0 / jnp.sqrt(squares / total_cells + EPSILON)


def exchange_sum(src, slots, send, recv, me, n, peer_of):
    mesh_id = pl.DeviceIdType.MESH
    copies = []
    for k in range(1, n):
        c = pltpu.make_async_remote_copy(
            src_ref=src, dst_ref=slots.at[me], send_sem=send.at[k], recv_sem=recv.at[me],
            device_id=peer_of((me + k) % n), device_id_type=mesh_id)
        c.start()
        copies.append(c)
    slots[me] = src[...]
    for k in range(1, n):
        other = (me + k) % n
        pltpu.make_async_remote_copy(
            src_ref=src, dst_ref=slots.at[other], send_sem=send.at[k], recv_sem=recv.at[other],
            device_id=peer_of(other), device_id_type=mesh_id).wait_recv()
    for c in copies:
        c.wait_send()
    return jnp.sum(slots[...], axis=0)


def run_stencil(det, cm, sends, g, h, nw, nn, total_cells):
    cx, cy, k = det.shape
    width = g.shape[1]
    steps = cx // ROWS
    vmem = pl.BlockSpec(memory_space=pltpu.VMEM)
    ops = cx * cy * k * 3 * 12
    return pl.pallas_call(
        functools.partial(stencil_kernel, nw, nn, float(total_cells)),
        grid=(steps,),
        in_specs=[vmem] * (4 + len(sends)),
        out_specs=[
            pl.BlockSpec((ROWS, cy, k), lambda i: (i, 0, 0)),
            pl.BlockSpec((1, k), lambda i: (0, 0)),
        ],
        out_shape=[
            jax.ShapeDtypeStruct((cx, cy, k), jnp.float32),
            jax.ShapeDtypeStruct((1, k), jnp.float32),
        ],
        scratch_shapes=[pltpu.VMEM((RING, width, k), jnp.float32) for _ in range(3)] + [
            pltpu.VMEM((8, k), jnp.float32),
            pltpu.VMEM((1, k), jnp.float32),
            pltpu.VMEM((1, k), jnp.float32),
            pltpu.VMEM((nn, 1, k), jnp.float32),
            pltpu.VMEM((nw, 1, k), jnp.float32),
            pltpu.SemaphoreType.DMA((nn,)),
            pltpu.SemaphoreType.DMA((nn,)),
            pltpu.SemaphoreType.DMA((nw,)),
            pltpu.SemaphoreType.DMA((nw,)),
        ] + [pltpu.VMEM(p.shape, p.dtype) for p in sends] + [
            pltpu.SemaphoreType.DMA((len(sends),)),
            pltpu.SemaphoreType.DMA((len(sends),)),
        ],
        compiler_params=pltpu.CompilerParams(
            dimension_semantics=("arbitrary",), vmem_limit_bytes=56 * 1024 * 1024,
            collective_id=0, has_side_effects=True,
        ),
        cost_estimate=pl.CostEstimate(
            flops=ops, transcendentals=0, bytes_accessed=det.size * 2 + cx * cy * k * 4 + g.size * 4
        ),
    )(det, cm, *sends, g, h)


def gather_kernel(nw, nn, cols, *refs):
    nd = len(DIRS)
    par_ref, ct_ref = refs[:2]
    gh_in = refs[2:2 + nd]
    o_ref = refs[2 + nd]
    gh_out = refs[3 + nd:3 + 2 * nd]
    pslots, stage, tslots, ps, pq, ts, tq, hs, hr = refs[3 + 2 * nd:]
    me_w = lax.axis_index("wide")
    me_n = lax.axis_index("narrow")
    mesh_id = pl.DeviceIdType.MESH
    barrier = pltpu.get_barrier_semaphore()
    for k in range(1, nn):
        pl.semaphore_signal(barrier, inc=1, device_id=(me_w, (me_n + k) % nn), device_id_type=mesh_id)
    extra = signal_others(barrier, me_w, me_n, nw, nn, VERTICAL)
    pl.semaphore_wait(barrier, nn - 1 + extra)
    halo_start(gh_in, gh_out, hs, hr, me_w, me_n, nw, nn)

    def par_copy(k, other, slot):
        return pltpu.make_async_remote_copy(
            src_ref=par_ref, dst_ref=pslots.at[slot], send_sem=ps.at[k], recv_sem=pq.at[slot],
            device_id=(me_w, other), device_id_type=mesh_id)

    sent = []
    for k in range(1, nn):
        c = par_copy(k, (me_n + k) % nn, me_n)
        c.start()
        sent.append(c)

    local_cells = ct_ref.shape[0]
    ncols = local_cells // cols

    def contribution(par):
        col = par % (ncols * nn)
        idx = (par // (ncols * nn)) * ncols + col % ncols
        idx = jnp.where(col // ncols == me_n, idx, -1)
        rows = lax.broadcasted_iota(jnp.int32, (local_cells, par.shape[-1]), 0)
        onehot = (rows == idx).astype(jnp.bfloat16)
        got = lax.dot_general(ct_ref[...], onehot, (((0,), (0,)), ((), ())),
                              preferred_element_type=jnp.float32)
        return got.astype(jnp.bfloat16)

    tslots[me_n] = contribution(par_ref[...])
    out_copies = []
    for k in range(1, nn):
        other = (me_n + k) % nn
        par_copy(k, other, other).wait_recv()
        stage[k] = contribution(pslots[other])
        c = pltpu.make_async_remote_copy(
            src_ref=stage.at[k], dst_ref=tslots.at[me_n], send_sem=ts.at[k], recv_sem=tq.at[me_n],
            device_id=(me_w, other), device_id_type=mesh_id)
        c.start()
        out_copies.append(c)
    for k in range(1, nn):
        other = (me_n + k) % nn
        pltpu.make_async_remote_copy(
            src_ref=stage.at[k], dst_ref=tslots.at[other], send_sem=ts.at[k], recv_sem=tq.at[other],
            device_id=(me_w, other), device_id_type=mesh_id).wait_recv()
    for c in sent + out_copies:
        c.wait_send()
    halo_finish(gh_in, gh_out, hs, hr, me_w, me_n, nw, nn)
    total = tslots[0].astype(jnp.float32)
    for j in range(1, nn):
        total = total + tslots[j].astype(jnp.float32)
    o_ref[...] = total


def gather_tiles(parents, coarse, gh_pieces, nw, nn):
    ccx, ccy, k = coarse.shape
    par = parents.reshape(1, -1)
    n_t = par.shape[-1]
    ct = coarse.reshape(ccx * ccy, k)
    vmem = pl.BlockSpec(memory_space=pltpu.VMEM)
    return pl.pallas_call(
        functools.partial(gather_kernel, nw, nn, ccx),
        in_specs=[vmem] * (2 + len(gh_pieces)),
        out_specs=[vmem] * (1 + len(gh_pieces)),
        out_shape=[jax.ShapeDtypeStruct((k, n_t), jnp.float32)]
        + [jax.ShapeDtypeStruct(p.shape, p.dtype) for p in gh_pieces],
        scratch_shapes=[
            pltpu.VMEM((nn, 1, n_t), jnp.int32),
            pltpu.VMEM((nn, k, n_t), jnp.bfloat16),
            pltpu.VMEM((nn, k, n_t), jnp.bfloat16),
            pltpu.SemaphoreType.DMA((nn,)),
            pltpu.SemaphoreType.DMA((nn,)),
            pltpu.SemaphoreType.DMA((nn,)),
            pltpu.SemaphoreType.DMA((nn,)),
            pltpu.SemaphoreType.DMA((len(gh_pieces),)),
            pltpu.SemaphoreType.DMA((len(gh_pieces),)),
        ],
        compiler_params=pltpu.CompilerParams(collective_id=1, has_side_effects=True),
    )(par, ct, *gh_pieces)


def scale_kernel(x_ref, s_ref, o_ref):
    o_ref[...] = x_ref[...] * s_ref[...]


def scale_rows(x, inv):
    cx, cy, k = x.shape
    return pl.pallas_call(
        scale_kernel,
        grid=(cx // SCALE_ROWS,),
        in_specs=[pl.BlockSpec((SCALE_ROWS, cy, k), lambda i: (i, 0, 0)), pl.BlockSpec((1, k), lambda i: (0, 0))],
        out_specs=pl.BlockSpec((SCALE_ROWS, cy, k), lambda i: (i, 0, 0)),
        out_shape=jax.ShapeDtypeStruct(x.shape, x.dtype),
        cost_estimate=pl.CostEstimate(flops=x.size, transcendentals=0, bytes_accessed=x.size * 8),
    )(x, inv)


def local(detail, coarse, diagonal, parents, tile_mask):
    tiles_x, tiles_y = parents.shape
    cells_x, cells_y, columns = detail.shape
    nw, nn = lax.axis_size("wide"), lax.axis_size("narrow")
    total_cells = cells_x * nw * cells_y * nn
    mask_float = tile_mask.astype(jnp.float32)

    h = HALO
    cell_mask = jnp.repeat(jnp.repeat(mask_float, TS, axis=0), TS, axis=1)
    g_own = (cell_mask * (4.0 + diagonal) - CENTER) / HALF_WIDTH
    h_own = cell_mask / HALF_WIDTH
    gh = jnp.stack([g_own, h_own])

    def edge(a, dw, dn, rows_axis, cols_axis):
        idx = [slice(None)] * a.ndim
        if dw == 1:
            idx[rows_axis] = slice(a.shape[rows_axis] - h, None)
        elif dw == -1:
            idx[rows_axis] = slice(0, h)
        if dn == 1:
            idx[cols_axis] = slice(a.shape[cols_axis] - h, None)
        elif dn == -1:
            idx[cols_axis] = slice(0, h)
        return a[tuple(idx)]

    cell_mask_t = cell_mask.T
    gh_t = jnp.stack([(cell_mask_t * (4.0 + diagonal.T) - CENTER) / HALF_WIDTH, cell_mask_t / HALF_WIDTH])
    gh_pieces = []
    for dw, dn in DIRS:
        gh_pieces.append(edge(gh_t, dn, dw, 1, 2) if dw == 0 else edge(gh, dw, dn, 1, 2))
    got = gather_tiles(parents, coarse, gh_pieces, nw, nn)
    tile_values = got[0].T
    hg = {dirn: got[1 + k] for k, dirn in enumerate(DIRS)}
    tv = tile_values.reshape(tiles_x, tiles_y, columns)

    m_rows = jnp.repeat(mask_float, TS, axis=1)
    m0 = jnp.broadcast_to(m_rows[:, :, None], (tiles_x, cells_y, columns))
    cm0 = m0 * jnp.repeat(tv, TS, axis=1)

    c0_top = cm0[0][None] + m0[0][None] * detail[:h].astype(jnp.float32)
    c0_bot = cm0[-1][None] + m0[-1][None] * detail[-h:].astype(jnp.float32)
    cm_rep = jnp.repeat(cm0, TS, axis=0)
    m_rep = jnp.repeat(m0, TS, axis=0)
    c0_left = cm_rep[:, :h] + m_rep[:, :h] * detail[:, :h].astype(jnp.float32)
    c0_right = cm_rep[:, -h:] + m_rep[:, -h:] * detail[:, -h:].astype(jnp.float32)
    c0_pieces = {
        (1, 0): c0_bot, (-1, 0): c0_top,
        (0, 1): c0_right.transpose(1, 0, 2), (0, -1): c0_left.transpose(1, 0, 2),
        (1, 1): c0_bot[:, -h:], (1, -1): c0_bot[:, :h], (-1, 1): c0_top[:, -h:], (-1, -1): c0_top[:, :h],
    }
    sends = [c0_pieces[dirn] for dirn in DIRS]

    rpad = LPAD - h
    width = cells_y + 2 * LPAD
    zc = jnp.zeros((2, cells_x, rpad), jnp.float32)
    def cols(x, lo, hi):
        return jnp.pad(x, ((0, 0), (0, 0), (lo, hi)))

    def rows_of(x, lo, hi):
        return jnp.pad(x, ((0, 0), (lo, hi), (0, 0)))

    top = cols(hg[(1, 1)], rpad, width - LPAD) + cols(hg[(1, 0)], LPAD, LPAD) + cols(hg[(1, -1)], LPAD + cells_y, rpad)
    bot = cols(hg[(-1, 1)], rpad, width - LPAD) + cols(hg[(-1, 0)], LPAD, LPAD) + cols(hg[(-1, -1)], LPAD + cells_y, rpad)
    mid_t = rows_of(hg[(0, 1)], rpad, width - LPAD) + rows_of(gh_t, LPAD, LPAD) + rows_of(hg[(0, -1)], LPAD + cells_y, rpad)
    mid = mid_t.transpose(0, 2, 1)
    gh_ext = rows_of(top, 0, cells_x + h) + rows_of(mid, h, h) + rows_of(bot, cells_x + h, 0)
    g_b = jnp.broadcast_to(gh_ext[0][:, :, None], (cells_x + 2 * h, width, columns))
    h_rows = jnp.concatenate(
        [gh_ext[1][0:1], gh_ext[1][h:h + cells_x:TS], gh_ext[1][h + cells_x:h + cells_x + 1]], axis=0)
    h_b = jnp.broadcast_to(h_rows[:, :, None], (tiles_x + 2, width, columns))

    cheb_three, inv = run_stencil(detail, cm0, sends, g_b, h_b, nw, nn, total_cells)
    return scale_rows(cheb_three, inv)


def solution(mesh):
    in_specs = (
        P("wide", "narrow", None),
        P("wide", "narrow", None),
        P("wide", "narrow"),
        P("wide", "narrow"),
        P("wide", "narrow"),
    )
    out_specs = P("wide", "narrow", None)
    return jax.shard_map(local, mesh=mesh, in_specs=in_specs, out_specs=out_specs, check_vma=False)
```
